128 devices in a mesh: gx: 16 (over x, z), gy: 8 (over y, core).
Axes of the slice: x: 4, y: 4, z: 4, core: 2. Of those that a mesh axis runs over, the one named last changes fastest.
Arguments:
- populations: float32 [4096, 19, 512], P(('gx', 'gy')), may hold values from 0.6 to 1.4
- neighbours: int32 [4096, 6], P(('gx', 'gy')), may hold values from -1 to 4095, as said below
- positions: float32 [16384, 3, 642], P(('gx', 'gy')), may hold values from 0.5 to 7.5
- stiffness: float32 [16384], P(('gx', 'gy')), may hold values from 0.005 to 0.02
- cell_owner: int32 [16384, 1], P(('gx', 'gy')), may hold values from 0 to 127; in each aligned block of 128 rows (0 to 127, 128 to 255, ...) at most 2 rows name the same one
- cell_block: int32 [16384], P(('gx', 'gy')), may hold values from 0 to 31
- triangles: int32 [1280, 3], replicated, may hold values from 0 to 641, all different within a row
Outputs:
- read_pops: float32 [4096, 19, 512], P(('gx', 'gy'))
The draws below stay inside these ranges and needn't reach their ends.
Inputs may be any that keep to these rules, and one draw needn't show every extreme that they name: Each entry is -1 or a block id whose owner (id // 32, an index in the order gx+gy) lies at most one step away, cyclically, along gx and along gy from the owner of the block in that row. Faces are reciprocal: neighbours[b, 2a+1] = c exactly when neighbours[c, 2a] = b. `cell_owner`: among the rows of one device at most 2 cells name the same owner; owners are device indices in the order gx+gy. `triangles`: the three vertices of a row differ; every vertex appears in some row.
All inputs are finite; a program needn't handle non-finite values.
Results may differ from the reference program's by a relative error of at most 0.0003.
Values sent between devices are 32-bit elements; how exact they have to be, the bound alone decides.
No kernel may reach another device: no remote copies, remote signals or barrier semaphores. Data moves between devices by JAX's collectives and lax.ppermute only.
A program may use at most 128 MiB of HBM per device.

```python
import math
import jax
import jax.numpy as jnp
import numpy as np
from jax import lax

SITES = 512
Q = 19
NV = 642
NTRI = 1280
BLK_DEV = 32
CELL_DEV = 128
NDEV = 128
NBLK = 4096
NCELL = 16384
CAP = 2
N_GX = 16
N_GY = 8


def draw_neighbours(key, part):
    blocks_all = BLK_DEV * N_GX * N_GY
    block_ids = jnp.arange(blocks_all, dtype=jnp.int32)
    owners = block_ids // BLK_DEV
    slot_ids = block_ids % BLK_DEV
    grid_row = owners // N_GY
    grid_col = owners % N_GY
    columns = []
    for axis in range(3):
        keys = jax.random.split(jax.random.fold_in(key, 17 + axis), 4)
        shift_row = 2 * jax.random.randint(keys[0], (), 0, 2) - 1
        shift_col = jax.random.randint(keys[1], (N_GX,), -1, 2)
        perm_keys = jax.random.split(keys[2], N_GX * N_GY)
        perms = jax.vmap(lambda one_key: jax.random.permutation(one_key, BLK_DEV))(perm_keys).astype(jnp.int32)
        walls = jax.random.randint(keys[3], (blocks_all,), 0, 8) == 0
        new_row = (grid_row + shift_row) % N_GX
        new_col = (grid_col + shift_col[grid_row]) % N_GY
        partner = ((new_row * N_GY + new_col) * BLK_DEV + perms[owners, slot_ids]).astype(jnp.int32)
        upper = jnp.where(walls, -1, partner).astype(jnp.int32)
        lower = jnp.full((blocks_all,), -1, jnp.int32).at[partner].set(jnp.where(walls, -1, block_ids).astype(jnp.int32))
        columns.append(lower)
        columns.append(upper)
    return jnp.stack(columns, axis=1).astype(jnp.int32)


def with_ends(values, stream_key, least, top_value):
    place = [jax.random.randint(jax.random.fold_in(stream_key, axis), (), 0, length) for axis, length in enumerate(values.shape)]
    widest = values.shape.index(max(values.shape))
    beside = place[:widest] + [(place[widest] + 1) % values.shape[widest]] + place[widest + 1:]
    return values.at[tuple(place)].set(least).at[tuple(beside)].set(top_value)


def block_levels(rng, extent, shards, low, high):
    def one(position, blocks):
        draws = jax.random.uniform(jax.random.fold_in(jax.random.fold_in(rng, 6), position), (blocks,), jnp.float32, low / len(shards), high / len(shards))
        return jnp.repeat(jnp.exp(draws), extent[position] // blocks).reshape((-1,) + (1,) * (len(extent) - position - 1))

    level = one(*shards[0])
    for cut in shards[1:]:
        level = level * one(*cut)
    return level


def different_ones(key, rows, count, top, lift):
    order = jax.random.permutation(jax.random.fold_in(key, 1), count)
    pull = order
    for power in range(3):
        pull = pull * pull // count
    pull = pull * lift // count
    lots = jax.random.randint(jax.random.fold_in(key, 2), (rows, count), 0, 4096) + pull
    fixed_rows = jax.random.permutation(jax.random.fold_in(key, 3), rows)[jnp.arange(count) % rows]
    lots = jnp.where(jnp.arange(rows)[:, None] == fixed_rows[None, :], 1 << 14, lots)
    priority = lots * count + jnp.arange(count)
    return lax.top_k(priority.astype(jnp.int32), top)[1].astype(jnp.int32)


def deal_out(rng, own, number, rows, amount, top, most, lean):
    ranking = jax.random.permutation(rng, amount)
    heavy_load, ordinary = portions_of(amount, rows * top, most, lean, True), portions_of(amount, rows * top, most, lean, False)
    places = jnp.arange(amount)

    def named(tallies, offset_by):
        used = int((tallies > 0).sum())
        fixed = max(1, used // 4)
        passed = fixed + (places - fixed + offset_by * (used - fixed)) % max(1, amount - fixed)
        return jnp.zeros((amount,), jnp.int32).at[ranking[jnp.where(places < fixed, places, passed)]].set(jnp.asarray(tallies, jnp.int32))

    tallies = jnp.where(number % 4 == 0, named(heavy_load, number // 4), named(ordinary, number - number // 4 - 1))
    mixed = jax.random.permutation(jax.random.fold_in(own, 3), amount)
    giver, receiver = mixed[0:amount // 2 * 2:2], mixed[1:amount // 2 * 2:2]
    slack = jnp.minimum(tallies[giver] - 1, most - tallies[receiver]) // 2
    slack = jnp.where((giver == ranking[0]) | (receiver == ranking[0]) | (tallies[receiver] == 0), 0, jnp.maximum(slack, 0))
    passed = jax.random.randint(jax.random.fold_in(own, 4), (amount // 2,), 0, 1 << 20) % (slack + 1)
    tallies = tallies.at[giver].add(-passed).at[receiver].add(passed)
    items = jnp.searchsorted(jnp.cumsum(tallies), jnp.arange(rows * top), side="right").astype(jnp.int32)
    table = items.reshape(top, rows).T
    table = table[jax.random.permutation(jax.random.fold_in(own, 1), rows)]
    offset_by = jax.random.randint(jax.random.fold_in(own, 2), (rows, 1), 0, top)
    return jnp.take_along_axis(table, (jnp.arange(top)[None, :] + offset_by) % top, axis=1)


def portions_of(number_of, total, reach, slope, full):
    loads = [(1 << 20) // math.isqrt(rank ** slope) + 1 for rank in range(1, number_of + 1)]
    largest = reach if full else min(reach, max(-(-total // number_of), total * loads[0] // sum(loads)))
    least = 1 if total - largest >= number_of - 1 else 0
    counts, rest = [largest] + [least] * (number_of - 1), total - largest - least * (number_of - 1)
    while rest > 0:
        movable = [i for i in range(1, number_of) if counts[i] < largest] or [i for i in range(1, number_of) if counts[i] < reach]
        whole, left = sum([loads[i] for i in movable]), rest
        for i in movable:
            extra = min(reach - counts[i], max(1, left * loads[i] // whole), rest)
            counts[i] = counts[i] + extra
            rest = rest - extra
    return np.array(counts)


def setup_inputs(seed: int = 0) -> dict:
    streams_of = jax.random.split(jax.random.key(seed), 8)
    populations = jnp.clip(0.6 + 0.79999995 * jax.random.uniform(streams_of[0], (NBLK, Q, SITES), jnp.float32) ** block_levels(streams_of[0], (NBLK, Q, SITES), ((0, 128),), -0.2, 0.2), 0.6, 1.4)
    neighbours = draw_neighbours(jax.random.fold_in(streams_of[7], 71), 0)
    positions = jnp.clip(0.5 + 7.0 * jax.random.uniform(streams_of[2], (NCELL, 3, NV), jnp.float32) ** block_levels(streams_of[2], (NCELL, 3, NV), ((0, 128),), -0.2, 0.2), 0.5, 7.5)
    stiffness = jnp.clip(jnp.exp(math.log(0.02) - 1.3862944 * jax.random.uniform(streams_of[3], (NCELL,), jnp.float32) ** block_levels(streams_of[3], (NCELL,), ((0, 128),), -0.2, 0.2)), 0.005, 0.02)
    cell_owner_keys = jax.random.split(jax.random.fold_in(streams_of[4], 1), NCELL // CELL_DEV)
    cell_owner_turns = jax.random.permutation(jax.random.fold_in(streams_of[4], 3), NCELL // CELL_DEV)
    cell_owner = jax.vmap(lambda own, number: deal_out(jax.random.fold_in(streams_of[4], 2), own, number, CELL_DEV, NDEV, 1, CAP, 2))(cell_owner_keys, cell_owner_turns).reshape((NCELL, 1))
    cell_block = with_ends(jax.random.randint(streams_of[5], (NCELL,), 0, BLK_DEV), jax.random.fold_in(streams_of[5], 1), 0, BLK_DEV - 1).astype(jnp.int32)
    triangles = different_ones(streams_of[6], NTRI, NV, 3, 0)
    return dict(populations=populations, neighbours=neighbours, positions=positions, stiffness=stiffness, cell_owner=cell_owner, cell_block=cell_block, triangles=triangles)


lattice_vel = [[0, 0, 0], [1, 0, 0], [-1, 0, 0], [0, 1, 0], [0, -1, 0], [0, 0, 1], [0, 0, -1],
               [1, 1, 0], [-1, -1, 0], [1, -1, 0], [-1, 1, 0], [1, 0, 1], [-1, 0, -1], [1, 0, -1], [-1, 0, 1],
               [0, 1, 1], [0, -1, -1], [0, 1, -1], [0, -1, 1]]
lattice_wts = [1.0 / 3.0] + [1.0 / 18.0] * 6 + [1.0 / 36.0] * 12
opposite = [0, 2, 1, 4, 3, 6, 5, 8, 7, 10, 9, 12, 11, 14, 13, 16, 15, 18, 17]
relax_time = 0.6
highest = lax.Precision.HIGHEST


def membrane(points, stiff, triangles):
    first = points[:, :, triangles[:, 0]]
    second = points[:, :, triangles[:, 1]]
    third = points[:, :, triangles[:, 2]]
    parts = jnp.concatenate([second + third - 2.0 * first, first + third - 2.0 * second,
                             first + second - 2.0 * third], axis=2)
    owners = jnp.concatenate([triangles[:, 0], triangles[:, 1], triangles[:, 2]])
    summed = jax.ops.segment_sum(jnp.moveaxis(parts, 2, 0), owners, num_segments=points.shape[2])
    return stiff[:, None, None] * jnp.moveaxis(summed, 0, 2)


def spread_group(points, forces):
    count = points.shape[0]
    verts = points.shape[2]
    grid = jnp.arange(8).astype(jnp.float32)
    hats = jnp.maximum(0.0, 1.0 - jnp.abs(grid[None, None, :, None] - points[:, :, None, :]))
    plane = (hats[:, 1, :, None, :] * hats[:, 2, None, :, :]).reshape(count, 64, verts)
    left = hats[:, 0, None, :, :] * forces[:, :, None, :]
    result = jnp.einsum('ncix,nmx->ncim', left, plane, precision=highest)
    return result.reshape(count, 3, 512)


def collide(norm_pops, force):
    weights = jnp.asarray(lattice_wts, jnp.float32)[None, :, None]
    velocity_set = jnp.asarray(lattice_vel, jnp.float32)
    pops = norm_pops * weights
    density = jnp.sum(pops, axis=1)
    moment = jnp.einsum('qc,bqs->bcs', velocity_set, pops, precision=highest) + 0.5 * force
    velocity = moment / density[:, None, :]
    along = jnp.einsum('qc,bcs->bqs', velocity_set, velocity, precision=highest)
    push = jnp.einsum('qc,bcs->bqs', velocity_set, force, precision=highest)
    speed_sq = jnp.sum(velocity * velocity, axis=1)
    work = jnp.sum(velocity * force, axis=1)
    equil = weights * density[:, None, :] * (1.0 + 3.0 * along + 4.5 * along * along - 1.5 * speed_sq[:, None, :])
    source = weights * (1.0 - 0.5 / relax_time) * (3.0 * (push - work[:, None, :]) + 9.0 * along * push)
    return pops - (pops - equil) / relax_time + source


def put_plane(array, axis, where, plane):
    picker = [slice(None)] * array.ndim
    picker[axis] = where
    return array.at[tuple(picker)].set(plane)


def stream(padded, presence, post):
    blocks = post.shape[0]
    results = []
    for direction in range(19):
        step_x, step_y, step_z = lattice_vel[direction]
        moved = padded[:, direction, 1 - step_x:9 - step_x, 1 - step_y:9 - step_y, 1 - step_z:9 - step_z]
        there = presence[:, 1 - step_x:9 - step_x, 1 - step_y:9 - step_y, 1 - step_z:9 - step_z]
        back = post[:, opposite[direction]].reshape(blocks, 8, 8, 8)
        results.append(jnp.where(there > 0.5, moved, back))
    return jnp.stack(results, axis=1).reshape(blocks, 19, 512)


def cell_spread(positions, stiffness, triangles):
    cells = positions.shape[0]
    group = math.gcd(cells, 256)
    batches = cells // group

    def one_group(bundle):
        return spread_group(bundle[0], membrane(bundle[0], bundle[1], triangles))

    result = lax.map(one_group, (positions.reshape((batches, group) + positions.shape[1:]),
                                 stiffness.reshape(batches, group)))
    return result.reshape(cells, 3, 512)


def reference(populations, neighbours, positions, stiffness, cell_owner, cell_block, triangles):
    blocks = populations.shape[0]
    home = (cell_owner[:, 0] * BLK_DEV + cell_block).astype(jnp.int32)
    spread = cell_spread(positions, stiffness, triangles)
    body_force = jax.ops.segment_sum(spread, home, num_segments=blocks)
    post = collide(populations, body_force)
    padded = jnp.pad(post.reshape(blocks, 19, 8, 8, 8), ((0, 0), (0, 0), (1, 1), (1, 1), (1, 1)))
    presence = jnp.pad(jnp.ones((blocks, 8, 8, 8), jnp.float32), ((0, 0), (1, 1), (1, 1), (1, 1)))
    for axis in range(3):
        pop_axis = axis + 2
        pres_axis = axis + 1
        low_pops = jnp.take(padded, 1, axis=pop_axis)
        high_pops = jnp.take(padded, 8, axis=pop_axis)
        low_pres = jnp.take(presence, 1, axis=pres_axis)
        high_pres = jnp.take(presence, 8, axis=pres_axis)
        below = neighbours[:, 2 * axis]
        above = neighbours[:, 2 * axis + 1]
        keep_below = (below >= 0).astype(jnp.float32)
        keep_above = (above >= 0).astype(jnp.float32)
        safe_below = jnp.maximum(below, 0)
        safe_above = jnp.maximum(above, 0)
        lower_pops = high_pops[safe_below] * keep_below[:, None, None, None]
        lower_pres = high_pres[safe_below] * keep_below[:, None, None]
        upper_pops = low_pops[safe_above] * keep_above[:, None, None, None]
        upper_pres = low_pres[safe_above] * keep_above[:, None, None]
        padded = put_plane(padded, pop_axis, 0, lower_pops)
        padded = put_plane(padded, pop_axis, 9, upper_pops)
        presence = put_plane(presence, pres_axis, 0, lower_pres)
        presence = put_plane(presence, pres_axis, 9, upper_pres)
    return stream(padded, presence, post)
```

```python
import functools

import jax
import jax.numpy as jnp
import numpy as np
from jax import lax
from jax.experimental import pallas as pl
from jax.experimental.pallas import tpu as pltpu
from jax.sharding import PartitionSpec as P

vel = [
    (0, 0, 0), (1, 0, 0), (-1, 0, 0), (0, 1, 0), (0, -1, 0), (0, 0, 1), (0, 0, -1),
    (1, 1, 0), (-1, -1, 0), (1, -1, 0), (-1, 1, 0),
    (1, 0, 1), (-1, 0, -1), (1, 0, -1), (-1, 0, 1),
    (0, 1, 1), (0, -1, -1), (0, 1, -1), (0, -1, 1),
]
wts = [1.0 / 3.0] + [1.0 / 18.0] * 6 + [1.0 / 36.0] * 12
opposite = [0, 2, 1, 4, 3, 6, 5, 8, 7, 10, 9, 12, 11, 14, 13, 16, 15, 18, 17]
relax_time = 0.6
NEG, POS = {}, {}
for ax in range(3):
    NEG[ax] = [q for q in range(19) if vel[q][ax] == -1]
    POS[ax] = [q for q in range(19) if vel[q][ax] == 1]
EDGE_Q = list(range(7, 19))
FACE_TILES = 15
EDGE_TILE = 15
NT = 16
BOTH = ("gx", "gy")
f32, bf16, i32 = jnp.float32, jnp.bfloat16, jnp.int32


def split(x):
    high = x.astype(bf16).astype(f32)
    return high, x - high


def nt_dot(a, b):
    return lax.dot_general(a, b, (((1,), (1,)), ((), ())), preferred_element_type=f32)


def hat(x, grid):
    return jnp.maximum(0.0, 1.0 - jnp.abs(x - grid))


def spread_kernel(owner, block, pos, stiff, tri, out, st, force, count):
    nv = pos.shape[2]
    cells = pos.shape[1]
    for r in range(0, nv, 128):
        ids = lax.broadcasted_iota(i32, (128, tri.shape[1]), 0) + r
        hit = (ids == tri[0:1, :]) | (ids == tri[1:2, :]) | (ids == tri[2:3, :])
        st[r : r + 128, :] = hit.astype(f32).astype(bf16)
    links = nt_dot(st[...], st[...])
    rows = lax.broadcasted_iota(i32, (nv, nv), 0)
    cols = lax.broadcasted_iota(i32, (nv, nv), 1)
    springs = jnp.where(rows == cols, -2.0 * links, links)
    s_hi, s_lo = split(springs)
    s_hi, s_lo = s_hi.astype(bf16), s_lo.astype(bf16)
    for d in range(3):
        x_hi, x_lo = split(pos[d])
        x_hi, x_lo = x_hi.astype(bf16), x_lo.astype(bf16)
        total = (
            jnp.dot(x_hi, s_hi, preferred_element_type=f32)
            + jnp.dot(x_lo, s_hi, preferred_element_type=f32)
            + jnp.dot(x_hi, s_lo, preferred_element_type=f32)
        )
        force[d] = total * stiff[...]
    out[:, 0:3072] = jnp.zeros((out.shape[0], 3072), f32)
    out[:, 3072:3200] = jnp.full((out.shape[0], 128), -1.0, f32)

    def clear(t, carry):
        count[t] = 0
        return carry

    lax.fori_loop(0, out.shape[0], clear, 0)
    sub8 = lax.broadcasted_iota(i32, (8, nv), 0)
    g_even = (2 * (sub8 % 4)).astype(f32)
    g_odd = g_even + 1.0
    g_all = sub8.astype(f32)
    first4 = sub8 < 4
    lane8 = lax.broadcasted_iota(i32, (8, 128), 1)
    sub = lax.broadcasted_iota(i32, (8, 128), 0)

    def one(c):
        x = jnp.broadcast_to(pos[0, pl.ds(c, 1), :], (8, nv))
        y = jnp.broadcast_to(pos[1, pl.ds(c, 1), :], (8, nv))
        z = jnp.broadcast_to(pos[2, pl.ds(c, 1), :], (8, nv))
        f0 = jnp.broadcast_to(force[0, pl.ds(c, 1), :], (8, nv))
        f1 = jnp.broadcast_to(force[1, pl.ds(c, 1), :], (8, nv))
        f2 = jnp.broadcast_to(force[2, pl.ds(c, 1), :], (8, nv))
        h_even = hat(x, g_even)
        h_odd = hat(x, g_odd)
        f01 = jnp.where(first4, f0, f1)
        left = jnp.concatenate(
            [h_even * f01, jnp.where(first4, h_even, h_odd) * f2, h_odd * f01], axis=0
        )
        l_hi, l_lo = split(left)
        left2 = jnp.concatenate([l_hi, l_lo], axis=0).astype(bf16)
        hz = hat(z, g_all)
        plane = jnp.concatenate([hat(y, float(j)) * hz for j in range(8)], axis=0)
        p_hi, p_lo = split(plane)
        plane2 = jnp.concatenate([p_hi, p_lo], axis=0).astype(bf16)
        prod = nt_dot(left2, plane2)
        both = prod[0:24] + prod[24:48]
        res = both + pltpu.roll(both, 64, 1)
        main = jnp.where(lane8 < 64, res[0:8], res[16:24])
        mid = res[8:16]
        tail = jnp.where(lane8 < 64, mid, pltpu.roll(mid, 4, 0))
        t = owner[c]
        r = count[t]
        count[t] = r + 1
        base = pl.multiple_of((t // 8) * 8, 8)
        mine = sub == t % 8
        for k in range(12):
            row = main[k : k + 1] if k < 8 else tail[k - 8 : k - 7]
            at = pl.multiple_of(r * 1536 + 128 * k, 128)
            pltpu.store(out.at[pl.ds(base, 8), pl.ds(at, 128)], jnp.broadcast_to(row, (8, 128)), mask=mine)
        label = jnp.full((8, 128), block[c].astype(f32))
        pltpu.store(out.at[pl.ds(base, 8), 3072:3200], label, mask=mine & (lane8 == r))

    def step(n, carry):
        for m in range(4):
            one(n * 4 + m)
        return carry

    lax.fori_loop(0, cells // 4, step, 0)


def spread(owner, block, positions, stiffness, triangles, devices):
    cells, _, verts = positions.shape
    nv = -(-verts // 256) * 256
    pos = jnp.pad(
        jnp.transpose(positions, (1, 0, 2)), ((0, 0), (0, 0), (0, nv - verts)), constant_values=-100.0
    )
    tri = jnp.transpose(triangles)
    smem = pl.BlockSpec(memory_space=pltpu.SMEM)
    vmem = pl.BlockSpec(memory_space=pltpu.VMEM)
    return pl.pallas_call(
        spread_kernel,
        out_shape=jax.ShapeDtypeStruct((devices, 3200), f32),
        in_specs=[smem, smem, vmem, vmem, vmem],
        out_specs=vmem,
        scratch_shapes=[
            pltpu.VMEM((nv, triangles.shape[0]), bf16),
            pltpu.VMEM((3, cells, nv), f32),
            pltpu.SMEM((devices,), i32),
        ],
        compiler_params=pltpu.CompilerParams(vmem_limit_bytes=48 << 20),
        name="spread",
    )(owner, block, pos, stiffness[:, None], tri)


def lane_take(x, index):
    return jnp.take_along_axis(x, index, axis=1)


def collide_kernel(got, pops, post, table, body):
    slots = got.shape[0]
    lane = lax.broadcasted_iota(i32, (slots, 128), 1)
    ids = got[:, 3072:3200]
    picks = []
    for r in range(2):
        col = jnp.broadcast_to(ids[:, r : r + 1], (slots, 128))
        hit = (col == lane.astype(f32)).astype(f32)
        picks.append(jnp.transpose(hit)[0:32].astype(bf16))
    for n in range(3):
        total = jnp.zeros((32, 512), f32)
        for r in range(2):
            part = got[:, r * 1536 + n * 512 : r * 1536 + (n + 1) * 512]
            hi, lo = split(part)
            total = total + jnp.dot(picks[r], hi.astype(bf16), preferred_element_type=f32)
            total = total + jnp.dot(picks[r], lo.astype(bf16), preferred_element_type=f32)
        body[n] = total

    lanes = lax.broadcasted_iota(i32, (8, 128), 1)
    low = lanes < 64
    keep = 1.0 - 1.0 / relax_time
    gain = 1.0 - 0.5 / relax_time

    def group(g, carry):
        rows = pl.ds(pl.multiple_of(g * 8, 8), 8)
        for a in range(4):
            cut = slice(128 * a, 128 * (a + 1))
            f = [pops[rows, q, cut] * wts[q] for q in range(19)]
            force = [body[d, rows, cut] for d in range(3)]
            rho = f[0]
            for q in range(1, 19):
                rho = rho + f[q]
            u = []
            for d in range(3):
                m = 0.5 * force[d]
                for q in range(1, 19):
                    if vel[q][d] == 1:
                        m = m + f[q]
                    elif vel[q][d] == -1:
                        m = m - f[q]
                u.append(m / rho)
            speed = u[0] * u[0] + u[1] * u[1] + u[2] * u[2]
            work = u[0] * force[0] + u[1] * force[1] + u[2] * force[2]
            rho_t = rho * (1.0 / relax_time)
            flat = rho_t * (1.0 - 1.5 * speed) - (3.0 * gain) * work
            post[0, rows, cut] = keep * f[0] + wts[0] * flat
            for q in range(1, 19, 2):
                along = push = None
                for d in range(3):
                    e = vel[q][d]
                    if e:
                        along = e * u[d] if along is None else along + e * u[d]
                        push = e * force[d] if push is None else push + e * force[d]
                even = wts[q] * (flat + along * (4.5 * rho_t * along + (9.0 * gain) * push))
                odd = wts[q] * (3.0 * rho_t * along + (3.0 * gain) * push)
                post[q, rows, cut] = keep * f[q] + (even + odd)
                post[q + 1, rows, cut] = keep * f[q + 1] + (even - odd)
        for n in range(5):
            table[n, rows, :] = jnp.where(low, post[NEG[0][n], rows, 0:128], post[POS[0][n], rows, 384:512])
            m = lanes % 64
            first, second = m // 8, m % 8
            for ax in (1, 2):
                picked = None
                for a in range(4):
                    inside = (first % 2) * 64
                    if ax == 1:
                        at_low, at_high = inside + second, inside + 56 + second
                    else:
                        at_low, at_high = inside + second * 8, inside + second * 8 + 7
                    cut = slice(128 * a, 128 * (a + 1))
                    val = jnp.where(
                        low, lane_take(post[NEG[ax][n], rows, cut], at_low), lane_take(post[POS[ax][n], rows, cut], at_high)
                    )
                    picked = val if picked is None else jnp.where(first // 2 == a, val, picked)
                table[5 * ax + n, rows, :] = picked
        line = jnp.zeros((8, 128), f32)
        w = lanes % 8
        for n, q in enumerate(EDGE_Q):
            ex, ey, ez = vel[q]
            at = [7 if e == 1 else 0 for e in vel[q]]
            mine = lanes // 8 == n
            if ex:
                a = 3 if ex == 1 else 0
                base = 64 if ex == 1 else 0
                where_ = base + (at[1] * 8 + w if ey else w * 8 + at[2])
                val = lane_take(post[q, rows, 128 * a : 128 * (a + 1)], where_)
                line = jnp.where(mine, val, line)
            else:
                where_ = (w % 2) * 64 + at[1] * 8 + at[2]
                for a in range(4):
                    val = lane_take(post[q, rows, 128 * a : 128 * (a + 1)], where_)
                    line = jnp.where(mine & (w // 2 == a), val, line)
        table[EDGE_TILE, rows, :] = line
        return carry

    lax.fori_loop(0, 4, group, 0)


def collide(got, populations):
    vmem = pl.BlockSpec(memory_space=pltpu.VMEM)
    return pl.pallas_call(
        collide_kernel,
        out_shape=(jax.ShapeDtypeStruct((19, 32, 512), f32), jax.ShapeDtypeStruct((NT, 32, 128), f32)),
        in_specs=[vmem, vmem],
        out_specs=(vmem, vmem),
        scratch_shapes=[pltpu.VMEM((3, 32, 512), f32)],
        compiler_params=pltpu.CompilerParams(vmem_limit_bytes=48 << 20),
        name="collide",
    )(got, populations)


def stream_kernel(where_face, where_edge, post, there, mid, down, up, down2, up2, out, table, ghost, sem):
    parts = [(mid, 50, 50), (down, 0, 50), (up, 100, 50), (down2, 150, 5), (up2, 155, 5)]
    copies = [
        pltpu.make_async_copy(ref, table.at[pl.ds(at, size)], sem.at[n]) for n, (ref, at, size) in enumerate(parts)
    ]
    for c in copies:
        c.start()
    for c in copies:
        c.wait()
    lanes = lax.broadcasted_iota(i32, (8, 128), 1)
    sub = lax.broadcasted_iota(i32, (8, 128), 0)

    def row_of(at, tile):
        return table[at // 32 + tile, pl.ds(at % 32, 8, stride=0), :]

    def fetch(g, carry):
        rows = pl.ds(pl.multiple_of(g * 8, 8), 8)
        for ax in range(3):
            made = [jnp.zeros((8, 128), f32)] * 5
            for i in range(8):
                low_at = where_face[(g * 8 + i) * 6 + 2 * ax]
                high_at = where_face[(g * 8 + i) * 6 + 2 * ax + 1]
                for n in range(5):
                    t = 5 * ax + n
                    both = jnp.where(lanes < 64, row_of(high_at, t), row_of(low_at, t))
                    made[n] = jnp.where(sub == i, both, made[n])
            for n in range(5):
                ghost[5 * ax + n, rows, :] = made[n]
        line = jnp.zeros((8, 128), f32)
        for i in range(8):
            for n in range(12):
                at = where_edge[(g * 8 + i) * 12 + n]
                line = jnp.where((lanes // 8 == n) & (sub == i), row_of(at, 0), line)
        ghost[EDGE_TILE, rows, :] = line
        return carry

    lax.fori_loop(0, 4, fetch, 0)
    jj = (lanes // 8) % 8
    kk = lanes % 8

    def group(g, carry):
        rows = pl.ds(pl.multiple_of(g * 8, 8), 8)
        flags = there[rows, :]

        def flag(n):
            return jnp.broadcast_to(flags[:, n : n + 1], (8, 128)) > 0.5

        face_on = [flag(n) for n in range(6)]
        edge_on = [flag(6 + n) for n in range(12)]
        edges = ghost[EDGE_TILE, rows, :]
        out[rows, 0, :] = post[0, rows, :]
        for q in range(1, 19):
            e = vel[q]
            ex, ey, ez = e
            shift = ex * 64 + ey * 8 + ez
            tiles = [post[q, rows, 128 * a : 128 * (a + 1)] for a in range(4)]
            rolled = [pltpu.roll(t, shift % 128, 1) for t in tiles]
            for a in range(4):
                if shift > 0:
                    val = jnp.where(lanes < shift, rolled[(a - 1) % 4], rolled[a])
                else:
                    val = jnp.where(lanes >= 128 + shift, rolled[(a + 1) % 4], rolled[a])
                ii = 2 * a + lanes // 64
                back = post[opposite[q], rows, 128 * a : 128 * (a + 1)]
                coords = (ii, jj, kk)
                crossing = [None if e[d] == 0 else coords[d] == (0 if e[d] == 1 else 7) for d in range(3)]
                if ex == 1 and a != 0 or ex == -1 and a != 3:
                    crossing[0] = None
                axes = [d for d in range(3) if crossing[d] is not None]
                if axes:
                    out_of = crossing[axes[0]]
                    for d in axes[1:]:
                        out_of = out_of | crossing[d]
                    val = jnp.where(out_of, back, val)
                for d in axes:
                    face = 2 * d + (0 if e[d] == 1 else 1)
                    n = (POS[d] if e[d] == 1 else NEG[d]).index(q)
                    source = ghost[5 * d + n, rows, :]
                    base = 64 if e[d] == 1 else 0
                    if d == 0:
                        brought = pltpu.roll(source, (64 + ey * 8 + ez) % 128, 1)
                    elif d == 1:
                        brought = lane_take(source, base + ((ii - ex) * 8 + kk - ez) % 64)
                    else:
                        brought = lane_take(source, base + ((ii - ex) * 8 + jj - ey) % 64)
                    use = crossing[d] & face_on[face]
                    for other in axes:
                        if other != d:
                            use = use & ~crossing[other]
                    val = jnp.where(use, brought, val)
                if len(axes) == 2:
                    n = q - 7
                    along = kk if ez == 0 else (jj if ey == 0 else ii)
                    brought = lane_take(edges, 8 * n + along)
                    val = jnp.where(crossing[axes[0]] & crossing[axes[1]] & edge_on[n], brought, val)
                out[rows, q, 128 * a : 128 * (a + 1)] = val
        return carry

    lax.fori_loop(0, 4, group, 0)


def stream(where_face, where_edge, post, there, mid, down, up, down2, up2):
    smem = pl.BlockSpec(memory_space=pltpu.SMEM)
    vmem = pl.BlockSpec(memory_space=pltpu.VMEM)
    hbm = pl.BlockSpec(memory_space=pl.ANY)
    return pl.pallas_call(
        stream_kernel,
        out_shape=jax.ShapeDtypeStruct((32, 19, 512), f32),
        in_specs=[smem, smem, vmem, vmem] + [hbm] * 5,
        out_specs=vmem,
        scratch_shapes=[
            pltpu.VMEM((160, 32, 128), f32),
            pltpu.VMEM((NT, 32, 128), f32),
            pltpu.SemaphoreType.DMA((5,)),
        ],
        compiler_params=pltpu.CompilerParams(vmem_limit_bytes=48 << 20),
        name="stream",
    )(where_face, where_edge, post, there, mid, down, up, down2, up2)


def send(array, axis, step):
    size = lax.axis_size(axis)
    return lax.ppermute(array, axis, [(i, (i + step) % size) for i in range(size)])


def look_up(neighbours):
    rows_gx, rows_gy = lax.axis_size("gx"), lax.axis_size("gy")
    me_x, me_y = lax.axis_index("gx"), lax.axis_index("gy")
    column = jnp.concatenate([send(neighbours, "gx", 1), neighbours, send(neighbours, "gx", -1)], axis=0)
    near = jnp.concatenate([send(column, "gy", 1), column, send(column, "gy", -1)], axis=0)

    def place(ids, reach):
        safe = jnp.maximum(ids, 0)
        owner = safe // 32
        x = (owner // rows_gy - me_x + reach) % rows_gx
        y = (owner % rows_gy - me_y + reach) % rows_gy
        return x, y, safe % 32

    x, y, slot = place(neighbours, 1)
    on_face = neighbours >= 0
    where_face = jnp.where(on_face, (y * 50 + x * 16) * 32 + slot, 0)
    near_row = (y * 3 + x) * 32 + slot
    second = jnp.take(near, jnp.where(on_face, near_row, 0)[:, 2:6].reshape(-1), axis=0).reshape(32, 4, 6)
    two = []
    for q in EDGE_Q:
        e = vel[q]
        axes = [d for d in range(3) if e[d]]
        f1 = 2 * axes[1] + (0 if e[axes[1]] == 1 else 1)
        f2 = 2 * axes[0] + (0 if e[axes[0]] == 1 else 1)
        two.append(jnp.where(on_face[:, f1], second[:, f1 - 2, f2], -1))
    two = jnp.stack(two, axis=1)
    x, y, slot = place(two, 2)
    on_edge = two >= 0
    inner = (y - 1) * 50 + jnp.where(x == 0, 48, jnp.where(x == 4, 49, (x - 1) * 16 + EDGE_TILE))
    tile = jnp.where(y == 0, 150 + x, jnp.where(y == 4, 155 + x, inner))
    where_edge = jnp.where(on_edge, tile * 32 + slot, 0)
    there = jnp.concatenate([on_face, on_edge], axis=1).astype(f32)
    there = jnp.pad(there, ((0, 0), (0, 128 - 18)))
    return where_face.reshape(-1), where_edge.reshape(-1), there


def exchange(table):
    edge = table[EDGE_TILE : EDGE_TILE + 1]
    left, right = send(table, "gx", 1), send(table, "gx", -1)
    left2, right2 = send(edge, "gx", 2), send(edge, "gx", -2)
    mid = jnp.concatenate([left, table, right, left2, right2], axis=0)
    edges = jnp.concatenate([left2, left[EDGE_TILE:], edge, right[EDGE_TILE:], right2], axis=0)
    return mid, send(mid, "gy", 1), send(mid, "gy", -1), send(edges, "gy", 2), send(edges, "gy", -2)


def body(populations, neighbours, positions, stiffness, cell_owner, cell_block, triangles):
    devices = lax.axis_size("gx") * lax.axis_size("gy")
    where_face, where_edge, there = look_up(neighbours)
    slots = spread(cell_owner[:, 0], cell_block, positions, stiffness, triangles, devices)
    got = lax.all_to_all(slots, BOTH, split_axis=0, concat_axis=0, tiled=True)
    post, table = collide(got, populations)
    return stream(where_face, where_edge, post, there, *exchange(table))


def solution(mesh):
    placed = (
        P(BOTH, None, None),
        P(BOTH, None),
        P(BOTH, None, None),
        P(BOTH),
        P(BOTH, None),
        P(BOTH),
        P(),
    )
    return jax.shard_map(
        body, mesh=mesh, in_specs=placed, out_specs=P(BOTH, None, None), check_vma=False
    )
```

```python
import functools

import jax
import jax.numpy as jnp
import numpy as np
from jax import lax
from jax.experimental import pallas as pl
from jax.experimental.pallas import tpu as pltpu
from jax.sharding import PartitionSpec as P

vel = [
    (0, 0, 0), (1, 0, 0), (-1, 0, 0), (0, 1, 0), (0, -1, 0), (0, 0, 1), (0, 0, -1),
    (1, 1, 0), (-1, -1, 0), (1, -1, 0), (-1, 1, 0),
    (1, 0, 1), (-1, 0, -1), (1, 0, -1), (-1, 0, 1),
    (0, 1, 1), (0, -1, -1), (0, 1, -1), (0, -1, 1),
]
wts = [1.0 / 3.0] + [1.0 / 18.0] * 6 + [1.0 / 36.0] * 12
opposite = [0, 2, 1, 4, 3, 6, 5, 8, 7, 10, 9, 12, 11, 14, 13, 16, 15, 18, 17]
relax_time = 0.6
NEG, POS = {}, {}
for ax in range(3):
    NEG[ax] = [q for q in range(19) if vel[q][ax] == -1]
    POS[ax] = [q for q in range(19) if vel[q][ax] == 1]
EDGE_Q = list(range(7, 19))
FACE_TILES = 15
EDGE_TILE = 15
NT = 16
NOWHERE = 160 * 32
WIDE = 3328
BOTH = ("gx", "gy")
f32, bf16, i32 = jnp.float32, jnp.bfloat16, jnp.int32


def nt_dot(a, b):
    return lax.dot_general(a, b, (((1,), (1,)), ((), ())), preferred_element_type=f32)


def hat(x, grid):
    return jnp.maximum(0.0, 1.0 - jnp.abs(x - grid))


def spread_kernel(owner_in, block_in, stiff_in, raw_in, tri_in, near_in, out, owner, block, stiff, raw, tri, near, sem, st, pos, force, hats, count):
    cells, nv = pos.shape[1:]
    verts = raw.shape[1]
    pairs = ((tri_in, tri), (raw_in, raw), (near_in, near), (owner_in, owner), (block_in, block), (stiff_in, stiff))
    copies = [pltpu.make_async_copy(a, b, sem.at[n]) for n, (a, b) in enumerate(pairs)]
    for c in copies:
        c.start()
    for c in copies:
        c.wait()
    for r in range(0, nv, 128):
        ids = lax.broadcasted_iota(i32, (128, tri.shape[1]), 0) + r
        hit = (ids == tri[0:1, :]) | (ids == tri[1:2, :]) | (ids == tri[2:3, :])
        st[r : r + 128, :] = hit.astype(f32).astype(bf16)
        for d in range(3):
            have = min(verts - r, 128)
            piece = raw[d, r : r + have, :]
            if have < 128:
                piece = jnp.concatenate([piece, jnp.full((128 - have, cells), -100.0, f32)], axis=0)
            pos[d, :, r : r + 128] = jnp.transpose(piece)
    links = nt_dot(st[...], st[...])
    rows = lax.broadcasted_iota(i32, (nv, nv), 0)
    cols = lax.broadcasted_iota(i32, (nv, nv), 1)
    springs = jnp.where(rows == cols, -2.0 * links, links)
    s_hi = springs.astype(bf16)
    s_lo = (springs - s_hi.astype(f32)).astype(bf16)
    for d in range(3):
        x = pos[d]
        x_hi = x.astype(bf16)
        x_lo = (x - x_hi.astype(f32)).astype(bf16)
        force[d] = (
            jnp.dot(x_hi, s_hi, preferred_element_type=f32)
            + jnp.dot(x_lo, s_hi, preferred_element_type=f32)
            + jnp.dot(x_hi, s_lo, preferred_element_type=f32)
        )
    sub = lax.broadcasted_iota(i32, (8, 128), 0)
    lane = lax.broadcasted_iota(i32, (8, 128), 1)
    slots = out.shape[0]
    tail_row = jnp.full((8, 128), -1.0, f32)
    table_row = jnp.zeros((8, 128), f32)
    for f in range(4):
        one_face = jnp.concatenate([near[f : f + 1, :].astype(f32), jnp.zeros((1, 96), f32)], axis=1)
        one_face = jnp.broadcast_to(one_face, (8, 128))
        table_row = jnp.where(lane // 32 == f, pltpu.roll(one_face, 32 * f, 1) if f else one_face, table_row)
    out[:, 0:3072] = jnp.zeros((slots, 3072), f32)

    def clear(t, carry):
        base = pl.ds(pl.multiple_of(t * 8, 8), 8)
        out[base, 3072:3200] = tail_row
        out[base, 3200:3328] = table_row
        for m in range(8):
            count[t * 8 + m] = 0
        return carry

    lax.fori_loop(0, slots // 8, clear, 0)
    sub8 = lax.broadcasted_iota(i32, (8, nv), 0)
    g_even = (2 * (sub8 % 4)).astype(f32)
    g_odd = g_even + 1.0
    g_all = sub8.astype(f32)
    first4 = sub8 < 4

    def one(c, m):
        x = jnp.broadcast_to(pos[0, pl.ds(c, 1), :], (8, nv))
        y = jnp.broadcast_to(pos[1, pl.ds(c, 1), :], (8, nv))
        z = jnp.broadcast_to(pos[2, pl.ds(c, 1), :], (8, nv))
        f0 = jnp.broadcast_to(force[0, pl.ds(c, 1), :], (8, nv))
        f1 = jnp.broadcast_to(force[1, pl.ds(c, 1), :], (8, nv))
        f2 = jnp.broadcast_to(force[2, pl.ds(c, 1), :], (8, nv))
        h_even = hat(x, g_even)
        h_odd = hat(x, g_odd)
        f01 = jnp.where(first4, f0, f1)
        left = jnp.concatenate(
            [h_even * f01, jnp.where(first4, h_even, h_odd) * f2, h_odd * f01], axis=0
        )
        l_lo = left - left.astype(bf16).astype(f32)
        left2 = jnp.concatenate([left, l_lo], axis=0).astype(bf16)
        hats[m] = hat(y, g_all)
        hz = hat(z, g_all)
        plane = jnp.concatenate(
            [jnp.broadcast_to(hats[m, j : j + 1, :], (8, nv)) * hz for j in range(8)], axis=0
        )
        p_hi = plane.astype(bf16)
        p_lo = (plane - p_hi.astype(f32)).astype(bf16)
        prod = nt_dot(left2, jnp.concatenate([p_hi, p_lo], axis=0))
        both = prod[0:24] + prod[24:48]
        res = (both + pltpu.roll(both, 64, 1)) * stiff[c]
        main = jnp.where(lane < 64, res[0:8], res[16:24])
        mid = res[8:16]
        tail = jnp.where(lane < 64, mid, pltpu.roll(mid, 4, 0))
        t = owner[c]
        r = count[t]
        count[t] = r + 1
        base = pl.multiple_of((t // 8) * 8, 8)
        mine = sub == t % 8
        for k in range(12):
            row = main[k : k + 1] if k < 8 else tail[k - 8 : k - 7]
            at = pl.multiple_of(r * 1536 + 128 * k, 128)
            pltpu.store(out.at[pl.ds(base, 8), pl.ds(at, 128)], jnp.broadcast_to(row, (8, 128)), mask=mine)
        label = jnp.full((8, 128), block[c].astype(f32))
        pltpu.store(out.at[pl.ds(base, 8), 3072:3200], label, mask=mine & (lane == r))

    def step(n, carry):
        for m in range(16):
            one(n * 16 + m, m)
        return carry

    lax.fori_loop(0, cells // 16, step, 0)


def spread(owner, block, positions, stiffness, triangles, neighbours, devices):
    cells, _, verts = positions.shape
    nv = -(-verts // 256) * 256
    inputs = (owner, block, stiffness, jnp.transpose(positions, (1, 2, 0)), jnp.transpose(triangles), jnp.transpose(neighbours))
    hbm = pl.BlockSpec(memory_space=pltpu.HBM)
    vmem = pl.BlockSpec(memory_space=pltpu.VMEM)
    return pl.pallas_call(
        spread_kernel,
        out_shape=jax.ShapeDtypeStruct((devices, WIDE), f32),
        in_specs=[hbm] * 6,
        out_specs=vmem,
        scratch_shapes=[
            pltpu.SMEM((cells,), i32),
            pltpu.SMEM((cells,), i32),
            pltpu.SMEM((cells,), f32),
            pltpu.VMEM((3, verts, cells), f32),
            pltpu.VMEM((3, triangles.shape[0]), i32),
            pltpu.VMEM((6, 32), i32),
            pltpu.SemaphoreType.DMA((6,)),
            pltpu.VMEM((nv, triangles.shape[0]), bf16),
            pltpu.VMEM((3, cells, nv), f32),
            pltpu.VMEM((3, cells, nv), f32),
            pltpu.VMEM((16, 8, nv), f32),
            pltpu.SMEM((devices,), i32),
        ],
        compiler_params=pltpu.CompilerParams(vmem_limit_bytes=48 << 20),
        name="spread",
    )(*[pltpu.with_memory_space_constraint(x, pltpu.HBM) for x in inputs])


def lane_take(x, index):
    return jnp.take_along_axis(x, index, axis=1)


def find(n_gx, n_gy, me_x, me_y, near, got, square):
    square[...] = jnp.full((128, 128), -1.0, f32)
    square[0:6, 0:32] = near[...].astype(f32)
    ids = jnp.transpose(square[...])[0:32]
    known = got[:, 3200:3328]
    k_hi = known.astype(bf16)
    k_lo = (known - k_hi.astype(f32)).astype(bf16)
    lane = lax.broadcasted_iota(i32, (32, 128), 1)
    hop = ids.astype(i32)
    for f1 in range(2, 6):
        first = jnp.broadcast_to(ids[:, f1 : f1 + 1], (32, 128)).astype(i32)
        safe = jnp.maximum(first, 0)
        owner = lax.shift_right_logical(safe, 5)
        pick = (owner == lane).astype(f32).astype(bf16)
        rows = jnp.dot(pick, k_hi, preferred_element_type=f32) + jnp.dot(pick, k_lo, preferred_element_type=f32)
        for n, q in enumerate(EDGE_Q):
            d1, d2 = [d for d in range(3) if vel[q][d]]
            if f1 == 2 * d2 + (0 if vel[q][d2] == 1 else 1):
                f2 = 2 * d1 + (0 if vel[q][d1] == 1 else 1)
                second = jnp.take_along_axis(rows, f2 * 32 + lax.bitwise_and(safe, 31), axis=1)
                second = jnp.where(first >= 0, second.astype(i32), -1)
                hop = jnp.where(lane == 6 + n, second, hop)
    safe = jnp.maximum(hop, 0)
    owner = lax.shift_right_logical(safe, 5)
    slot = lax.bitwise_and(safe, 31)
    reach = jnp.where(lane < 6, 1, 2)
    x = lax.rem(lax.div(owner, n_gy) - me_x + reach + n_gx, n_gx)
    y = lax.rem(lax.rem(owner, n_gy) - me_y + reach + n_gy, n_gy)
    column = jnp.where(x == 0, 48, jnp.where(x == 4, 49, (x - 1) * 16 + EDGE_TILE))
    edge = jnp.where(y == 0, 150 + x, jnp.where(y == 4, 155 + x, (y - 1) * 50 + column))
    tile = jnp.where(lane < 6, y * 50 + x * 16, edge)
    return jnp.where(hop >= 0, tile * 32 + slot, NOWHERE)


def collide_kernel(sizes, near, got, pops, post, table, where_, body, square):
    slots = got.shape[0]
    n_gx, n_gy = sizes
    me_x, me_y = lax.axis_index("gx"), lax.axis_index("gy")
    where_[...] = find(n_gx, n_gy, me_x, me_y, near, got, square)
    lane = lax.broadcasted_iota(i32, (slots, 128), 1)
    ids = got[:, 3072:3200]
    picks = []
    for r in range(2):
        col = jnp.broadcast_to(ids[:, r : r + 1], (slots, 128))
        hit = (col == lane.astype(f32)).astype(f32)
        picks.append(jnp.transpose(hit)[0:32].astype(bf16))
    for n in range(3):
        total = jnp.zeros((32, 512), f32)
        for r in range(2):
            part = got[:, r * 1536 + n * 512 : r * 1536 + (n + 1) * 512]
            hi = part.astype(bf16)
            lo = (part - hi.astype(f32)).astype(bf16)
            total = total + jnp.dot(picks[r], hi, preferred_element_type=f32)
            total = total + jnp.dot(picks[r], lo, preferred_element_type=f32)
        body[n] = total
    lanes = lax.broadcasted_iota(i32, (8, 128), 1)
    low = lanes < 64
    keep = 1.0 - 1.0 / relax_time
    gain = 1.0 - 0.5 / relax_time

    def group(g, carry):
        rows = pl.ds(pl.multiple_of(g * 8, 8), 8)
        for a in range(4):
            cut = slice(128 * a, 128 * (a + 1))
            f = [pops[q, rows, cut] * wts[q] for q in range(19)]
            force = [body[d, rows, cut] for d in range(3)]
            rho = f[0]
            for q in range(1, 19):
                rho = rho + f[q]
            u = []
            for d in range(3):
                m = 0.5 * force[d]
                for q in range(1, 19):
                    if vel[q][d] == 1:
                        m = m + f[q]
                    elif vel[q][d] == -1:
                        m = m - f[q]
                u.append(m / rho)
            speed = u[0] * u[0] + u[1] * u[1] + u[2] * u[2]
            work = u[0] * force[0] + u[1] * force[1] + u[2] * force[2]
            rho_t = rho * (1.0 / relax_time)
            flat = rho_t * (1.0 - 1.5 * speed) - (3.0 * gain) * work
            post[0, rows, cut] = keep * f[0] + wts[0] * flat
            for q in range(1, 19, 2):
                along = push = None
                for d in range(3):
                    e = vel[q][d]
                    if e:
                        along = e * u[d] if along is None else along + e * u[d]
                        push = e * force[d] if push is None else push + e * force[d]
                even = wts[q] * (flat + along * (4.5 * rho_t * along + (9.0 * gain) * push))
                odd = wts[q] * (3.0 * rho_t * along + (3.0 * gain) * push)
                post[q, rows, cut] = keep * f[q] + (even + odd)
                post[q + 1, rows, cut] = keep * f[q + 1] + (even - odd)
        for n in range(5):
            table[n, rows, :] = jnp.where(low, post[NEG[0][n], rows, 0:128], post[POS[0][n], rows, 384:512])
            m = lanes % 64
            first, second = m // 8, m % 8
            for ax in (1, 2):
                picked = None
                for a in range(4):
                    inside = (first % 2) * 64
                    if ax == 1:
                        at_low, at_high = inside + second, inside + 56 + second
                    else:
                        at_low, at_high = inside + second * 8, inside + second * 8 + 7
                    cut = slice(128 * a, 128 * (a + 1))
                    val = jnp.where(
                        low, lane_take(post[NEG[ax][n], rows, cut], at_low), lane_take(post[POS[ax][n], rows, cut], at_high)
                    )
                    picked = val if picked is None else jnp.where(first // 2 == a, val, picked)
                table[5 * ax + n, rows, :] = picked
        line = jnp.zeros((8, 128), f32)
        w = lanes % 8
        for n, q in enumerate(EDGE_Q):
            ex, ey, ez = vel[q]
            at = [7 if e == 1 else 0 for e in vel[q]]
            mine = lanes // 8 == n
            if ex:
                a = 3 if ex == 1 else 0
                base = 64 if ex == 1 else 0
                where_ = base + (at[1] * 8 + w if ey else w * 8 + at[2])
                val = lane_take(post[q, rows, 128 * a : 128 * (a + 1)], where_)
                line = jnp.where(mine, val, line)
            else:
                where_ = (w % 2) * 64 + at[1] * 8 + at[2]
                for a in range(4):
                    val = lane_take(post[q, rows, 128 * a : 128 * (a + 1)], where_)
                    line = jnp.where(mine & (w // 2 == a), val, line)
        table[EDGE_TILE, rows, :] = line
        return carry

    lax.fori_loop(0, 4, group, 0)


def collide(got, populations, neighbours):
    vmem = pl.BlockSpec(memory_space=pltpu.VMEM)
    sizes = (lax.axis_size("gx"), lax.axis_size("gy"))
    return pl.pallas_call(
        functools.partial(collide_kernel, sizes),
        out_shape=(
            jax.ShapeDtypeStruct((19, 32, 512), f32),
            jax.ShapeDtypeStruct((NT, 32, 128), f32),
            jax.ShapeDtypeStruct((32, 128), i32),
        ),
        in_specs=[vmem, vmem, vmem],
        out_specs=(vmem, vmem, vmem),
        scratch_shapes=[
            pltpu.VMEM((3, 32, 512), f32),
            pltpu.VMEM((128, 128), f32),
        ],
        compiler_params=pltpu.CompilerParams(vmem_limit_bytes=48 << 20),
        name="collide",
    )(jnp.transpose(neighbours), got, jnp.transpose(populations, (1, 0, 2)))


def stream_kernel(where_in, post, mid, down, up, down2, up2, out, table, ghost, where_, sem):
    parts = [(mid, 50, 50), (down, 0, 50), (up, 100, 50), (down2, 150, 5), (up2, 155, 5)]
    copies = [pltpu.make_async_copy(where_in, where_, sem.at[5])] + [
        pltpu.make_async_copy(ref, table.at[pl.ds(at * 32, size * 32)], sem.at[n])
        for n, (ref, at, size) in enumerate(parts)
    ]
    for c in copies:
        c.start()
    table[NOWHERE:, :] = jnp.full((NT * 32, 128), jnp.nan, f32)
    for c in copies:
        c.wait()
    lanes = lax.broadcasted_iota(i32, (8, 128), 1)
    sub = lax.broadcasted_iota(i32, (8, 128), 0)

    def row_of(at, tile):
        return table[pl.ds(at + 32 * tile, 8, stride=0), :]

    def fetch(g, carry):
        rows = pl.ds(pl.multiple_of(g * 8, 8), 8)
        for ax in range(3):
            made = [jnp.zeros((8, 128), f32)] * 5
            for i in range(8):
                low_at = where_[g * 8 + i, 2 * ax]
                high_at = where_[g * 8 + i, 2 * ax + 1]
                for n in range(5):
                    t = 5 * ax + n
                    both = jnp.where(lanes < 64, row_of(high_at, t), row_of(low_at, t))
                    made[n] = jnp.where(sub == i, both, made[n])
            for n in range(5):
                ghost[5 * ax + n, rows, :] = made[n]
        line = jnp.zeros((8, 128), f32)
        for i in range(8):
            for n in range(12):
                at = where_[g * 8 + i, 6 + n]
                line = jnp.where((lanes // 8 == n) & (sub == i), row_of(at, 0), line)
        ghost[EDGE_TILE, rows, :] = line
        return carry

    lax.fori_loop(0, 4, fetch, 0)
    jj = (lanes // 8) % 8
    kk = lanes % 8

    def group(g, carry):
        rows = pl.ds(pl.multiple_of(g * 8, 8), 8)
        edges = ghost[EDGE_TILE, rows, :]
        out[0, rows, :] = post[0, rows, :]
        for q in range(1, 19):
            e = vel[q]
            ex, ey, ez = e
            shift = ex * 64 + ey * 8 + ez
            tiles = [post[q, rows, 128 * a : 128 * (a + 1)] for a in range(4)]
            rolled = [pltpu.roll(t, shift % 128, 1) for t in tiles]
            for a in range(4):
                if shift > 0:
                    val = jnp.where(lanes < shift, rolled[(a - 1) % 4], rolled[a])
                else:
                    val = jnp.where(lanes >= 128 + shift, rolled[(a + 1) % 4], rolled[a])
                ii = 2 * a + lanes // 64
                back = post[opposite[q], rows, 128 * a : 128 * (a + 1)]
                coords = (ii, jj, kk)
                crossing = [None if e[d] == 0 else coords[d] == (0 if e[d] == 1 else 7) for d in range(3)]
                if ex == 1 and a != 0 or ex == -1 and a != 3:
                    crossing[0] = None
                axes = [d for d in range(3) if crossing[d] is not None]
                if axes:
                    out_of = crossing[axes[0]]
                    for d in axes[1:]:
                        out_of = out_of | crossing[d]
                    val = jnp.where(out_of, back, val)
                for d in axes:
                    n = (POS[d] if e[d] == 1 else NEG[d]).index(q)
                    source = ghost[5 * d + n, rows, :]
                    base = 64 if e[d] == 1 else 0
                    if d == 0:
                        brought = pltpu.roll(source, (64 + ey * 8 + ez) % 128, 1)
                    elif d == 1:
                        brought = lane_take(source, base + ((ii - ex) * 8 + kk - ez) % 64)
                    else:
                        brought = lane_take(source, base + ((ii - ex) * 8 + jj - ey) % 64)
                    use = crossing[d] & (brought == brought)
                    for other in axes:
                        if other != d:
                            use = use & ~crossing[other]
                    val = jnp.where(use, brought, val)
                if len(axes) == 2:
                    n = q - 7
                    along = kk if ez == 0 else (jj if ey == 0 else ii)
                    brought = lane_take(edges, 8 * n + along)
                    val = jnp.where(crossing[axes[0]] & crossing[axes[1]] & (brought == brought), brought, val)
                out[q, rows, 128 * a : 128 * (a + 1)] = val
        return carry

    lax.fori_loop(0, 4, group, 0)


def stream(where_, post, *parts):
    vmem = pl.BlockSpec(memory_space=pltpu.VMEM)
    anywhere = pl.BlockSpec(memory_space=pl.ANY)
    return pl.pallas_call(
        stream_kernel,
        out_shape=jax.ShapeDtypeStruct((19, 32, 512), f32),
        in_specs=[anywhere, vmem] + [anywhere] * 5,
        out_specs=vmem,
        scratch_shapes=[
            pltpu.VMEM(((160 + NT) * 32, 128), f32),
            pltpu.VMEM((NT, 32, 128), f32),
            pltpu.SMEM((32, 128), i32),
            pltpu.SemaphoreType.DMA((6,)),
        ],
        compiler_params=pltpu.CompilerParams(vmem_limit_bytes=48 << 20),
        name="stream",
    )(where_, post, *[p.reshape(-1, 128) for p in parts])


def send(array, axis, step):
    size = lax.axis_size(axis)
    return lax.ppermute(array, axis, [(i, (i + step) % size) for i in range(size)])


def exchange(table):
    edge = table[EDGE_TILE : EDGE_TILE + 1]
    left, right = send(table, "gx", 1), send(table, "gx", -1)
    left2, right2 = send(edge, "gx", 2), send(edge, "gx", -2)
    mid = jnp.concatenate([left, table, right, left2, right2], axis=0)
    edges = jnp.concatenate([left2, left[EDGE_TILE:], edge, right[EDGE_TILE:], right2], axis=0)
    return mid, send(mid, "gy", 1), send(mid, "gy", -1), send(edges, "gy", 2), send(edges, "gy", -2)


def body(populations, neighbours, positions, stiffness, cell_owner, cell_block, triangles):
    devices = lax.axis_size("gx") * lax.axis_size("gy")
    slots = spread(cell_owner[:, 0], cell_block, positions, stiffness, triangles, neighbours, devices)
    got = lax.all_to_all(slots, BOTH, split_axis=0, concat_axis=0, tiled=True)
    post, table, where_ = collide(got, populations, neighbours)
    result = stream(where_, post, *exchange(table))
    return jnp.transpose(result, (1, 0, 2))


def solution(mesh):
    placed = (
        P(BOTH, None, None),
        P(BOTH, None),
        P(BOTH, None, None),
        P(BOTH),
        P(BOTH, None),
        P(BOTH),
        P(),
    )
    return jax.shard_map(
        body, mesh=mesh, in_specs=placed, out_specs=P(BOTH, None, None), check_vma=False
    )
```

```python
import functools

import jax
import jax.numpy as jnp
import numpy as np
from jax import lax
from jax.experimental import pallas as pl
from jax.experimental.pallas import tpu as pltpu
from jax.sharding import PartitionSpec as P

vel = [
    (0, 0, 0), (1, 0, 0), (-1, 0, 0), (0, 1, 0), (0, -1, 0), (0, 0, 1), (0, 0, -1),
    (1, 1, 0), (-1, -1, 0), (1, -1, 0), (-1, 1, 0),
    (1, 0, 1), (-1, 0, -1), (1, 0, -1), (-1, 0, 1),
    (0, 1, 1), (0, -1, -1), (0, 1, -1), (0, -1, 1),
]
wts = [1.0 / 3.0] + [1.0 / 18.0] * 6 + [1.0 / 36.0] * 12
opposite = [0, 2, 1, 4, 3, 6, 5, 8, 7, 10, 9, 12, 11, 14, 13, 16, 15, 18, 17]
relax_time = 0.6
NEG, POS = {}, {}
for ax in range(3):
    NEG[ax] = [q for q in range(19) if vel[q][ax] == -1]
    POS[ax] = [q for q in range(19) if vel[q][ax] == 1]
EDGE_Q = list(range(7, 19))
FACE_TILES = 15
EDGE_TILE = 15
NT = 16
IDS = 96
HAVE = 114
WIDE = 3328
BOTH = ("gx", "gy")
f32, bf16, i32 = jnp.float32, jnp.bfloat16, jnp.int32


def nt_dot(a, b):
    return lax.dot_general(a, b, (((1,), (1,)), ((), ())), preferred_element_type=f32)


def hat(x, grid):
    return jnp.maximum(0.0, 1.0 - jnp.abs(x - grid))


def spread_kernel(owner_in, block_in, stiff_in, raw_in, tri_in, near_in, out, owner, block, stiff, raw, tri, near, sem, st, pos, force, hats, count):
    cells, nv = pos.shape[1:]
    verts = raw.shape[1]
    pairs = ((tri_in, tri), (raw_in, raw), (near_in, near), (owner_in, owner), (block_in, block), (stiff_in, stiff))
    copies = [pltpu.make_async_copy(a, b, sem.at[n]) for n, (a, b) in enumerate(pairs)]
    for c in copies:
        c.start()
    for c in copies:
        c.wait()
    for r in range(0, nv, 128):
        ids = lax.broadcasted_iota(i32, (128, tri.shape[1]), 0) + r
        hit = (ids == tri[0:1, :]) | (ids == tri[1:2, :]) | (ids == tri[2:3, :])
        st[r : r + 128, :] = hit.astype(f32).astype(bf16)
        for d in range(3):
            have = min(verts - r, 128)
            piece = raw[d, r : r + have, :]
            if have < 128:
                piece = jnp.concatenate([piece, jnp.full((128 - have, cells), -100.0, f32)], axis=0)
            pos[d, :, r : r + 128] = jnp.transpose(piece)
    links = nt_dot(st[...], st[...])
    rows = lax.broadcasted_iota(i32, (nv, nv), 0)
    cols = lax.broadcasted_iota(i32, (nv, nv), 1)
    springs = jnp.where(rows == cols, -2.0 * links, links)
    s_hi = springs.astype(bf16)
    s_lo = (springs - s_hi.astype(f32)).astype(bf16)
    for d in range(3):
        x = pos[d]
        x_hi = x.astype(bf16)
        x_lo = (x - x_hi.astype(f32)).astype(bf16)
        force[d] = (
            jnp.dot(x_hi, s_hi, preferred_element_type=f32)
            + jnp.dot(x_lo, s_hi, preferred_element_type=f32)
            + jnp.dot(x_hi, s_lo, preferred_element_type=f32)
        )
    sub = lax.broadcasted_iota(i32, (8, 128), 0)
    lane = lax.broadcasted_iota(i32, (8, 128), 1)
    slots = out.shape[0]
    tail_row = jnp.full((8, 128), -1.0, f32)
    table_row = jnp.zeros((8, 128), f32)
    for f in range(4):
        one_face = jnp.concatenate([near[f + 2 : f + 3, :].astype(f32), jnp.zeros((1, 96), f32)], axis=1)
        one_face = jnp.broadcast_to(one_face, (8, 128))
        table_row = jnp.where(lane // 32 == f, pltpu.roll(one_face, 32 * f, 1) if f else one_face, table_row)
    out[:, 0:3072] = jnp.zeros((slots, 3072), f32)

    def clear(t, carry):
        base = pl.ds(pl.multiple_of(t * 8, 8), 8)
        out[base, 3072:3200] = tail_row
        out[base, 3200:3328] = table_row
        for m in range(8):
            count[t * 8 + m] = 0
        return carry

    lax.fori_loop(0, slots // 8, clear, 0)
    sub8 = lax.broadcasted_iota(i32, (8, nv), 0)
    g_even = (2 * (sub8 % 4)).astype(f32)
    g_odd = g_even + 1.0
    g_all = sub8.astype(f32)
    first4 = sub8 < 4

    def one(c, m):
        x = jnp.broadcast_to(pos[0, pl.ds(c, 1), :], (8, nv))
        y = jnp.broadcast_to(pos[1, pl.ds(c, 1), :], (8, nv))
        z = jnp.broadcast_to(pos[2, pl.ds(c, 1), :], (8, nv))
        f0 = jnp.broadcast_to(force[0, pl.ds(c, 1), :], (8, nv))
        f1 = jnp.broadcast_to(force[1, pl.ds(c, 1), :], (8, nv))
        f2 = jnp.broadcast_to(force[2, pl.ds(c, 1), :], (8, nv))
        h_even = hat(x, g_even)
        h_odd = hat(x, g_odd)
        f01 = jnp.where(first4, f0, f1)
        left = jnp.concatenate(
            [h_even * f01, jnp.where(first4, h_even, h_odd) * f2, h_odd * f01], axis=0
        )
        l_lo = left - left.astype(bf16).astype(f32)
        left2 = jnp.concatenate([left, l_lo], axis=0).astype(bf16)
        hats[m] = hat(y, g_all)
        hz = hat(z, g_all)
        plane = jnp.concatenate(
            [jnp.broadcast_to(hats[m, j : j + 1, :], (8, nv)) * hz for j in range(8)], axis=0
        )
        p_hi = plane.astype(bf16)
        p_lo = (plane - p_hi.astype(f32)).astype(bf16)
        prod = nt_dot(left2, jnp.concatenate([p_hi, p_lo], axis=0))
        both = prod[0:24] + prod[24:48]
        res = (both + pltpu.roll(both, 64, 1)) * stiff[c]
        main = jnp.where(lane < 64, res[0:8], res[16:24])
        mid = res[8:16]
        tail = jnp.where(lane < 64, mid, pltpu.roll(mid, 4, 0))
        t = owner[c]
        r = count[t]
        count[t] = r + 1
        base = pl.multiple_of((t // 8) * 8, 8)
        mine = sub == t % 8
        for k in range(12):
            row = main[k : k + 1] if k < 8 else tail[k - 8 : k - 7]
            at = pl.multiple_of(r * 1536 + 128 * k, 128)
            pltpu.store(out.at[pl.ds(base, 8), pl.ds(at, 128)], jnp.broadcast_to(row, (8, 128)), mask=mine)
        label = jnp.full((8, 128), block[c].astype(f32))
        pltpu.store(out.at[pl.ds(base, 8), 3072:3200], label, mask=mine & (lane == r))

    def step(n, carry):
        for m in range(16):
            one(n * 16 + m, m)
        return carry

    lax.fori_loop(0, cells // 16, step, 0)


def spread(owner, block, positions, stiffness, triangles, neighbours, devices):
    cells, _, verts = positions.shape
    nv = -(-verts // 256) * 256
    inputs = (owner, block, stiffness, jnp.transpose(positions, (1, 2, 0)), jnp.transpose(triangles), jnp.transpose(neighbours))
    hbm = pl.BlockSpec(memory_space=pltpu.HBM)
    vmem = pl.BlockSpec(memory_space=pltpu.VMEM)
    return pl.pallas_call(
        spread_kernel,
        out_shape=jax.ShapeDtypeStruct((devices, WIDE), f32),
        in_specs=[hbm] * 6,
        out_specs=vmem,
        scratch_shapes=[
            pltpu.SMEM((cells,), i32),
            pltpu.SMEM((cells,), i32),
            pltpu.SMEM((cells,), f32),
            pltpu.VMEM((3, verts, cells), f32),
            pltpu.VMEM((3, triangles.shape[0]), i32),
            pltpu.VMEM((6, 32), i32),
            pltpu.SemaphoreType.DMA((6,)),
            pltpu.VMEM((nv, triangles.shape[0]), bf16),
            pltpu.VMEM((3, cells, nv), f32),
            pltpu.VMEM((3, cells, nv), f32),
            pltpu.VMEM((16, 8, nv), f32),
            pltpu.SMEM((devices,), i32),
        ],
        compiler_params=pltpu.CompilerParams(vmem_limit_bytes=48 << 20),
        name="spread",
    )(*[pltpu.with_memory_space_constraint(x, pltpu.HBM) for x in inputs])


def lane_take(x, index):
    return jnp.take_along_axis(x, index, axis=1)


def find(near, got, square):
    square[...] = jnp.full((128, 128), -1.0, f32)
    square[0:6, 0:32] = near[...].astype(f32)
    goal = jnp.transpose(square[...])[0:32]
    known = got[:, 3200:3328]
    k_hi = known.astype(bf16)
    k_lo = (known - k_hi.astype(f32)).astype(bf16)
    lane = lax.broadcasted_iota(i32, (32, 128), 1)
    for f1 in range(4):
        first = jnp.broadcast_to(goal[:, f1 : f1 + 1], (32, 128)).astype(i32)
        safe = jnp.maximum(first, 0)
        pick = (lax.shift_right_logical(safe, 5) == lane).astype(f32).astype(bf16)
        rows = jnp.dot(pick, k_hi, preferred_element_type=f32) + jnp.dot(pick, k_lo, preferred_element_type=f32)
        for n, q in enumerate(EDGE_Q):
            d1, d2 = [d for d in range(3) if vel[q][d]]
            if f1 == 2 * d1 + (1 if vel[q][d1] == 1 else 0):
                f2 = 2 * d2 + (1 if vel[q][d2] == 1 else 0)
                second = jnp.take_along_axis(rows, (f2 - 2) * 32 + lax.bitwise_and(safe, 31), axis=1)
                goal = jnp.where(lane == 6 + n, jnp.where(first >= 0, second, -1.0), goal)
    return goal


def collide_kernel(near, got, pops, post, table, goal, body, square):
    slots = got.shape[0]
    goal[...] = find(near, got, square)
    lane = lax.broadcasted_iota(i32, (slots, 128), 1)
    ids = got[:, 3072:3200]
    picks = []
    for r in range(2):
        col = jnp.broadcast_to(ids[:, r : r + 1], (slots, 128))
        hit = (col == lane.astype(f32)).astype(f32)
        picks.append(jnp.transpose(hit)[0:32].astype(bf16))
    for n in range(3):
        total = jnp.zeros((32, 512), f32)
        for r in range(2):
            part = got[:, r * 1536 + n * 512 : r * 1536 + (n + 1) * 512]
            hi = part.astype(bf16)
            lo = (part - hi.astype(f32)).astype(bf16)
            total = total + jnp.dot(picks[r], hi, preferred_element_type=f32)
            total = total + jnp.dot(picks[r], lo, preferred_element_type=f32)
        body[n] = total
    lanes = lax.broadcasted_iota(i32, (8, 128), 1)
    low = lanes < 64
    keep = 1.0 - 1.0 / relax_time
    gain = 1.0 - 0.5 / relax_time

    def group(g, carry):
        rows = pl.ds(pl.multiple_of(g * 8, 8), 8)
        for a in range(4):
            cut = slice(128 * a, 128 * (a + 1))
            f = [pops[q, rows, cut] * wts[q] for q in range(19)]
            force = [body[d, rows, cut] for d in range(3)]
            rho = f[0]
            for q in range(1, 19):
                rho = rho + f[q]
            u = []
            for d in range(3):
                m = 0.5 * force[d]
                for q in range(1, 19):
                    if vel[q][d] == 1:
                        m = m + f[q]
                    elif vel[q][d] == -1:
                        m = m - f[q]
                u.append(m / rho)
            speed = u[0] * u[0] + u[1] * u[1] + u[2] * u[2]
            work = u[0] * force[0] + u[1] * force[1] + u[2] * force[2]
            rho_t = rho * (1.0 / relax_time)
            flat = rho_t * (1.0 - 1.5 * speed) - (3.0 * gain) * work
            post[0, rows, cut] = keep * f[0] + wts[0] * flat
            for q in range(1, 19, 2):
                along = push = None
                for d in range(3):
                    e = vel[q][d]
                    if e:
                        along = e * u[d] if along is None else along + e * u[d]
                        push = e * force[d] if push is None else push + e * force[d]
                even = wts[q] * (flat + along * (4.5 * rho_t * along + (9.0 * gain) * push))
                odd = wts[q] * (3.0 * rho_t * along + (3.0 * gain) * push)
                post[q, rows, cut] = keep * f[q] + (even + odd)
                post[q + 1, rows, cut] = keep * f[q + 1] + (even - odd)
        for n in range(5):
            table[n, rows, :] = jnp.where(low, post[NEG[0][n], rows, 0:128], post[POS[0][n], rows, 384:512])
            m = lanes % 64
            first, second = m // 8, m % 8
            for ax in (1, 2):
                picked = None
                for a in range(4):
                    inside = (first % 2) * 64
                    if ax == 1:
                        at_low, at_high = inside + second, inside + 56 + second
                    else:
                        at_low, at_high = inside + second * 8, inside + second * 8 + 7
                    cut = slice(128 * a, 128 * (a + 1))
                    val = jnp.where(
                        low, lane_take(post[NEG[ax][n], rows, cut], at_low), lane_take(post[POS[ax][n], rows, cut], at_high)
                    )
                    picked = val if picked is None else jnp.where(first // 2 == a, val, picked)
                table[5 * ax + n, rows, :] = picked
        line = jnp.where(lanes < HAVE, pltpu.roll(goal[rows, :], IDS, 1), 1.0)
        w = lanes % 8
        for n, q in enumerate(EDGE_Q):
            ex, ey, ez = vel[q]
            at = [7 if e == 1 else 0 for e in vel[q]]
            mine = lanes // 8 == n
            if ex:
                a = 3 if ex == 1 else 0
                base = 64 if ex == 1 else 0
                where_ = base + (at[1] * 8 + w if ey else w * 8 + at[2])
                val = lane_take(post[q, rows, 128 * a : 128 * (a + 1)], where_)
                line = jnp.where(mine, val, line)
            else:
                where_ = (w % 2) * 64 + at[1] * 8 + at[2]
                for a in range(4):
                    val = lane_take(post[q, rows, 128 * a : 128 * (a + 1)], where_)
                    line = jnp.where(mine & (w // 2 == a), val, line)
        table[EDGE_TILE, rows, :] = line
        return carry

    lax.fori_loop(0, 4, group, 0)


def collide(got, populations, neighbours):
    vmem = pl.BlockSpec(memory_space=pltpu.VMEM)
    return pl.pallas_call(
        collide_kernel,
        out_shape=(
            jax.ShapeDtypeStruct((19, 32, 512), f32),
            jax.ShapeDtypeStruct((NT, 32, 128), f32),
            jax.ShapeDtypeStruct((32, 128), f32),
        ),
        in_specs=[vmem, vmem, vmem],
        out_specs=(vmem, vmem, vmem),
        scratch_shapes=[
            pltpu.VMEM((3, 32, 512), f32),
            pltpu.VMEM((128, 128), f32),
        ],
        compiler_params=pltpu.CompilerParams(vmem_limit_bytes=48 << 20),
        name="collide",
    )(jnp.transpose(neighbours), got, jnp.transpose(populations, (1, 0, 2)))


def route_kernel(sizes, left2, left, mine, right, right2, down, own, up, down2, up2, lines):
    n_gy = sizes[1]
    me_x, me_y = lax.axis_index("gx"), lax.axis_index("gy")
    for n, part in enumerate((left[EDGE_TILE], mine[EDGE_TILE], right[EDGE_TILE], left2[0], right2[0])):
        lines[32 * n : 32 * (n + 1), :] = part
    lines[160:256, :] = jnp.full((96, 128), -1.0, f32)
    ids = [jnp.transpose(lines[0:128, :]), jnp.transpose(lines[128:256, :])]
    slot = lax.broadcasted_iota(i32, (32, 128), 0).astype(f32)
    low = lax.broadcasted_iota(i32, (32, 128), 1) < 64
    named = {}
    for dy in range(-2, 3):
        owner = me_x * n_gy + lax.rem(me_y + (dy + n_gy), n_gy)
        named[dy] = slot + (owner * 32).astype(f32)

    def hot(half, row, dy):
        picked = jnp.broadcast_to(ids[half][IDS + row : IDS + row + 1, :], (32, 128)) == named[dy]
        return picked.astype(f32)

    none = jnp.zeros((32, 128), f32)
    for ax in range(3):
        planes = jnp.concatenate(
            [
                jnp.concatenate([left[t], mine[t], right[t], none], axis=0)
                for t in range(5 * ax, 5 * ax + 5)
            ],
            axis=1,
        )
        p_hi = planes.astype(bf16)
        p_lo = (planes - p_hi.astype(f32)).astype(bf16)
        picks = jnp.concatenate([hot(0, 2 * ax + s, dy) for s in range(2) for dy in (-1, 0, 1)], axis=0).astype(bf16)
        moved = jnp.dot(picks, p_hi, preferred_element_type=f32) + jnp.dot(picks, p_lo, preferred_element_type=f32)
        for k, goal in enumerate((down, own, up)):
            for n in range(5):
                cut = slice(128 * n, 128 * (n + 1))
                goal[5 * ax + n] = jnp.where(
                    low, moved[32 * k : 32 * (k + 1), cut], moved[96 + 32 * k : 96 + 32 * (k + 1), cut]
                )
    e_hi = lines[...].astype(bf16)
    e_lo = (lines[...] - e_hi.astype(f32)).astype(bf16)
    both = jnp.concatenate([e_hi, e_lo], axis=1)
    lane = lax.broadcasted_iota(i32, (160, 128), 1)
    total = jnp.zeros((160, 128), f32)
    for n in range(12):
        picks = jnp.concatenate(
            [jnp.concatenate([hot(h, 6 + n, dy) for dy in range(-2, 3)], axis=0) for h in range(2)], axis=1
        ).astype(bf16)
        moved = jnp.dot(picks, both, preferred_element_type=f32)
        wanted = (lane // 8 == n) | (lane == HAVE + n)
        total = jnp.where(wanted, moved[:, 0:128] + moved[:, 128:256], total)
    for k, goal in enumerate((down2, down, own, up, up2)):
        goal[goal.shape[0] - 1] = total[32 * k : 32 * (k + 1)]


def route(left2, left, mine, right, right2):
    vmem = pl.BlockSpec(memory_space=pltpu.VMEM)
    sizes = (lax.axis_size("gx"), lax.axis_size("gy"))
    big = jax.ShapeDtypeStruct(mine.shape, f32)
    small = jax.ShapeDtypeStruct(left2.shape, f32)
    return pl.pallas_call(
        functools.partial(route_kernel, sizes),
        out_shape=(big, big, big, small, small),
        in_specs=[vmem] * 5,
        out_specs=(vmem,) * 5,
        scratch_shapes=[pltpu.VMEM((256, 128), f32)],
        compiler_params=pltpu.CompilerParams(vmem_limit_bytes=48 << 20),
        name="route",
    )(left2, left, mine, right, right2)


def stream_kernel(goal, post, own, below, above, below2, above2, out):
    lanes = lax.broadcasted_iota(i32, (8, 128), 1)
    jj = (lanes // 8) % 8
    kk = lanes % 8

    def group(g, carry):
        rows = pl.ds(pl.multiple_of(g * 8, 8), 8)
        near = goal[rows, :]
        ghost = []
        for ax in range(3):
            have = lane_take(near, jnp.where(lanes < 64, 2 * ax + 1, 2 * ax)) >= 0.0
            for t in range(5 * ax, 5 * ax + 5):
                came = own[t, rows, :] + below[t, rows, :] + above[t, rows, :]
                ghost.append(jnp.where(have, came, jnp.nan))
        came = own[EDGE_TILE, rows, :] + below[EDGE_TILE, rows, :] + above[EDGE_TILE, rows, :]
        came = came + below2[0, rows, :] + above2[0, rows, :]
        have = lane_take(came, jnp.minimum(HAVE + lanes // 8, 127)) > 0.5
        edges = jnp.where(have, came, jnp.nan)
        out[0, rows, :] = post[0, rows, :]
        for q in range(1, 19):
            e = vel[q]
            ex, ey, ez = e
            shift = ex * 64 + ey * 8 + ez
            tiles = [post[q, rows, 128 * a : 128 * (a + 1)] for a in range(4)]
            rolled = [pltpu.roll(t, shift % 128, 1) for t in tiles]
            for a in range(4):
                if shift > 0:
                    val = jnp.where(lanes < shift, rolled[(a - 1) % 4], rolled[a])
                else:
                    val = jnp.where(lanes >= 128 + shift, rolled[(a + 1) % 4], rolled[a])
                ii = 2 * a + lanes // 64
                back = post[opposite[q], rows, 128 * a : 128 * (a + 1)]
                coords = (ii, jj, kk)
                crossing = [None if e[d] == 0 else coords[d] == (0 if e[d] == 1 else 7) for d in range(3)]
                if ex == 1 and a != 0 or ex == -1 and a != 3:
                    crossing[0] = None
                axes = [d for d in range(3) if crossing[d] is not None]
                if axes:
                    out_of = crossing[axes[0]]
                    for d in axes[1:]:
                        out_of = out_of | crossing[d]
                    val = jnp.where(out_of, back, val)
                for d in axes:
                    n = (POS[d] if e[d] == 1 else NEG[d]).index(q)
                    source = ghost[5 * d + n]
                    base = 64 if e[d] == 1 else 0
                    if d == 0:
                        brought = pltpu.roll(source, (64 + ey * 8 + ez) % 128, 1)
                    elif d == 1:
                        brought = lane_take(source, base + ((ii - ex) * 8 + kk - ez) % 64)
                    else:
                        brought = lane_take(source, base + ((ii - ex) * 8 + jj - ey) % 64)
                    use = crossing[d] & (brought == brought)
                    for other in axes:
                        if other != d:
                            use = use & ~crossing[other]
                    val = jnp.where(use, brought, val)
                if len(axes) == 2:
                    n = q - 7
                    along = kk if ez == 0 else (jj if ey == 0 else ii)
                    brought = lane_take(edges, 8 * n + along)
                    val = jnp.where(crossing[axes[0]] & crossing[axes[1]] & (brought == brought), brought, val)
                out[q, rows, 128 * a : 128 * (a + 1)] = val
        return carry

    lax.fori_loop(0, 4, group, 0)


def stream(goal, post, *parts):
    vmem = pl.BlockSpec(memory_space=pltpu.VMEM)
    return pl.pallas_call(
        stream_kernel,
        out_shape=jax.ShapeDtypeStruct((19, 32, 512), f32),
        in_specs=[vmem] * 7,
        out_specs=vmem,
        compiler_params=pltpu.CompilerParams(vmem_limit_bytes=48 << 20),
        name="stream",
    )(goal, post, *parts)


def send(array, axis, step):
    size = lax.axis_size(axis)
    return lax.ppermute(array, axis, [(i, (i + step) % size) for i in range(size)])


def exchange(table):
    edge = table[EDGE_TILE : EDGE_TILE + 1]
    left, right = send(table, "gx", 1), send(table, "gx", -1)
    left2, right2 = send(edge, "gx", 2), send(edge, "gx", -2)
    down, own, up, down2, up2 = route(left2, left, table, right, right2)
    return own, send(up, "gy", 1), send(down, "gy", -1), send(up2, "gy", 2), send(down2, "gy", -2)


def body(populations, neighbours, positions, stiffness, cell_owner, cell_block, triangles):
    devices = lax.axis_size("gx") * lax.axis_size("gy")
    slots = spread(cell_owner[:, 0], cell_block, positions, stiffness, triangles, neighbours, devices)
    got = lax.all_to_all(slots, BOTH, split_axis=0, concat_axis=0, tiled=True)
    post, table, goal = collide(got, populations, neighbours)
    result = stream(goal, post, *exchange(table))
    return jnp.transpose(result, (1, 0, 2))


def solution(mesh):
    placed = (
        P(BOTH, None, None),
        P(BOTH, None),
        P(BOTH, None, None),
        P(BOTH),
        P(BOTH, None),
        P(BOTH),
        P(),
    )
    return jax.shard_map(
        body, mesh=mesh, in_specs=placed, out_specs=P(BOTH, None, None), check_vma=False
    )
```

```python
import functools

import jax
import jax.numpy as jnp
import numpy as np
from jax import lax
from jax.experimental import pallas as pl
from jax.experimental.pallas import tpu as pltpu
from jax.sharding import PartitionSpec as P

vel = [
    (0, 0, 0), (1, 0, 0), (-1, 0, 0), (0, 1, 0), (0, -1, 0), (0, 0, 1), (0, 0, -1),
    (1, 1, 0), (-1, -1, 0), (1, -1, 0), (-1, 1, 0),
    (1, 0, 1), (-1, 0, -1), (1, 0, -1), (-1, 0, 1),
    (0, 1, 1), (0, -1, -1), (0, 1, -1), (0, -1, 1),
]
wts = [1.0 / 3.0] + [1.0 / 18.0] * 6 + [1.0 / 36.0] * 12
opposite = [0, 2, 1, 4, 3, 6, 5, 8, 7, 10, 9, 12, 11, 14, 13, 16, 15, 18, 17]
relax_time = 0.6
NEG, POS = {}, {}
for ax in range(3):
    NEG[ax] = [q for q in range(19) if vel[q][ax] == -1]
    POS[ax] = [q for q in range(19) if vel[q][ax] == 1]
EDGE_Q = list(range(7, 19))
FACE_TILES = 15
EDGE_TILE = 15
NT = 16
IDS = 96
HAVE = 114
WIDE = 3328
BOTH = ("gx", "gy")
f32, bf16, i32 = jnp.float32, jnp.bfloat16, jnp.int32


def nt_dot(a, b):
    return lax.dot_general(a, b, (((1,), (1,)), ((), ())), preferred_element_type=f32)


def hat(x, grid):
    return jnp.maximum(0.0, 1.0 - jnp.abs(x - grid))


def spread_kernel(owner_in, block_in, stiff_in, raw_in, tri_in, near_in, out, owner, block, stiff, raw, tri, near, sem, st, pos, force, hats, count):
    cells, nv = pos.shape[1:]
    verts = raw.shape[1]
    pairs = ((tri_in, tri), (raw_in, raw), (near_in, near), (owner_in, owner), (block_in, block), (stiff_in, stiff))
    copies = [pltpu.make_async_copy(a, b, sem.at[n]) for n, (a, b) in enumerate(pairs)]
    for c in copies:
        c.start()
    copies[0].wait()
    for r in range(0, nv, 128):
        ids = lax.broadcasted_iota(i32, (128, tri.shape[1]), 0) + r
        hit = (ids == tri[0:1, :]) | (ids == tri[1:2, :]) | (ids == tri[2:3, :])
        st[r : r + 128, :] = hit.astype(f32).astype(bf16)
    links = nt_dot(st[...], st[...])
    for c in copies[1:]:
        c.wait()
    for r in range(0, nv, 128):
        for d in range(3):
            have = min(verts - r, 128)
            piece = raw[d, r : r + have, :]
            if have < 128:
                piece = jnp.concatenate([piece, jnp.full((128 - have, cells), -100.0, f32)], axis=0)
            pos[d, :, r : r + 128] = jnp.transpose(piece)
    rows = lax.broadcasted_iota(i32, (nv, nv), 0)
    cols = lax.broadcasted_iota(i32, (nv, nv), 1)
    springs = jnp.where(rows == cols, -2.0 * links, links)
    s_hi = springs.astype(bf16)
    s_lo = (springs - s_hi.astype(f32)).astype(bf16)
    x = jnp.concatenate([pos[0], pos[1], pos[2]], axis=0)
    x_hi = x.astype(bf16)
    x_lo = (x - x_hi.astype(f32)).astype(bf16)
    most = jnp.dot(jnp.concatenate([x_hi, x_lo], axis=0), s_hi, preferred_element_type=f32)
    rest = jnp.dot(x_hi, s_lo, preferred_element_type=f32)
    for d in range(3):
        lo, hi = d * cells, (d + 1) * cells
        force[d] = most[lo:hi] + most[3 * cells + lo : 3 * cells + hi] + rest[lo:hi]
    sub = lax.broadcasted_iota(i32, (8, 128), 0)
    lane = lax.broadcasted_iota(i32, (8, 128), 1)
    slots = out.shape[0]
    tail_row = jnp.full((8, 128), -1.0, f32)
    table_row = jnp.zeros((8, 128), f32)
    for f in range(4):
        one_face = jnp.concatenate([near[f + 2 : f + 3, :].astype(f32), jnp.zeros((1, 96), f32)], axis=1)
        one_face = jnp.broadcast_to(one_face, (8, 128))
        table_row = jnp.where(lane // 32 == f, pltpu.roll(one_face, 32 * f, 1) if f else one_face, table_row)

    def clear(t, carry):
        for m in range(8):
            out[t * 8 + m, :, 0:3072] = jnp.zeros((1, 3072), f32)
            out[t * 8 + m, :, 3072:3200] = tail_row[0:1]
            out[t * 8 + m, :, 3200:3328] = table_row[0:1]
            count[t * 8 + m] = 0
        return carry

    lax.fori_loop(0, slots // 8, clear, 0)
    sub8 = lax.broadcasted_iota(i32, (8, nv), 0)
    g_even = (2 * (sub8 % 4)).astype(f32)
    g_odd = g_even + 1.0
    g_all = sub8.astype(f32)
    first4 = sub8 < 4

    def product(first, m):
        c = first + m
        near8 = pl.ds(pl.multiple_of(first + m // 8 * 8, 8), 8)
        x = jnp.broadcast_to(pos[0, near8, :][m % 8 : m % 8 + 1], (8, nv))
        y = jnp.broadcast_to(pos[1, near8, :][m % 8 : m % 8 + 1], (8, nv))
        z = jnp.broadcast_to(pos[2, near8, :][m % 8 : m % 8 + 1], (8, nv))
        f0 = jnp.broadcast_to(force[0, near8, :][m % 8 : m % 8 + 1], (8, nv))
        f1 = jnp.broadcast_to(force[1, near8, :][m % 8 : m % 8 + 1], (8, nv))
        f2 = jnp.broadcast_to(force[2, near8, :][m % 8 : m % 8 + 1], (8, nv))
        h_even = hat(x, g_even)
        h_odd = hat(x, g_odd)
        f01 = jnp.where(first4, f0, f1)
        left = jnp.concatenate(
            [h_even * f01, jnp.where(first4, h_even, h_odd) * f2, h_odd * f01], axis=0
        )
        l_lo = left - left.astype(bf16).astype(f32)
        left2 = jnp.concatenate([left, l_lo], axis=0).astype(bf16)
        hy = hat(y, g_all)
        hz = hat(z, g_all)
        plane = jnp.concatenate(
            [jnp.broadcast_to(hy[j : j + 1], (8, nv)) * hz for j in range(8)], axis=0
        )
        p_hi = plane.astype(bf16)
        p_lo = (plane - p_hi.astype(f32)).astype(bf16)
        prod = nt_dot(left2, jnp.concatenate([p_hi, p_lo], axis=0))
        hats[m] = prod[0:24] + prod[24:48]

    def place(c, m):
        both = hats[m]
        res = (both + pltpu.roll(both, 64, 1)) * stiff[c]
        main = jnp.where(lane < 64, res[0:8], res[16:24])
        mid = res[8:16]
        tail = jnp.where(lane < 64, mid, pltpu.roll(mid, 4, 0))
        t = owner[c]
        r = count[t]
        count[t] = r + 1
        for k in range(12):
            row = main[k : k + 1] if k < 8 else tail[k - 8 : k - 7]
            out[t, :, pl.ds(pl.multiple_of(r * 1536 + 128 * k, 128), 128)] = row
        old = out[t, :, 3072:3200]
        out[t, :, 3072:3200] = jnp.where(lane[0:1] == r, block[c].astype(f32), old)

    group = hats.shape[0]

    def finish(first):
        for m in range(group):
            place(first + m, m)

    for m in range(group):
        product(0, m)

    def step(n, carry):
        finish((n - 1) * group)
        for m in range(group):
            product(n * group, m)
        return carry

    lax.fori_loop(1, cells // group, step, 0)
    finish(cells - group)


def spread(owner, block, positions, stiffness, triangles, neighbours, devices):
    cells, _, verts = positions.shape
    nv = -(-verts // 256) * 256
    inputs = (owner, block, stiffness, jnp.transpose(positions, (1, 2, 0)), jnp.transpose(triangles), jnp.transpose(neighbours))
    hbm = pl.BlockSpec(memory_space=pltpu.HBM)
    vmem = pl.BlockSpec(memory_space=pltpu.VMEM)
    return pl.pallas_call(
        spread_kernel,
        out_shape=jax.ShapeDtypeStruct((devices, 1, WIDE), f32),
        in_specs=[hbm] * 6,
        out_specs=vmem,
        scratch_shapes=[
            pltpu.SMEM((cells,), i32),
            pltpu.SMEM((cells,), i32),
            pltpu.SMEM((cells,), f32),
            pltpu.VMEM((3, verts, cells), f32),
            pltpu.VMEM((3, triangles.shape[0]), i32),
            pltpu.VMEM((6, 32), i32),
            pltpu.SemaphoreType.DMA((6,)),
            pltpu.VMEM((nv, triangles.shape[0]), bf16),
            pltpu.VMEM((3, cells, nv), f32),
            pltpu.VMEM((3, cells, nv), f32),
            pltpu.VMEM((16, 24, 128), f32),
            pltpu.SMEM((devices,), i32),
        ],
        compiler_params=pltpu.CompilerParams(vmem_limit_bytes=48 << 20),
        name="spread",
    )(*[pltpu.with_memory_space_constraint(x, pltpu.HBM) for x in inputs])


def lane_take(x, index):
    return jnp.take_along_axis(x, index, axis=1)


def find(near, got, square):
    square[...] = jnp.full((128, 128), -1.0, f32)
    square[0:6, 0:32] = near[...].astype(f32)
    goal = jnp.transpose(square[...])[0:32]
    known = got[:, 3200:3328]
    k_hi = known.astype(bf16)
    k_lo = (known - k_hi.astype(f32)).astype(bf16)
    lane = lax.broadcasted_iota(i32, (32, 128), 1)
    for f1 in range(4):
        first = jnp.broadcast_to(goal[:, f1 : f1 + 1], (32, 128)).astype(i32)
        safe = jnp.maximum(first, 0)
        pick = (lax.shift_right_logical(safe, 5) == lane).astype(f32).astype(bf16)
        rows = jnp.dot(pick, k_hi, preferred_element_type=f32) + jnp.dot(pick, k_lo, preferred_element_type=f32)
        for n, q in enumerate(EDGE_Q):
            d1, d2 = [d for d in range(3) if vel[q][d]]
            if f1 == 2 * d1 + (1 if vel[q][d1] == 1 else 0):
                f2 = 2 * d2 + (1 if vel[q][d2] == 1 else 0)
                second = jnp.take_along_axis(rows, (f2 - 2) * 32 + lax.bitwise_and(safe, 31), axis=1)
                goal = jnp.where(lane == 6 + n, jnp.where(first >= 0, second, -1.0), goal)
    return goal


def collide_kernel(near, got, pops, post, table, goal, body, square):
    slots = got.shape[0]
    goal[...] = find(near, got, square)
    lane = lax.broadcasted_iota(i32, (slots, 128), 1)
    ids = got[:, 3072:3200]
    picks = []
    for r in range(2):
        col = jnp.broadcast_to(ids[:, r : r + 1], (slots, 128))
        hit = (col == lane.astype(f32)).astype(f32)
        picks.append(jnp.transpose(hit)[0:32].astype(bf16))
    for n in range(3):
        total = jnp.zeros((32, 512), f32)
        for r in range(2):
            part = got[:, r * 1536 + n * 512 : r * 1536 + (n + 1) * 512]
            hi = part.astype(bf16)
            lo = (part - hi.astype(f32)).astype(bf16)
            total = total + jnp.dot(picks[r], hi, preferred_element_type=f32)
            total = total + jnp.dot(picks[r], lo, preferred_element_type=f32)
        body[n] = total
    lanes = lax.broadcasted_iota(i32, (8, 128), 1)
    low = lanes < 64
    keep = 1.0 - 1.0 / relax_time
    gain = 1.0 - 0.5 / relax_time

    def group(g, carry):
        rows = pl.ds(pl.multiple_of(g * 8, 8), 8)
        for a in range(4):
            cut = slice(128 * a, 128 * (a + 1))
            f = [pops[q, rows, cut] * wts[q] for q in range(19)]
            force = [body[d, rows, cut] for d in range(3)]
            rho = f[0]
            for q in range(1, 19):
                rho = rho + f[q]
            u = []
            for d in range(3):
                m = 0.5 * force[d]
                for q in range(1, 19):
                    if vel[q][d] == 1:
                        m = m + f[q]
                    elif vel[q][d] == -1:
                        m = m - f[q]
                u.append(m / rho)
            speed = u[0] * u[0] + u[1] * u[1] + u[2] * u[2]
            work = u[0] * force[0] + u[1] * force[1] + u[2] * force[2]
            rho_t = rho * (1.0 / relax_time)
            flat = rho_t * (1.0 - 1.5 * speed) - (3.0 * gain) * work
            post[0, rows, cut] = keep * f[0] + wts[0] * flat
            for q in range(1, 19, 2):
                along = push = None
                for d in range(3):
                    e = vel[q][d]
                    if e:
                        along = e * u[d] if along is None else along + e * u[d]
                        push = e * force[d] if push is None else push + e * force[d]
                even = wts[q] * (flat + along * (4.5 * rho_t * along + (9.0 * gain) * push))
                odd = wts[q] * (3.0 * rho_t * along + (3.0 * gain) * push)
                post[q, rows, cut] = keep * f[q] + (even + odd)
                post[q + 1, rows, cut] = keep * f[q + 1] + (even - odd)
        for n in range(5):
            table[n, rows, :] = jnp.where(low, post[NEG[0][n], rows, 0:128], post[POS[0][n], rows, 384:512])
            m = lanes % 64
            first, second = m // 8, m % 8
            for ax in (1, 2):
                picked = None
                for a in range(4):
                    inside = (first % 2) * 64
                    if ax == 1:
                        at_low, at_high = inside + second, inside + 56 + second
                    else:
                        at_low, at_high = inside + second * 8, inside + second * 8 + 7
                    cut = slice(128 * a, 128 * (a + 1))
                    val = jnp.where(
                        low, lane_take(post[NEG[ax][n], rows, cut], at_low), lane_take(post[POS[ax][n], rows, cut], at_high)
                    )
                    picked = val if picked is None else jnp.where(first // 2 == a, val, picked)
                table[5 * ax + n, rows, :] = picked
        line = jnp.where(lanes < HAVE, pltpu.roll(goal[rows, :], IDS, 1), 1.0)
        w = lanes % 8
        for n, q in enumerate(EDGE_Q):
            ex, ey, ez = vel[q]
            at = [7 if e == 1 else 0 for e in vel[q]]
            mine = lanes // 8 == n
            if ex:
                a = 3 if ex == 1 else 0
                base = 64 if ex == 1 else 0
                where_ = base + (at[1] * 8 + w if ey else w * 8 + at[2])
                val = lane_take(post[q, rows, 128 * a : 128 * (a + 1)], where_)
                line = jnp.where(mine, val, line)
            else:
                where_ = (w % 2) * 64 + at[1] * 8 + at[2]
                for a in range(4):
                    val = lane_take(post[q, rows, 128 * a : 128 * (a + 1)], where_)
                    line = jnp.where(mine & (w // 2 == a), val, line)
        table[EDGE_TILE, rows, :] = line
        return carry

    lax.fori_loop(0, 4, group, 0)


def collide(got, populations, neighbours):
    vmem = pl.BlockSpec(memory_space=pltpu.VMEM)
    return pl.pallas_call(
        collide_kernel,
        out_shape=(
            jax.ShapeDtypeStruct((19, 32, 512), f32),
            jax.ShapeDtypeStruct((NT, 32, 128), f32),
            jax.ShapeDtypeStruct((32, 128), f32),
        ),
        in_specs=[vmem, vmem, vmem],
        out_specs=(vmem, vmem, vmem),
        scratch_shapes=[
            pltpu.VMEM((3, 32, 512), f32),
            pltpu.VMEM((128, 128), f32),
        ],
        compiler_params=pltpu.CompilerParams(vmem_limit_bytes=48 << 20),
        name="collide",
    )(jnp.transpose(neighbours), got, jnp.transpose(populations, (1, 0, 2)))


def route_kernel(sizes, left2, left, mine, right, right2, down, own, up, down2, up2, lines):
    n_gy = sizes[1]
    me_x, me_y = lax.axis_index("gx"), lax.axis_index("gy")
    for n, part in enumerate((left[EDGE_TILE], mine[EDGE_TILE], right[EDGE_TILE], left2[0], right2[0])):
        lines[32 * n : 32 * (n + 1), :] = part
    lines[160:256, :] = jnp.full((96, 128), -1.0, f32)
    ids = [jnp.transpose(lines[0:128, :]), jnp.transpose(lines[128:256, :])]
    slot = lax.broadcasted_iota(i32, (32, 128), 0).astype(f32)
    low = lax.broadcasted_iota(i32, (32, 128), 1) < 64
    named = {}
    for dy in range(-2, 3):
        owner = me_x * n_gy + lax.rem(me_y + (dy + n_gy), n_gy)
        named[dy] = slot + (owner * 32).astype(f32)

    def hot(half, row, dy):
        picked = jnp.broadcast_to(ids[half][IDS + row : IDS + row + 1, :], (32, 128)) == named[dy]
        return picked.astype(f32)

    none = jnp.zeros((32, 128), f32)
    for ax in range(3):
        planes = jnp.concatenate(
            [
                jnp.concatenate([left[t], mine[t], right[t], none], axis=0)
                for t in range(5 * ax, 5 * ax + 5)
            ],
            axis=1,
        )
        p_hi = planes.astype(bf16)
        p_lo = (planes - p_hi.astype(f32)).astype(bf16)
        picks = jnp.concatenate([hot(0, 2 * ax + s, dy) for s in range(2) for dy in (-1, 0, 1)], axis=0).astype(bf16)
        moved = jnp.dot(picks, p_hi, preferred_element_type=f32) + jnp.dot(picks, p_lo, preferred_element_type=f32)
        for k, goal in enumerate((down, own, up)):
            for n in range(5):
                cut = slice(128 * n, 128 * (n + 1))
                goal[5 * ax + n] = jnp.where(
                    low, moved[32 * k : 32 * (k + 1), cut], moved[96 + 32 * k : 96 + 32 * (k + 1), cut]
                )
    e_hi = lines[...].astype(bf16)
    e_lo = (lines[...] - e_hi.astype(f32)).astype(bf16)
    both = jnp.concatenate([e_hi, e_lo], axis=1)
    lane = lax.broadcasted_iota(i32, (160, 128), 1)
    total = jnp.zeros((160, 128), f32)
    for n in range(12):
        picks = jnp.concatenate(
            [jnp.concatenate([hot(h, 6 + n, dy) for dy in range(-2, 3)], axis=0) for h in range(2)], axis=1
        ).astype(bf16)
        moved = jnp.dot(picks, both, preferred_element_type=f32)
        wanted = (lane // 8 == n) | (lane == HAVE + n)
        total = jnp.where(wanted, moved[:, 0:128] + moved[:, 128:256], total)
    for k, goal in enumerate((down2, down, own, up, up2)):
        goal[goal.shape[0] - 1] = total[32 * k : 32 * (k + 1)]


def route(left2, left, mine, right, right2):
    vmem = pl.BlockSpec(memory_space=pltpu.VMEM)
    sizes = (lax.axis_size("gx"), lax.axis_size("gy"))
    big = jax.ShapeDtypeStruct(mine.shape, f32)
    small = jax.ShapeDtypeStruct(left2.shape, f32)
    return pl.pallas_call(
        functools.partial(route_kernel, sizes),
        out_shape=(big, big, big, small, small),
        in_specs=[vmem] * 5,
        out_specs=(vmem,) * 5,
        scratch_shapes=[pltpu.VMEM((256, 128), f32)],
        compiler_params=pltpu.CompilerParams(vmem_limit_bytes=48 << 20),
        name="route",
    )(left2, left, mine, right, right2)


def stream_kernel(goal, post, own, below, above, below2, above2, out):
    lanes = lax.broadcasted_iota(i32, (8, 128), 1)
    jj = (lanes // 8) % 8
    kk = lanes % 8

    def group(g, carry):
        rows = pl.ds(pl.multiple_of(g * 8, 8), 8)
        near = goal[rows, :]
        ghost = []
        for ax in range(3):
            have = lane_take(near, jnp.where(lanes < 64, 2 * ax + 1, 2 * ax)) >= 0.0
            for t in range(5 * ax, 5 * ax + 5):
                came = own[t, rows, :] + below[t, rows, :] + above[t, rows, :]
                ghost.append(jnp.where(have, came, jnp.nan))
        came = own[EDGE_TILE, rows, :] + below[EDGE_TILE, rows, :] + above[EDGE_TILE, rows, :]
        came = came + below2[0, rows, :] + above2[0, rows, :]
        have = lane_take(came, jnp.minimum(HAVE + lanes // 8, 127)) > 0.5
        edges = jnp.where(have, came, jnp.nan)
        out[0, rows, :] = post[0, rows, :]
        for q in range(1, 19):
            e = vel[q]
            ex, ey, ez = e
            shift = ex * 64 + ey * 8 + ez
            tiles = [post[q, rows, 128 * a : 128 * (a + 1)] for a in range(4)]
            rolled = [pltpu.roll(t, shift % 128, 1) for t in tiles]
            for a in range(4):
                if shift > 0:
                    val = jnp.where(lanes < shift, rolled[(a - 1) % 4], rolled[a])
                else:
                    val = jnp.where(lanes >= 128 + shift, rolled[(a + 1) % 4], rolled[a])
                ii = 2 * a + lanes // 64
                back = post[opposite[q], rows, 128 * a : 128 * (a + 1)]
                coords = (ii, jj, kk)
                crossing = [None if e[d] == 0 else coords[d] == (0 if e[d] == 1 else 7) for d in range(3)]
                if ex == 1 and a != 0 or ex == -1 and a != 3:
                    crossing[0] = None
                axes = [d for d in range(3) if crossing[d] is not None]
                if axes:
                    out_of = crossing[axes[0]]
                    for d in axes[1:]:
                        out_of = out_of | crossing[d]
                    val = jnp.where(out_of, back, val)
                for d in axes:
                    n = (POS[d] if e[d] == 1 else NEG[d]).index(q)
                    source = ghost[5 * d + n]
                    base = 64 if e[d] == 1 else 0
                    if d == 0:
                        brought = pltpu.roll(source, (64 + ey * 8 + ez) % 128, 1)
                    elif d == 1:
                        brought = lane_take(source, base + ((ii - ex) * 8 + kk - ez) % 64)
                    else:
                        brought = lane_take(source, base + ((ii - ex) * 8 + jj - ey) % 64)
                    use = crossing[d] & (brought == brought)
                    for other in axes:
                        if other != d:
                            use = use & ~crossing[other]
                    val = jnp.where(use, brought, val)
                if len(axes) == 2:
                    n = q - 7
                    along = kk if ez == 0 else (jj if ey == 0 else ii)
                    brought = lane_take(edges, 8 * n + along)
                    val = jnp.where(crossing[axes[0]] & crossing[axes[1]] & (brought == brought), brought, val)
                out[q, rows, 128 * a : 128 * (a + 1)] = val
        return carry

    lax.fori_loop(0, 4, group, 0)


def stream(goal, post, *parts):
    vmem = pl.BlockSpec(memory_space=pltpu.VMEM)
    return pl.pallas_call(
        stream_kernel,
        out_shape=jax.ShapeDtypeStruct((19, 32, 512), f32),
        in_specs=[vmem] * 7,
        out_specs=vmem,
        compiler_params=pltpu.CompilerParams(vmem_limit_bytes=48 << 20),
        name="stream",
    )(goal, post, *parts)


def send(array, axis, step):
    size = lax.axis_size(axis)
    return lax.ppermute(array, axis, [(i, (i + step) % size) for i in range(size)])


def exchange(table):
    edge = table[EDGE_TILE : EDGE_TILE + 1]
    left, right = send(table, "gx", 1), send(table, "gx", -1)
    left2, right2 = send(edge, "gx", 2), send(edge, "gx", -2)
    down, own, up, down2, up2 = route(left2, left, table, right, right2)
    return own, send(up, "gy", 1), send(down, "gy", -1), send(up2, "gy", 2), send(down2, "gy", -2)


def body(populations, neighbours, positions, stiffness, cell_owner, cell_block, triangles):
    devices = lax.axis_size("gx") * lax.axis_size("gy")
    slots = spread(cell_owner[:, 0], cell_block, positions, stiffness, triangles, neighbours, devices)
    got = lax.all_to_all(slots, BOTH, split_axis=0, concat_axis=0, tiled=True)
    post, table, goal = collide(got.reshape(devices, WIDE), populations, neighbours)
    result = stream(goal, post, *exchange(table))
    return jnp.transpose(result, (1, 0, 2))


def solution(mesh):
    placed = (
        P(BOTH, None, None),
        P(BOTH, None),
        P(BOTH, None, None),
        P(BOTH),
        P(BOTH, None),
        P(BOTH),
        P(),
    )
    return jax.shard_map(
        body, mesh=mesh, in_specs=placed, out_specs=P(BOTH, None, None), check_vma=False
    )
```

```python
import functools

import jax
import jax.numpy as jnp
import numpy as np
from jax import lax
from jax.experimental import pallas as pl
from jax.experimental.pallas import tpu as pltpu
from jax.sharding import PartitionSpec as P

vel = [
    (0, 0, 0), (1, 0, 0), (-1, 0, 0), (0, 1, 0), (0, -1, 0), (0, 0, 1), (0, 0, -1),
    (1, 1, 0), (-1, -1, 0), (1, -1, 0), (-1, 1, 0),
    (1, 0, 1), (-1, 0, -1), (1, 0, -1), (-1, 0, 1),
    (0, 1, 1), (0, -1, -1), (0, 1, -1), (0, -1, 1),
]
wts = [1.0 / 3.0] + [1.0 / 18.0] * 6 + [1.0 / 36.0] * 12
opposite = [0, 2, 1, 4, 3, 6, 5, 8, 7, 10, 9, 12, 11, 14, 13, 16, 15, 18, 17]
relax_time = 0.6
NEG, POS = {}, {}
for ax in range(3):
    NEG[ax] = [q for q in range(19) if vel[q][ax] == -1]
    POS[ax] = [q for q in range(19) if vel[q][ax] == 1]
EDGE_Q = list(range(7, 19))
FACE_TILES = 15
EDGE_TILE = 15
NT = 16
IDS = 96
HAVE = 114
WIDE = 3328
BOTH = ("gx", "gy")
f32, bf16, i32 = jnp.float32, jnp.bfloat16, jnp.int32


def nt_dot(a, b):
    return lax.dot_general(a, b, (((1,), (1,)), ((), ())), preferred_element_type=f32)


def hat(x, grid):
    return jnp.maximum(0.0, 1.0 - jnp.abs(x - grid))


def spread_kernel(owner_in, block_in, stiff_in, raw_in, tri_in, near_in, out, owner, block, stiff, raw, tri, near, sem, st, pos, force, hats, count):
    cells, nv = pos.shape[1:]
    verts = raw.shape[1]
    pairs = ((tri_in, tri), (raw_in, raw), (near_in, near), (owner_in, owner), (block_in, block), (stiff_in, stiff))
    copies = [pltpu.make_async_copy(a, b, sem.at[n]) for n, (a, b) in enumerate(pairs)]
    for c in copies:
        c.start()
    copies[0].wait()
    for r in range(0, nv, 128):
        ids = lax.broadcasted_iota(i32, (128, tri.shape[1]), 0) + r
        hit = (ids == tri[0:1, :]) | (ids == tri[1:2, :]) | (ids == tri[2:3, :])
        st[r : r + 128, :] = hit.astype(f32).astype(jnp.float8_e4m3fn)
    links = nt_dot(st[...], st[...])
    for c in copies[1:]:
        c.wait()
    for r in range(0, nv, 128):
        for d in range(3):
            have = min(verts - r, 128)
            piece = raw[d, r : r + have, :]
            if have < 128:
                piece = jnp.concatenate([piece, jnp.full((128 - have, cells), -100.0, f32)], axis=0)
            pos[d, :, r : r + 128] = jnp.transpose(piece)
    rows = lax.broadcasted_iota(i32, (nv, nv), 0)
    cols = lax.broadcasted_iota(i32, (nv, nv), 1)
    springs = jnp.where(rows == cols, -2.0 * links, links)
    s_hi = springs.astype(bf16)
    s_lo = (springs - s_hi.astype(f32)).astype(bf16)
    x = jnp.concatenate([pos[0], pos[1], pos[2]], axis=0)
    x_hi = x.astype(bf16)
    x_lo = (x - x_hi.astype(f32)).astype(bf16)
    most = jnp.dot(jnp.concatenate([x_hi, x_lo], axis=0), s_hi, preferred_element_type=f32)
    for d in range(3):
        lo, hi = d * cells, (d + 1) * cells
        force[d] = most[lo:hi] + most[3 * cells + lo : 3 * cells + hi]

    @pl.when(jnp.max(jnp.abs(springs)) > 256.0)
    def _():
        rest = jnp.dot(x_hi, s_lo, preferred_element_type=f32)
        for d in range(3):
            force[d] = force[d] + rest[d * cells : (d + 1) * cells]

    sub = lax.broadcasted_iota(i32, (8, 128), 0)
    lane = lax.broadcasted_iota(i32, (8, 128), 1)
    slots = out.shape[0]
    tail_row = jnp.full((8, 128), -1.0, f32)
    table_row = jnp.zeros((8, 128), f32)
    for f in range(4):
        one_face = jnp.concatenate([near[f + 2 : f + 3, :].astype(f32), jnp.zeros((1, 96), f32)], axis=1)
        one_face = jnp.broadcast_to(one_face, (8, 128))
        table_row = jnp.where(lane // 32 == f, pltpu.roll(one_face, 32 * f, 1) if f else one_face, table_row)

    def clear(t, carry):
        for m in range(8):
            out[t * 8 + m, :, 0:3072] = jnp.zeros((1, 3072), f32)
            out[t * 8 + m, :, 3072:3200] = tail_row[0:1]
            out[t * 8 + m, :, 3200:3328] = table_row[0:1]
            count[t * 8 + m] = 0
        return carry

    lax.fori_loop(0, slots // 8, clear, 0)
    sub8 = lax.broadcasted_iota(i32, (8, nv), 0)
    g_even = (2 * (sub8 % 4)).astype(f32)
    g_odd = g_even + 1.0
    g_all = sub8.astype(f32)
    first4 = sub8 < 4

    def product(first, m):
        c = first + m
        near8 = pl.ds(pl.multiple_of(first + m // 8 * 8, 8), 8)
        x = jnp.broadcast_to(pos[0, near8, :][m % 8 : m % 8 + 1], (8, nv))
        y = jnp.broadcast_to(pos[1, near8, :][m % 8 : m % 8 + 1], (8, nv))
        z = jnp.broadcast_to(pos[2, near8, :][m % 8 : m % 8 + 1], (8, nv))
        f0 = jnp.broadcast_to(force[0, near8, :][m % 8 : m % 8 + 1], (8, nv))
        f1 = jnp.broadcast_to(force[1, near8, :][m % 8 : m % 8 + 1], (8, nv))
        f2 = jnp.broadcast_to(force[2, near8, :][m % 8 : m % 8 + 1], (8, nv))
        h_even = hat(x, g_even)
        h_odd = hat(x, g_odd)
        f01 = jnp.where(first4, f0, f1)
        left = jnp.concatenate(
            [h_even * f01, jnp.where(first4, h_even, h_odd) * f2, h_odd * f01], axis=0
        )
        l_lo = left - left.astype(bf16).astype(f32)
        left2 = jnp.concatenate([left, l_lo], axis=0).astype(bf16)
        hy = hat(y, g_all)
        hz = hat(z, g_all)
        plane = jnp.concatenate(
            [jnp.broadcast_to(hy[j : j + 1], (8, nv)) * hz for j in range(8)], axis=0
        )
        p_hi = plane.astype(bf16)
        p_lo = (plane - p_hi.astype(f32)).astype(bf16)
        prod = nt_dot(left2, jnp.concatenate([p_hi, p_lo], axis=0))
        hats[m] = prod[0:24] + prod[24:48]

    def place(c, m):
        both = hats[m]
        res = (both + pltpu.roll(both, 64, 1)) * stiff[c]
        main = jnp.where(lane < 64, res[0:8], res[16:24])
        mid = res[8:16]
        tail = jnp.where(lane < 64, mid, pltpu.roll(mid, 4, 0))
        t = owner[c]
        r = count[t]
        count[t] = r + 1
        for k in range(12):
            row = main[k : k + 1] if k < 8 else tail[k - 8 : k - 7]
            out[t, :, pl.ds(pl.multiple_of(r * 1536 + 128 * k, 128), 128)] = row
        old = out[t, :, 3072:3200]
        out[t, :, 3072:3200] = jnp.where(lane[0:1] == r, block[c].astype(f32), old)

    group = hats.shape[0]

    def finish(first):
        for m in range(group):
            place(first + m, m)

    for m in range(group):
        product(0, m)

    def step(n, carry):
        finish((n - 1) * group)
        for m in range(group):
            product(n * group, m)
        return carry

    lax.fori_loop(1, cells // group, step, 0)
    finish(cells - group)


def spread(owner, block, positions, stiffness, triangles, neighbours, devices):
    cells, _, verts = positions.shape
    nv = -(-verts // 256) * 256
    inputs = (owner, block, stiffness, jnp.transpose(positions, (1, 2, 0)), jnp.transpose(triangles), jnp.transpose(neighbours))
    hbm = pl.BlockSpec(memory_space=pltpu.HBM)
    vmem = pl.BlockSpec(memory_space=pltpu.VMEM)
    return pl.pallas_call(
        spread_kernel,
        out_shape=jax.ShapeDtypeStruct((devices, 1, WIDE), f32),
        in_specs=[hbm] * 6,
        out_specs=vmem,
        scratch_shapes=[
            pltpu.SMEM((cells,), i32),
            pltpu.SMEM((cells,), i32),
            pltpu.SMEM((cells,), f32),
            pltpu.VMEM((3, verts, cells), f32),
            pltpu.VMEM((3, triangles.shape[0]), i32),
            pltpu.VMEM((6, 32), i32),
            pltpu.SemaphoreType.DMA((6,)),
            pltpu.VMEM((nv, triangles.shape[0]), jnp.float8_e4m3fn),
            pltpu.VMEM((3, cells, nv), f32),
            pltpu.VMEM((3, cells, nv), f32),
            pltpu.VMEM((16, 24, 128), f32),
            pltpu.SMEM((devices,), i32),
        ],
        compiler_params=pltpu.CompilerParams(vmem_limit_bytes=48 << 20),
        name="spread",
    )(*[pltpu.with_memory_space_constraint(x, pltpu.HBM) for x in inputs])


def lane_take(x, index):
    return jnp.take_along_axis(x, index, axis=1)


def column(got, tile):
    tiles = WIDE // 128
    return got[pl.ds(tile, got.shape[0] // tiles, stride=tiles), :]


def find(near, got, square):
    square[...] = jnp.full((128, 128), -1.0, f32)
    square[0:6, 0:32] = near[...].astype(f32)
    goal = jnp.transpose(square[...])[0:32]
    known = column(got, 25)
    k_hi = known.astype(bf16)
    k_lo = (known - k_hi.astype(f32)).astype(bf16)
    lane = lax.broadcasted_iota(i32, (32, 128), 1)
    for f1 in range(4):
        first = jnp.broadcast_to(goal[:, f1 : f1 + 1], (32, 128)).astype(i32)
        safe = jnp.maximum(first, 0)
        pick = (lax.shift_right_logical(safe, 5) == lane).astype(f32).astype(bf16)
        rows = jnp.dot(pick, k_hi, preferred_element_type=f32) + jnp.dot(pick, k_lo, preferred_element_type=f32)
        for n, q in enumerate(EDGE_Q):
            d1, d2 = [d for d in range(3) if vel[q][d]]
            if f1 == 2 * d1 + (1 if vel[q][d1] == 1 else 0):
                f2 = 2 * d2 + (1 if vel[q][d2] == 1 else 0)
                second = jnp.take_along_axis(rows, (f2 - 2) * 32 + lax.bitwise_and(safe, 31), axis=1)
                goal = jnp.where(lane == 6 + n, jnp.where(first >= 0, second, -1.0), goal)
    return goal


def collide_kernel(near, got, pops, post, table, goal, body, square):
    slots = got.shape[0] * 128 // WIDE
    goal[...] = find(near, got, square)
    lane = lax.broadcasted_iota(i32, (slots, 128), 1)
    ids = column(got, 24)
    picks = []
    for r in range(2):
        col = jnp.broadcast_to(ids[:, r : r + 1], (slots, 128))
        hit = (col == lane.astype(f32)).astype(f32)
        picks.append(jnp.transpose(hit)[0:32].astype(bf16))
    for n in range(3):
        total = jnp.zeros((32, 512), f32)
        for r in range(2):
            part = jnp.concatenate([column(got, 12 * r + 4 * n + a) for a in range(4)], axis=1)
            hi = part.astype(bf16)
            lo = (part - hi.astype(f32)).astype(bf16)
            total = total + jnp.dot(picks[r], hi, preferred_element_type=f32)
            total = total + jnp.dot(picks[r], lo, preferred_element_type=f32)
        body[n] = total
    lanes = lax.broadcasted_iota(i32, (8, 128), 1)
    low = lanes < 64
    keep = 1.0 - 1.0 / relax_time
    gain = 1.0 - 0.5 / relax_time

    def group(g, carry):
        rows = pl.ds(pl.multiple_of(g * 8, 8), 8)
        for a in range(4):
            cut = slice(128 * a, 128 * (a + 1))
            f = [pops[q, rows, cut] * wts[q] for q in range(19)]
            force = [body[d, rows, cut] for d in range(3)]
            rho = f[0]
            for q in range(1, 19):
                rho = rho + f[q]
            u = []
            for d in range(3):
                m = 0.5 * force[d]
                for q in range(1, 19):
                    if vel[q][d] == 1:
                        m = m + f[q]
                    elif vel[q][d] == -1:
                        m = m - f[q]
                u.append(m / rho)
            speed = u[0] * u[0] + u[1] * u[1] + u[2] * u[2]
            work = u[0] * force[0] + u[1] * force[1] + u[2] * force[2]
            rho_t = rho * (1.0 / relax_time)
            flat = rho_t * (1.0 - 1.5 * speed) - (3.0 * gain) * work
            post[0, rows, cut] = keep * f[0] + wts[0] * flat
            for q in range(1, 19, 2):
                along = push = None
                for d in range(3):
                    e = vel[q][d]
                    if e:
                        along = e * u[d] if along is None else along + e * u[d]
                        push = e * force[d] if push is None else push + e * force[d]
                even = wts[q] * (flat + along * (4.5 * rho_t * along + (9.0 * gain) * push))
                odd = wts[q] * (3.0 * rho_t * along + (3.0 * gain) * push)
                post[q, rows, cut] = keep * f[q] + (even + odd)
                post[q + 1, rows, cut] = keep * f[q + 1] + (even - odd)
        for n in range(5):
            table[n, rows, :] = jnp.where(low, post[NEG[0][n], rows, 0:128], post[POS[0][n], rows, 384:512])
            m = lanes % 64
            first, second = m // 8, m % 8
            for ax in (1, 2):
                picked = None
                for a in range(4):
                    inside = (first % 2) * 64
                    if ax == 1:
                        at_low, at_high = inside + second, inside + 56 + second
                    else:
                        at_low, at_high = inside + second * 8, inside + second * 8 + 7
                    cut = slice(128 * a, 128 * (a + 1))
                    val = jnp.where(
                        low, lane_take(post[NEG[ax][n], rows, cut], at_low), lane_take(post[POS[ax][n], rows, cut], at_high)
                    )
                    picked = val if picked is None else jnp.where(first // 2 == a, val, picked)
                table[5 * ax + n, rows, :] = picked
        line = jnp.where(lanes < HAVE, pltpu.roll(goal[rows, :], IDS, 1), 1.0)
        w = lanes % 8
        for n, q in enumerate(EDGE_Q):
            ex, ey, ez = vel[q]
            at = [7 if e == 1 else 0 for e in vel[q]]
            mine = lanes // 8 == n
            if ex:
                a = 3 if ex == 1 else 0
                base = 64 if ex == 1 else 0
                where_ = base + (at[1] * 8 + w if ey else w * 8 + at[2])
                val = lane_take(post[q, rows, 128 * a : 128 * (a + 1)], where_)
                line = jnp.where(mine, val, line)
            else:
                where_ = (w % 2) * 64 + at[1] * 8 + at[2]
                for a in range(4):
                    val = lane_take(post[q, rows, 128 * a : 128 * (a + 1)], where_)
                    line = jnp.where(mine & (w // 2 == a), val, line)
        table[EDGE_TILE, rows, :] = line
        return carry

    lax.fori_loop(0, 4, group, 0, unroll=True)


def collide(got, populations, neighbours):
    vmem = pl.BlockSpec(memory_space=pltpu.VMEM)
    return pl.pallas_call(
        collide_kernel,
        out_shape=(
            jax.ShapeDtypeStruct((19, 32, 512), f32),
            jax.ShapeDtypeStruct((NT, 32, 128), f32),
            jax.ShapeDtypeStruct((32, 128), f32),
        ),
        in_specs=[vmem, vmem, vmem],
        out_specs=(vmem, vmem, vmem),
        scratch_shapes=[
            pltpu.VMEM((3, 32, 512), f32),
            pltpu.VMEM((128, 128), f32),
        ],
        compiler_params=pltpu.CompilerParams(vmem_limit_bytes=48 << 20),
        name="collide",
    )(jnp.transpose(neighbours), got, jnp.transpose(populations, (1, 0, 2)))


def route_kernel(sizes, left2, left, mine, right, right2, down, own, up, down2, up2, lines):
    n_gy = sizes[1]
    me_x, me_y = lax.axis_index("gx"), lax.axis_index("gy")
    for n, part in enumerate((left[EDGE_TILE], mine[EDGE_TILE], right[EDGE_TILE], left2[0], right2[0])):
        lines[32 * n : 32 * (n + 1), :] = part
    lines[160:256, :] = jnp.full((96, 128), -1.0, f32)
    ids = [jnp.transpose(lines[0:128, :]), jnp.transpose(lines[128:256, :])]
    slot = lax.broadcasted_iota(i32, (32, 128), 0).astype(f32)
    low = lax.broadcasted_iota(i32, (32, 128), 1) < 64
    named = {}
    for dy in range(-2, 3):
        owner = me_x * n_gy + lax.rem(me_y + (dy + n_gy), n_gy)
        named[dy] = slot + (owner * 32).astype(f32)

    def hot(half, row, dy):
        picked = jnp.broadcast_to(ids[half][IDS + row : IDS + row + 1, :], (32, 128)) == named[dy]
        return picked.astype(f32)

    none = jnp.zeros((32, 128), f32)
    for ax in range(3):
        planes = jnp.concatenate(
            [
                jnp.concatenate([left[t], mine[t], right[t], none], axis=0)
                for t in range(5 * ax, 5 * ax + 5)
            ],
            axis=1,
        )
        p_hi = planes.astype(bf16)
        p_lo = (planes - p_hi.astype(f32)).astype(bf16)
        picks = jnp.concatenate([hot(0, 2 * ax + s, dy) for s in range(2) for dy in (-1, 0, 1)], axis=0).astype(bf16)
        moved = jnp.dot(picks, p_hi, preferred_element_type=f32) + jnp.dot(picks, p_lo, preferred_element_type=f32)
        for k, goal in enumerate((down, own, up)):
            for n in range(5):
                cut = slice(128 * n, 128 * (n + 1))
                goal[5 * ax + n] = jnp.where(
                    low, moved[32 * k : 32 * (k + 1), cut], moved[96 + 32 * k : 96 + 32 * (k + 1), cut]
                )
    e_hi = lines[...].astype(bf16)
    e_lo = (lines[...] - e_hi.astype(f32)).astype(bf16)
    both = jnp.concatenate([e_hi, e_lo], axis=1)
    lane = lax.broadcasted_iota(i32, (160, 128), 1)
    total = jnp.zeros((160, 128), f32)
    for n in range(12):
        picks = jnp.concatenate(
            [jnp.concatenate([hot(h, 6 + n, dy) for dy in range(-2, 3)], axis=0) for h in range(2)], axis=1
        ).astype(bf16)
        moved = jnp.dot(picks, both, preferred_element_type=f32)
        wanted = (lane // 8 == n) | (lane == HAVE + n)
        total = jnp.where(wanted, moved[:, 0:128] + moved[:, 128:256], total)
    for k, goal in enumerate((down2, down, own, up, up2)):
        goal[goal.shape[0] - 1] = total[32 * k : 32 * (k + 1)]


def route(left2, left, mine, right, right2):
    vmem = pl.BlockSpec(memory_space=pltpu.VMEM)
    sizes = (lax.axis_size("gx"), lax.axis_size("gy"))
    big = jax.ShapeDtypeStruct(mine.shape, f32)
    small = jax.ShapeDtypeStruct(left2.shape, f32)
    return pl.pallas_call(
        functools.partial(route_kernel, sizes),
        out_shape=(big, big, big, small, small),
        in_specs=[vmem] * 5,
        out_specs=(vmem,) * 5,
        scratch_shapes=[pltpu.VMEM((256, 128), f32)],
        compiler_params=pltpu.CompilerParams(vmem_limit_bytes=48 << 20),
        name="route",
    )(left2, left, mine, right, right2)


def stream_kernel(goal, post, own, below, above, below2, above2, out):
    lanes = lax.broadcasted_iota(i32, (8, 128), 1)
    jj = (lanes // 8) % 8
    kk = lanes % 8

    def group(g, carry):
        rows = pl.ds(pl.multiple_of(g * 8, 8), 8)
        near = goal[rows, :]
        ghost = []
        for ax in range(3):
            have = lane_take(near, jnp.where(lanes < 64, 2 * ax + 1, 2 * ax)) >= 0.0
            for t in range(5 * ax, 5 * ax + 5):
                came = own[t, rows, :] + below[t, rows, :] + above[t, rows, :]
                ghost.append(jnp.where(have, came, jnp.nan))
        came = own[EDGE_TILE, rows, :] + below[EDGE_TILE, rows, :] + above[EDGE_TILE, rows, :]
        came = came + below2[0, rows, :] + above2[0, rows, :]
        have = lane_take(came, jnp.minimum(HAVE + lanes // 8, 127)) > 0.5
        edges = jnp.where(have, came, jnp.nan)
        out[0, rows, :] = post[0, rows, :]
        for q in range(1, 19):
            e = vel[q]
            ex, ey, ez = e
            shift = ex * 64 + ey * 8 + ez
            tiles = [post[q, rows, 128 * a : 128 * (a + 1)] for a in range(4)]
            rolled = [pltpu.roll(t, shift % 128, 1) for t in tiles]
            for a in range(4):
                if shift > 0:
                    val = jnp.where(lanes < shift, rolled[(a - 1) % 4], rolled[a])
                else:
                    val = jnp.where(lanes >= 128 + shift, rolled[(a + 1) % 4], rolled[a])
                ii = 2 * a + lanes // 64
                back = post[opposite[q], rows, 128 * a : 128 * (a + 1)]
                coords = (ii, jj, kk)
                crossing = [None if e[d] == 0 else coords[d] == (0 if e[d] == 1 else 7) for d in range(3)]
                if ex == 1 and a != 0 or ex == -1 and a != 3:
                    crossing[0] = None
                axes = [d for d in range(3) if crossing[d] is not None]
                if axes:
                    out_of = crossing[axes[0]]
                    for d in axes[1:]:
                        out_of = out_of | crossing[d]
                    val = jnp.where(out_of, back, val)
                for d in axes:
                    n = (POS[d] if e[d] == 1 else NEG[d]).index(q)
                    source = ghost[5 * d + n]
                    base = 64 if e[d] == 1 else 0
                    if d == 0:
                        brought = pltpu.roll(source, (64 + ey * 8 + ez) % 128, 1)
                    elif d == 1:
                        brought = lane_take(source, base + ((ii - ex) * 8 + kk - ez) % 64)
                    else:
                        brought = lane_take(source, base + ((ii - ex) * 8 + jj - ey) % 64)
                    use = crossing[d] & (brought == brought)
                    for other in axes:
                        if other != d:
                            use = use & ~crossing[other]
                    val = jnp.where(use, brought, val)
                if len(axes) == 2:
                    n = q - 7
                    along = kk if ez == 0 else (jj if ey == 0 else ii)
                    brought = lane_take(edges, 8 * n + along)
                    val = jnp.where(crossing[axes[0]] & crossing[axes[1]] & (brought == brought), brought, val)
                out[q, rows, 128 * a : 128 * (a + 1)] = val
        return carry

    lax.fori_loop(0, 4, group, 0)


def stream(goal, post, *parts):
    vmem = pl.BlockSpec(memory_space=pltpu.VMEM)
    return pl.pallas_call(
        stream_kernel,
        out_shape=jax.ShapeDtypeStruct((19, 32, 512), f32),
        in_specs=[vmem] * 7,
        out_specs=vmem,
        compiler_params=pltpu.CompilerParams(vmem_limit_bytes=48 << 20),
        name="stream",
    )(goal, post, *parts)


def send(array, axis, step):
    size = lax.axis_size(axis)
    return lax.ppermute(array, axis, [(i, (i + step) % size) for i in range(size)])


def exchange(table):
    edge = table[EDGE_TILE : EDGE_TILE + 1]
    left, right = send(table, "gx", 1), send(table, "gx", -1)
    left2, right2 = send(edge, "gx", 2), send(edge, "gx", -2)
    down, own, up, down2, up2 = route(left2, left, table, right, right2)
    return own, send(up, "gy", 1), send(down, "gy", -1), send(up2, "gy", 2), send(down2, "gy", -2)


def body(populations, neighbours, positions, stiffness, cell_owner, cell_block, triangles):
    devices = lax.axis_size("gx") * lax.axis_size("gy")
    slots = spread(cell_owner[:, 0], cell_block, positions, stiffness, triangles, neighbours, devices)
    got = lax.all_to_all(slots, BOTH, split_axis=0, concat_axis=0, tiled=True)
    post, table, goal = collide(got.reshape(-1, 128), populations, neighbours)
    result = stream(goal, post, *exchange(table))
    return jnp.transpose(result, (1, 0, 2))


def solution(mesh):
    placed = (
        P(BOTH, None, None),
        P(BOTH, None),
        P(BOTH, None, None),
        P(BOTH),
        P(BOTH, None),
        P(BOTH),
        P(),
    )
    return jax.shard_map(
        body, mesh=mesh, in_specs=placed, out_specs=P(BOTH, None, None), check_vma=False
    )
```

```python
import functools

import jax
import jax.numpy as jnp
import numpy as np
from jax import lax
from jax.experimental import pallas as pl
from jax.experimental.pallas import tpu as pltpu
from jax.sharding import PartitionSpec as P

vel = [
    (0, 0, 0), (1, 0, 0), (-1, 0, 0), (0, 1, 0), (0, -1, 0), (0, 0, 1), (0, 0, -1),
    (1, 1, 0), (-1, -1, 0), (1, -1, 0), (-1, 1, 0),
    (1, 0, 1), (-1, 0, -1), (1, 0, -1), (-1, 0, 1),
    (0, 1, 1), (0, -1, -1), (0, 1, -1), (0, -1, 1),
]
wts = [1.0 / 3.0] + [1.0 / 18.0] * 6 + [1.0 / 36.0] * 12
opposite = [0, 2, 1, 4, 3, 6, 5, 8, 7, 10, 9, 12, 11, 14, 13, 16, 15, 18, 17]
relax_time = 0.6
NEG, POS = {}, {}
for ax in range(3):
    NEG[ax] = [q for q in range(19) if vel[q][ax] == -1]
    POS[ax] = [q for q in range(19) if vel[q][ax] == 1]
EDGE_Q = list(range(7, 19))
FACE_TILES = 15
EDGE_TILE = 15
NT = 16
IDS = 96
HAVE = 114
WIDE = 3328
BOTH = ("gx", "gy")
f32, bf16, i32 = jnp.float32, jnp.bfloat16, jnp.int32


def nt_dot(a, b):
    return lax.dot_general(a, b, (((1,), (1,)), ((), ())), preferred_element_type=f32)


def hat(x, grid):
    return jnp.maximum(0.0, 1.0 - jnp.abs(x - grid))


def spread_kernel(owner_in, block_in, stiff_in, raw_in, tri_in, near_in, out, owner, block, stiff, raw, tri, near, sem, st, pos, force, hats, count):
    cells, nv = pos.shape[1:]
    verts = raw.shape[1]
    pairs = ((tri_in, tri), (raw_in, raw), (near_in, near), (owner_in, owner), (block_in, block), (stiff_in, stiff))
    copies = [pltpu.make_async_copy(a, b, sem.at[n]) for n, (a, b) in enumerate(pairs)]
    for c in copies:
        c.start()
    copies[0].wait()
    for r in range(0, nv, 128):
        ids = lax.broadcasted_iota(i32, (128, tri.shape[1]), 0) + r
        hit = (ids == tri[0:1, :]) | (ids == tri[1:2, :]) | (ids == tri[2:3, :])
        st[r : r + 128, :] = hit.astype(f32).astype(jnp.float8_e4m3fn)
    links = nt_dot(st[...], st[...])
    for c in copies[1:]:
        c.wait()
    for r in range(0, nv, 128):
        for d in range(3):
            have = min(verts - r, 128)
            piece = raw[d, r : r + have, :]
            if have < 128:
                piece = jnp.concatenate([piece, jnp.full((128 - have, cells), -100.0, f32)], axis=0)
            pos[d, :, r : r + 128] = jnp.transpose(piece)
    rows = lax.broadcasted_iota(i32, (nv, nv), 0)
    cols = lax.broadcasted_iota(i32, (nv, nv), 1)
    springs = jnp.where(rows == cols, -2.0 * links, links)
    s_hi = springs.astype(bf16)
    s_lo = (springs - s_hi.astype(f32)).astype(bf16)
    x = jnp.concatenate([pos[0], pos[1], pos[2]], axis=0)
    x_hi = x.astype(bf16)
    x_lo = (x - x_hi.astype(f32)).astype(bf16)
    most = jnp.dot(jnp.concatenate([x_hi, x_lo], axis=0), s_hi, preferred_element_type=f32)
    for d in range(3):
        lo, hi = d * cells, (d + 1) * cells
        force[d] = most[lo:hi] + most[3 * cells + lo : 3 * cells + hi]

    @pl.when(jnp.max(jnp.abs(springs)) > 256.0)
    def _():
        rest = jnp.dot(x_hi, s_lo, preferred_element_type=f32)
        for d in range(3):
            force[d] = force[d] + rest[d * cells : (d + 1) * cells]

    sub = lax.broadcasted_iota(i32, (8, 128), 0)
    lane = lax.broadcasted_iota(i32, (8, 128), 1)
    slots = out.shape[0]
    tail_row = jnp.full((8, 128), -1.0, f32)
    table_row = jnp.zeros((8, 128), f32)
    for f in range(4):
        one_face = jnp.concatenate([near[f + 2 : f + 3, :].astype(f32), jnp.zeros((1, 96), f32)], axis=1)
        one_face = jnp.broadcast_to(one_face, (8, 128))
        table_row = jnp.where(lane // 32 == f, pltpu.roll(one_face, 32 * f, 1) if f else one_face, table_row)

    def clear(t, carry):
        for m in range(8):
            out[t * 8 + m, :, 0:3072] = jnp.zeros((1, 3072), f32)
            out[t * 8 + m, :, 3072:3200] = tail_row[0:1]
            out[t * 8 + m, :, 3200:3328] = table_row[0:1]
            count[t * 8 + m] = 0
        return carry

    lax.fori_loop(0, slots // 8, clear, 0)
    sub8 = lax.broadcasted_iota(i32, (8, nv), 0)
    g_even = (2 * (sub8 % 4)).astype(f32)
    g_odd = g_even + 1.0
    g_all = sub8.astype(f32)
    first4 = sub8 < 4

    def product(first, m):
        c = first + m
        near8 = pl.ds(pl.multiple_of(first + m // 8 * 8, 8), 8)
        x = jnp.broadcast_to(pos[0, near8, :][m % 8 : m % 8 + 1], (8, nv))
        y = jnp.broadcast_to(pos[1, near8, :][m % 8 : m % 8 + 1], (8, nv))
        z = jnp.broadcast_to(pos[2, near8, :][m % 8 : m % 8 + 1], (8, nv))
        f0 = jnp.broadcast_to(force[0, near8, :][m % 8 : m % 8 + 1], (8, nv))
        f1 = jnp.broadcast_to(force[1, near8, :][m % 8 : m % 8 + 1], (8, nv))
        f2 = jnp.broadcast_to(force[2, near8, :][m % 8 : m % 8 + 1], (8, nv))
        h_even = hat(x, g_even)
        h_odd = hat(x, g_odd)
        f01 = jnp.where(first4, f0, f1)
        left = jnp.concatenate(
            [h_even * f01, jnp.where(first4, h_even, h_odd) * f2, h_odd * f01], axis=0
        )
        l_lo = left - left.astype(bf16).astype(f32)
        left2 = jnp.concatenate([left, l_lo], axis=0).astype(bf16)
        hy = hat(y, g_all)
        hz = hat(z, g_all)
        plane = jnp.concatenate(
            [jnp.broadcast_to(hy[j : j + 1], (8, nv)) * hz for j in range(8)], axis=0
        )
        p_hi = plane.astype(bf16)
        p_lo = (plane - p_hi.astype(f32)).astype(bf16)
        prod = nt_dot(left2, jnp.concatenate([p_hi, p_lo], axis=0))
        hats[m] = prod[0:24] + prod[24:48]

    def place(c, m):
        both = hats[m]
        res = (both + pltpu.roll(both, 64, 1)) * stiff[c]
        main = jnp.where(lane < 64, res[0:8], res[16:24])
        mid = res[8:16]
        tail = jnp.where(lane < 64, mid, pltpu.roll(mid, 4, 0))
        t = owner[c]
        r = count[t]
        count[t] = r + 1
        for k in range(12):
            row = main[k : k + 1] if k < 8 else tail[k - 8 : k - 7]
            out[t, :, pl.ds(pl.multiple_of(r * 1536 + 128 * k, 128), 128)] = row
        old = out[t, :, 3072:3200]
        out[t, :, 3072:3200] = jnp.where(lane[0:1] == r, block[c].astype(f32), old)

    group = hats.shape[0]

    def finish(first):
        for m in range(group):
            place(first + m, m)

    for m in range(group):
        product(0, m)

    def step(n, carry):
        finish((n - 1) * group)
        for m in range(group):
            product(n * group, m)
        return carry

    lax.fori_loop(1, cells // group, step, 0)
    finish(cells - group)


def spread(owner, block, positions, stiffness, triangles, neighbours, devices):
    cells, _, verts = positions.shape
    nv = -(-verts // 256) * 256
    inputs = (owner, block, stiffness, jnp.transpose(positions, (1, 2, 0)), jnp.transpose(triangles), jnp.transpose(neighbours))
    hbm = pl.BlockSpec(memory_space=pltpu.HBM)
    vmem = pl.BlockSpec(memory_space=pltpu.VMEM)
    return pl.pallas_call(
        spread_kernel,
        out_shape=jax.ShapeDtypeStruct((devices, 1, WIDE), f32),
        in_specs=[hbm] * 6,
        out_specs=vmem,
        scratch_shapes=[
            pltpu.SMEM((cells,), i32),
            pltpu.SMEM((cells,), i32),
            pltpu.SMEM((cells,), f32),
            pltpu.VMEM((3, verts, cells), f32),
            pltpu.VMEM((3, triangles.shape[0]), i32),
            pltpu.VMEM((6, 32), i32),
            pltpu.SemaphoreType.DMA((6,)),
            pltpu.VMEM((nv, triangles.shape[0]), jnp.float8_e4m3fn),
            pltpu.VMEM((3, cells, nv), f32),
            pltpu.VMEM((3, cells, nv), f32),
            pltpu.VMEM((16, 24, 128), f32),
            pltpu.SMEM((devices,), i32),
        ],
        compiler_params=pltpu.CompilerParams(vmem_limit_bytes=48 << 20),
        name="spread",
    )(*[pltpu.with_memory_space_constraint(x, pltpu.HBM) for x in inputs])


def lane_take(x, index):
    return jnp.take_along_axis(x, index, axis=1, mode="promise_in_bounds")


def column(got, tile):
    tiles = WIDE // 128
    return got[pl.ds(tile, got.shape[0] // tiles, stride=tiles), :]


def find(near, got, square):
    square[...] = jnp.full((128, 128), -1.0, f32)
    square[0:6, 0:32] = near[...].astype(f32)
    goal = jnp.transpose(square[...])[0:32]
    known = column(got, 25)
    k_hi = known.astype(bf16)
    k_lo = (known - k_hi.astype(f32)).astype(bf16)
    lane = lax.broadcasted_iota(i32, (32, 128), 1)
    for f1 in range(4):
        first = jnp.broadcast_to(goal[:, f1 : f1 + 1], (32, 128)).astype(i32)
        safe = jnp.maximum(first, 0)
        pick = (lax.shift_right_logical(safe, 5) == lane).astype(f32).astype(bf16)
        rows = jnp.dot(pick, k_hi, preferred_element_type=f32) + jnp.dot(pick, k_lo, preferred_element_type=f32)
        for n, q in enumerate(EDGE_Q):
            d1, d2 = [d for d in range(3) if vel[q][d]]
            if f1 == 2 * d1 + (1 if vel[q][d1] == 1 else 0):
                f2 = 2 * d2 + (1 if vel[q][d2] == 1 else 0)
                second = lane_take(rows, (f2 - 2) * 32 + lax.bitwise_and(safe, 31))
                goal = jnp.where(lane == 6 + n, jnp.where(first >= 0, second, -1.0), goal)
    return goal


def collide_kernel(near, got, pops, post, table, goal, body, square):
    slots = got.shape[0] * 128 // WIDE
    found = find(near, got, square)
    lane = lax.broadcasted_iota(i32, (slots, 128), 1)
    ids = column(got, 24)
    picks = []
    for r in range(2):
        col = jnp.broadcast_to(ids[:, r : r + 1], (slots, 128))
        hit = (col == lane.astype(f32)).astype(f32)
        picks.append(jnp.transpose(hit)[0:32].astype(bf16))
    for n in range(3):
        total = jnp.zeros((32, 512), f32)
        for r in range(2):
            part = jnp.concatenate([column(got, 12 * r + 4 * n + a) for a in range(4)], axis=1)
            hi = part.astype(bf16)
            lo = (part - hi.astype(f32)).astype(bf16)
            total = total + jnp.dot(picks[r], hi, preferred_element_type=f32)
            total = total + jnp.dot(picks[r], lo, preferred_element_type=f32)
        body[n] = total
    lanes = lax.broadcasted_iota(i32, (8, 128), 1)
    low = lanes < 64
    keep = 1.0 - 1.0 / relax_time
    gain = 1.0 - 0.5 / relax_time

    def group(g, carry):
        rows = pl.ds(pl.multiple_of(g * 8, 8), 8)
        for a in range(4):
            cut = slice(128 * a, 128 * (a + 1))
            f = [pops[q, rows, cut] * wts[q] for q in range(19)]
            force = [body[d, rows, cut] for d in range(3)]
            rho = f[0]
            for q in range(1, 19):
                rho = rho + f[q]
            u = []
            for d in range(3):
                m = 0.5 * force[d]
                for q in range(1, 19):
                    if vel[q][d] == 1:
                        m = m + f[q]
                    elif vel[q][d] == -1:
                        m = m - f[q]
                u.append(m / rho)
            speed = u[0] * u[0] + u[1] * u[1] + u[2] * u[2]
            work = u[0] * force[0] + u[1] * force[1] + u[2] * force[2]
            rho_t = rho * (1.0 / relax_time)
            flat = rho_t * (1.0 - 1.5 * speed) - (3.0 * gain) * work
            post[0, rows, cut] = keep * f[0] + wts[0] * flat
            for q in range(1, 19, 2):
                along = push = None
                for d in range(3):
                    e = vel[q][d]
                    if e:
                        along = e * u[d] if along is None else along + e * u[d]
                        push = e * force[d] if push is None else push + e * force[d]
                even = wts[q] * (flat + along * (4.5 * rho_t * along + (9.0 * gain) * push))
                odd = wts[q] * (3.0 * rho_t * along + (3.0 * gain) * push)
                post[q, rows, cut] = keep * f[q] + (even + odd)
                post[q + 1, rows, cut] = keep * f[q + 1] + (even - odd)
        for n in range(5):
            table[n, rows, :] = jnp.where(low, post[NEG[0][n], rows, 0:128], post[POS[0][n], rows, 384:512])
            first, second = (lanes >> 3) & 7, lanes & 7
            for ax in (1, 2):
                picked = None
                for a in range(4):
                    inside = (first & 1) * 64
                    if ax == 1:
                        at_low, at_high = inside + second, inside + 56 + second
                    else:
                        at_low, at_high = inside + second * 8, inside + second * 8 + 7
                    cut = slice(128 * a, 128 * (a + 1))
                    val = jnp.where(
                        low, lane_take(post[NEG[ax][n], rows, cut], at_low), lane_take(post[POS[ax][n], rows, cut], at_high)
                    )
                    picked = val if picked is None else jnp.where(first >> 1 == a, val, picked)
                table[5 * ax + n, rows, :] = picked
        line = jnp.ones((8, 128), f32)
        w = lanes & 7
        for n, q in enumerate(EDGE_Q):
            ex, ey, ez = vel[q]
            at = [7 if e == 1 else 0 for e in vel[q]]
            mine = lanes >> 3 == n
            if ex:
                a = 3 if ex == 1 else 0
                base = 64 if ex == 1 else 0
                where_ = base + (at[1] * 8 + w if ey else w * 8 + at[2])
                val = lane_take(post[q, rows, 128 * a : 128 * (a + 1)], where_)
                line = jnp.where(mine, val, line)
            else:
                where_ = (w & 1) * 64 + at[1] * 8 + at[2]
                for a in range(4):
                    val = lane_take(post[q, rows, 128 * a : 128 * (a + 1)], where_)
                    line = jnp.where(mine & (w >> 1 == a), val, line)
        table[EDGE_TILE, rows, :] = line
        return carry

    lax.fori_loop(0, 4, group, 0, unroll=True)
    goal[...] = found
    lane = lax.broadcasted_iota(i32, (32, 128), 1)
    table[EDGE_TILE] = jnp.where((lane >= IDS) & (lane < HAVE), pltpu.roll(found, IDS, 1), table[EDGE_TILE])


def collide(got, populations, neighbours):
    vmem = pl.BlockSpec(memory_space=pltpu.VMEM)
    return pl.pallas_call(
        collide_kernel,
        out_shape=(
            jax.ShapeDtypeStruct((19, 32, 512), f32),
            jax.ShapeDtypeStruct((NT, 32, 128), f32),
            jax.ShapeDtypeStruct((32, 128), f32),
        ),
        in_specs=[vmem, vmem, vmem],
        out_specs=(vmem, vmem, vmem),
        scratch_shapes=[
            pltpu.VMEM((3, 32, 512), f32),
            pltpu.VMEM((128, 128), f32),
        ],
        compiler_params=pltpu.CompilerParams(vmem_limit_bytes=48 << 20),
        name="collide",
    )(jnp.transpose(neighbours), got, jnp.transpose(populations, (1, 0, 2)))


def route_kernel(sizes, left2, left, mine, right, right2, down, own, up, down2, up2, lines):
    n_gy = sizes[1]
    me_x, me_y = lax.axis_index("gx"), lax.axis_index("gy")
    for n, part in enumerate((left[EDGE_TILE], mine[EDGE_TILE], right[EDGE_TILE], left2[0], right2[0])):
        lines[32 * n : 32 * (n + 1), :] = part
    lines[160:256, :] = jnp.full((96, 128), -1.0, f32)
    ids = [jnp.transpose(lines[0:128, :]), jnp.transpose(lines[128:256, :])]
    slot = lax.broadcasted_iota(i32, (32, 128), 0).astype(f32)
    low = lax.broadcasted_iota(i32, (32, 128), 1) < 64
    named = {}
    for dy in range(-2, 3):
        owner = me_x * n_gy + lax.rem(me_y + (dy + n_gy), n_gy)
        named[dy] = slot + (owner * 32).astype(f32)

    def hot(half, row, dy):
        picked = jnp.broadcast_to(ids[half][IDS + row : IDS + row + 1, :], (32, 128)) == named[dy]
        return picked.astype(f32)

    none = jnp.zeros((32, 128), f32)
    for ax in range(3):
        planes = jnp.concatenate(
            [
                jnp.concatenate([left[t], mine[t], right[t], none], axis=0)
                for t in range(5 * ax, 5 * ax + 5)
            ],
            axis=1,
        )
        p_hi = planes.astype(bf16)
        p_lo = (planes - p_hi.astype(f32)).astype(bf16)
        picks = jnp.concatenate([hot(0, 2 * ax + s, dy) for s in range(2) for dy in (-1, 0, 1)], axis=0).astype(bf16)
        moved = jnp.dot(picks, p_hi, preferred_element_type=f32) + jnp.dot(picks, p_lo, preferred_element_type=f32)
        for k, goal in enumerate((down, own, up)):
            for n in range(5):
                cut = slice(128 * n, 128 * (n + 1))
                goal[5 * ax + n] = jnp.where(
                    low, moved[32 * k : 32 * (k + 1), cut], moved[96 + 32 * k : 96 + 32 * (k + 1), cut]
                )
    e_hi = lines[...].astype(bf16)
    e_lo = (lines[...] - e_hi.astype(f32)).astype(bf16)
    both = jnp.concatenate([e_hi, e_lo], axis=1)
    lane = lax.broadcasted_iota(i32, (160, 128), 1)
    total = jnp.zeros((160, 128), f32)
    for n in range(12):
        picks = jnp.concatenate(
            [jnp.concatenate([hot(h, 6 + n, dy) for dy in range(-2, 3)], axis=0) for h in range(2)], axis=1
        ).astype(bf16)
        moved = jnp.dot(picks, both, preferred_element_type=f32)
        wanted = (lane >> 3 == n) | (lane == HAVE + n)
        total = jnp.where(wanted, moved[:, 0:128] + moved[:, 128:256], total)
    for k, goal in enumerate((down2, down, own, up, up2)):
        goal[goal.shape[0] - 1] = total[32 * k : 32 * (k + 1)]


def route(left2, left, mine, right, right2):
    vmem = pl.BlockSpec(memory_space=pltpu.VMEM)
    sizes = (lax.axis_size("gx"), lax.axis_size("gy"))
    big = jax.ShapeDtypeStruct(mine.shape, f32)
    small = jax.ShapeDtypeStruct(left2.shape, f32)
    return pl.pallas_call(
        functools.partial(route_kernel, sizes),
        out_shape=(big, big, big, small, small),
        in_specs=[vmem] * 5,
        out_specs=(vmem,) * 5,
        scratch_shapes=[pltpu.VMEM((256, 128), f32)],
        compiler_params=pltpu.CompilerParams(vmem_limit_bytes=48 << 20),
        name="route",
    )(left2, left, mine, right, right2)


def crossings(q, a):
    lanes = lax.broadcasted_iota(i32, (8, 128), 1)
    coords = (2 * a + (lanes >> 6), (lanes >> 3) & 7, lanes & 7)
    e = vel[q]
    found = [None if e[d] == 0 else coords[d] == (0 if e[d] == 1 else 7) for d in range(3)]
    if e[0] == 1 and a != 0 or e[0] == -1 and a != 3:
        found[0] = None
    return coords, found, [d for d in range(3) if found[d] is not None]


def inside_kernel(post, most):
    lanes = lax.broadcasted_iota(i32, (8, 128), 1)
    for g in range(4):
        rows = slice(8 * g, 8 * g + 8)
        most[0, rows, :] = post[0, rows, :]
        for q in range(1, 19):
            ex, ey, ez = vel[q]
            shift = ex * 64 + ey * 8 + ez
            rolled = [pltpu.roll(post[q, rows, 128 * a : 128 * (a + 1)], shift % 128, 1) for a in range(4)]
            for a in range(4):
                if shift > 0:
                    val = jnp.where(lanes < shift, rolled[(a - 1) % 4], rolled[a])
                else:
                    val = jnp.where(lanes >= 128 + shift, rolled[(a + 1) % 4], rolled[a])
                coords, crossing, axes = crossings(q, a)
                if axes:
                    out_of = crossing[axes[0]]
                    for d in axes[1:]:
                        out_of = out_of | crossing[d]
                    val = jnp.where(out_of, post[opposite[q], rows, 128 * a : 128 * (a + 1)], val)
                most[q, rows, 128 * a : 128 * (a + 1)] = val


def inside(post):
    vmem = pl.BlockSpec(memory_space=pltpu.VMEM)
    return pl.pallas_call(
        inside_kernel,
        out_shape=jax.ShapeDtypeStruct(post.shape, f32),
        in_specs=[vmem],
        out_specs=vmem,
        compiler_params=pltpu.CompilerParams(vmem_limit_bytes=48 << 20),
        name="inside",
    )(post)


def opened(ax):
    lane = lax.broadcasted_iota(i32, (128, 512), 0)
    site = lax.broadcasted_iota(i32, (128, 512), 1)
    i, j, k = site >> 6, (site >> 3) & 7, site & 7
    along, across = (k, j) if ax == 1 else (j, k)
    wanted = jnp.where(lane < 64, 7, 0)
    return ((i * 8 + along == (lane & 63)) & (across == wanted)).astype(f32).astype(bf16)


def ghost_kernel(goal, most, own, below, above, below2, above2, result, out, ghost, sem):
    lanes = lax.broadcasted_iota(i32, (8, 128), 1)
    low = lax.broadcasted_iota(i32, (32, 128), 1) < 64
    for ax in (1, 2):
        other = 2 if ax == 1 else 1
        shifted = []
        for n in range(5):
            t = 5 * ax + n
            came = own[t] + below[t] + above[t]
            steps = [(vel[q][0] * 8 + vel[q][other]) % 128 for q in (NEG[ax][n], POS[ax][n])]
            both = [pltpu.roll(came, step, 1) if step else came for step in steps]
            shifted.append(jnp.where(low, both[0], both[1]))
        planes = jnp.concatenate(shifted, axis=0)
        p_hi = planes.astype(bf16)
        p_lo = (planes - p_hi.astype(f32)).astype(bf16)
        to = opened(ax)
        ghost[ax - 1] = jnp.dot(p_hi, to, preferred_element_type=f32) + jnp.dot(p_lo, to, preferred_element_type=f32)
    leaving = []
    for g in range(4):
        rows = slice(8 * g, 8 * g + 8)
        near = goal[rows, :]
        there = [lane_take(near, jnp.full((8, 128), f, i32)) >= 0.0 for f in range(6)]
        came = own[EDGE_TILE, rows, :] + below[EDGE_TILE, rows, :] + above[EDGE_TILE, rows, :]
        came = came + below2[0, rows, :] + above2[0, rows, :]
        have = lane_take(came, jnp.minimum(HAVE + (lanes >> 3), 127)) > 0.5
        edges = jnp.where(have, came, jnp.nan)
        out[0, rows, :] = most[0, rows, :]
        for q in range(1, 19):
            e = vel[q]
            ex, ey, ez = e
            for a in range(4):
                val = most[q, rows, 128 * a : 128 * (a + 1)]
                (ii, jj, kk), crossing, axes = crossings(q, a)
                for d in axes:
                    n = (POS[d] if e[d] == 1 else NEG[d]).index(q)
                    if d == 0:
                        source = own[n, rows, :] + below[n, rows, :] + above[n, rows, :]
                        brought = pltpu.roll(source, (64 + ey * 8 + ez) % 128, 1)
                    else:
                        brought = ghost[d - 1, 32 * n + 8 * g : 32 * n + 8 * g + 8, 128 * a : 128 * (a + 1)]
                    use = crossing[d] & there[2 * d + (0 if e[d] == 1 else 1)]
                    for other in axes:
                        if other != d:
                            use = use & ~crossing[other]
                    val = jnp.where(use, brought, val)
                if len(axes) == 2:
                    along = kk if ez == 0 else (jj if ey == 0 else ii)
                    brought = lane_take(edges, 8 * (q - 7) + along)
                    val = jnp.where(crossing[axes[0]] & crossing[axes[1]] & (brought == brought), brought, val)
                out[q, rows, 128 * a : 128 * (a + 1)] = val
        leaving.append(pltpu.make_async_copy(out.at[:, rows, :], result.at[:, rows, :], sem.at[g]))
        leaving[-1].start()
    for c in leaving:
        c.wait()


def fill(goal, post, *parts):
    vmem = pl.BlockSpec(memory_space=pltpu.VMEM)
    return pl.pallas_call(
        ghost_kernel,
        out_shape=jax.ShapeDtypeStruct((19, 32, 512), f32),
        in_specs=[vmem] * 7,
        out_specs=pl.BlockSpec(memory_space=pltpu.HBM),
        scratch_shapes=[pltpu.VMEM(post.shape, f32), pltpu.VMEM((2, 160, 512), f32), pltpu.SemaphoreType.DMA((4,))],
        compiler_params=pltpu.CompilerParams(vmem_limit_bytes=48 << 20),
        name="fill",
    )(goal, post, *parts)


def send(array, axis, step):
    size = lax.axis_size(axis)
    return lax.ppermute(array, axis, [(i, (i + step) % size) for i in range(size)])


def exchange(table):
    edge = table[EDGE_TILE : EDGE_TILE + 1]
    left, right = send(table, "gx", 1), send(table, "gx", -1)
    left2, right2 = send(edge, "gx", 2), send(edge, "gx", -2)
    down, own, up, down2, up2 = route(left2, left, table, right, right2)
    return own, send(up, "gy", 1), send(down, "gy", -1), send(up2, "gy", 2), send(down2, "gy", -2)


def body(populations, neighbours, positions, stiffness, cell_owner, cell_block, triangles):
    devices = lax.axis_size("gx") * lax.axis_size("gy")
    slots = spread(cell_owner[:, 0], cell_block, positions, stiffness, triangles, neighbours, devices)
    got = lax.all_to_all(slots, BOTH, split_axis=0, concat_axis=0, tiled=True)
    post, table, goal = collide(got.reshape(-1, 128), populations, neighbours)
    result = fill(goal, inside(post), *exchange(table))
    return jnp.transpose(result, (1, 0, 2))


def solution(mesh):
    placed = (
        P(BOTH, None, None),
        P(BOTH, None),
        P(BOTH, None, None),
        P(BOTH),
        P(BOTH, None),
        P(BOTH),
        P(),
    )
    return jax.shard_map(
        body, mesh=mesh, in_specs=placed, out_specs=P(BOTH, None, None), check_vma=False
    )
```

```python
import functools

import jax
import jax.numpy as jnp
import numpy as np
from jax import lax
from jax.experimental import pallas as pl
from jax.experimental.pallas import tpu as pltpu
from jax.sharding import PartitionSpec as P

vel = [
    (0, 0, 0), (1, 0, 0), (-1, 0, 0), (0, 1, 0), (0, -1, 0), (0, 0, 1), (0, 0, -1),
    (1, 1, 0), (-1, -1, 0), (1, -1, 0), (-1, 1, 0),
    (1, 0, 1), (-1, 0, -1), (1, 0, -1), (-1, 0, 1),
    (0, 1, 1), (0, -1, -1), (0, 1, -1), (0, -1, 1),
]
wts = [1.0 / 3.0] + [1.0 / 18.0] * 6 + [1.0 / 36.0] * 12
opposite = [0, 2, 1, 4, 3, 6, 5, 8, 7, 10, 9, 12, 11, 14, 13, 16, 15, 18, 17]
relax_time = 0.6
NEG, POS = {}, {}
for ax in range(3):
    NEG[ax] = [q for q in range(19) if vel[q][ax] == -1]
    POS[ax] = [q for q in range(19) if vel[q][ax] == 1]
EDGE_Q = list(range(7, 19))
FACE_TILES = 15
EDGE_TILE = 15
NT = 16
IDS = 96
HAVE = 114
WIDE = 3328
BOTH = ("gx", "gy")
f32, bf16, i32 = jnp.float32, jnp.bfloat16, jnp.int32


def nt_dot(a, b):
    return lax.dot_general(a, b, (((1,), (1,)), ((), ())), preferred_element_type=f32)


def hat(x, grid):
    return jnp.maximum(0.0, 1.0 - jnp.abs(x - grid))


def spread_kernel(owner_in, block_in, stiff_in, raw_in, tri_in, near_in, out, owner, block, stiff, raw, tri, near, sem, st, pos, force, hats, count):
    cells, nv = pos.shape[1:]
    verts = raw.shape[1]
    pairs = ((tri_in, tri), (raw_in, raw), (near_in, near), (owner_in, owner), (block_in, block), (stiff_in, stiff))
    copies = [pltpu.make_async_copy(a, b, sem.at[n]) for n, (a, b) in enumerate(pairs)]
    for c in copies:
        c.start()
    copies[0].wait()
    for r in range(0, nv, 128):
        ids = lax.broadcasted_iota(i32, (128, tri.shape[1]), 0) + r
        hit = (ids == tri[0:1, :]) | (ids == tri[1:2, :]) | (ids == tri[2:3, :])
        st[r : r + 128, :] = hit.astype(f32).astype(jnp.float8_e4m3fn)
    links = nt_dot(st[...], st[...])
    for c in copies[1:]:
        c.wait()
    for r in range(0, nv, 128):
        for d in range(3):
            have = min(verts - r, 128)
            piece = raw[d, r : r + have, :]
            if have < 128:
                piece = jnp.concatenate([piece, jnp.full((128 - have, cells), -100.0, f32)], axis=0)
            pos[d, :, r : r + 128] = jnp.transpose(piece)
    rows = lax.broadcasted_iota(i32, (nv, nv), 0)
    cols = lax.broadcasted_iota(i32, (nv, nv), 1)
    springs = jnp.where(rows == cols, -2.0 * links, links)
    s_hi = springs.astype(bf16)
    s_lo = (springs - s_hi.astype(f32)).astype(bf16)
    x = jnp.concatenate([pos[0], pos[1], pos[2]], axis=0)
    x_hi = x.astype(bf16)
    x_lo = (x - x_hi.astype(f32)).astype(bf16)
    most = jnp.dot(jnp.concatenate([x_hi, x_lo], axis=0), s_hi, preferred_element_type=f32)
    for d in range(3):
        lo, hi = d * cells, (d + 1) * cells
        force[d] = most[lo:hi] + most[3 * cells + lo : 3 * cells + hi]

    @pl.when(jnp.max(jnp.abs(springs)) > 256.0)
    def _():
        rest = jnp.dot(x_hi, s_lo, preferred_element_type=f32)
        for d in range(3):
            force[d] = force[d] + rest[d * cells : (d + 1) * cells]

    sub = lax.broadcasted_iota(i32, (8, 128), 0)
    lane = lax.broadcasted_iota(i32, (8, 128), 1)
    slots = out.shape[0]
    tail_row = jnp.full((8, 128), -1.0, f32)
    table_row = jnp.zeros((8, 128), f32)
    for f in range(4):
        one_face = jnp.concatenate([near[f + 2 : f + 3, :].astype(f32), jnp.zeros((1, 96), f32)], axis=1)
        one_face = jnp.broadcast_to(one_face, (8, 128))
        table_row = jnp.where(lane // 32 == f, pltpu.roll(one_face, 32 * f, 1) if f else one_face, table_row)

    def clear(t, carry):
        for m in range(8):
            out[t * 8 + m, :, 0:3072] = jnp.zeros((1, 3072), f32)
            out[t * 8 + m, :, 3072:3200] = tail_row[0:1]
            out[t * 8 + m, :, 3200:3328] = table_row[0:1]
            count[t * 8 + m] = 0
        return carry

    lax.fori_loop(0, slots // 8, clear, 0)
    sub8 = lax.broadcasted_iota(i32, (8, nv), 0)
    g_even = (2 * (sub8 % 4)).astype(f32)
    g_odd = g_even + 1.0
    g_all = sub8.astype(f32)
    first4 = sub8 < 4

    def product(first, m):
        c = first + m
        near8 = pl.ds(pl.multiple_of(first + m // 8 * 8, 8), 8)
        x = jnp.broadcast_to(pos[0, near8, :][m % 8 : m % 8 + 1], (8, nv))
        y = jnp.broadcast_to(pos[1, near8, :][m % 8 : m % 8 + 1], (8, nv))
        z = jnp.broadcast_to(pos[2, near8, :][m % 8 : m % 8 + 1], (8, nv))
        f0 = jnp.broadcast_to(force[0, near8, :][m % 8 : m % 8 + 1], (8, nv))
        f1 = jnp.broadcast_to(force[1, near8, :][m % 8 : m % 8 + 1], (8, nv))
        f2 = jnp.broadcast_to(force[2, near8, :][m % 8 : m % 8 + 1], (8, nv))
        h_even = hat(x, g_even)
        h_odd = hat(x, g_odd)
        f01 = jnp.where(first4, f0, f1)
        left = jnp.concatenate(
            [h_even * f01, jnp.where(first4, h_even, h_odd) * f2, h_odd * f01], axis=0
        )
        l_lo = left - left.astype(bf16).astype(f32)
        left2 = jnp.concatenate([left, l_lo], axis=0).astype(bf16)
        hy = hat(y, g_all)
        hz = hat(z, g_all)
        plane = jnp.concatenate(
            [jnp.broadcast_to(hy[j : j + 1], (8, nv)) * hz for j in range(8)], axis=0
        )
        p_hi = plane.astype(bf16)
        p_lo = (plane - p_hi.astype(f32)).astype(bf16)
        prod = nt_dot(left2, jnp.concatenate([p_hi, p_lo], axis=0))
        hats[m] = prod[0:24] + prod[24:48]

    def place(c, m):
        both = hats[m]
        res = (both + pltpu.roll(both, 64, 1)) * stiff[c]
        main = jnp.where(lane < 64, res[0:8], res[16:24])
        mid = res[8:16]
        tail = jnp.where(lane < 64, mid, pltpu.roll(mid, 4, 0))
        t = owner[c]
        r = count[t]
        count[t] = r + 1
        for k in range(12):
            row = main[k : k + 1] if k < 8 else tail[k - 8 : k - 7]
            out[t, :, pl.ds(pl.multiple_of(r * 1536 + 128 * k, 128), 128)] = row
        old = out[t, :, 3072:3200]
        out[t, :, 3072:3200] = jnp.where(lane[0:1] == r, block[c].astype(f32), old)

    group = hats.shape[0]

    def finish(first):
        for m in range(group):
            place(first + m, m)

    for m in range(group):
        product(0, m)

    def step(n, carry):
        finish((n - 1) * group)
        for m in range(group):
            product(n * group, m)
        return carry

    lax.fori_loop(1, cells // group, step, 0)
    finish(cells - group)


def spread(owner, block, positions, stiffness, triangles, neighbours, devices):
    cells, _, verts = positions.shape
    nv = -(-verts // 256) * 256
    inputs = (owner, block, stiffness, jnp.transpose(positions, (1, 2, 0)), jnp.transpose(triangles), jnp.transpose(neighbours))
    hbm = pl.BlockSpec(memory_space=pltpu.HBM)
    vmem = pl.BlockSpec(memory_space=pltpu.VMEM)
    return pl.pallas_call(
        spread_kernel,
        out_shape=jax.ShapeDtypeStruct((devices, 1, WIDE), f32),
        in_specs=[hbm] * 6,
        out_specs=vmem,
        scratch_shapes=[
            pltpu.SMEM((cells,), i32),
            pltpu.SMEM((cells,), i32),
            pltpu.SMEM((cells,), f32),
            pltpu.VMEM((3, verts, cells), f32),
            pltpu.VMEM((3, triangles.shape[0]), i32),
            pltpu.VMEM((6, 32), i32),
            pltpu.SemaphoreType.DMA((6,)),
            pltpu.VMEM((nv, triangles.shape[0]), jnp.float8_e4m3fn),
            pltpu.VMEM((3, cells, nv), f32),
            pltpu.VMEM((3, cells, nv), f32),
            pltpu.VMEM((16, 24, 128), f32),
            pltpu.SMEM((devices,), i32),
        ],
        compiler_params=pltpu.CompilerParams(vmem_limit_bytes=48 << 20),
        name="spread",
    )(*[pltpu.with_memory_space_constraint(x, pltpu.HBM) for x in inputs])


def lane_take(x, index):
    return jnp.take_along_axis(x, index, axis=1, mode="promise_in_bounds")


def column(got, tile):
    tiles = WIDE // 128
    return got[pl.ds(tile, got.shape[0] // tiles, stride=tiles), :]


def find(near, got, square):
    square[...] = jnp.full((128, 128), -1.0, f32)
    square[0:6, 0:32] = near[...].astype(f32)
    goal = jnp.transpose(square[...])[0:32]
    known = column(got, 25)
    k_hi = known.astype(bf16)
    k_lo = (known - k_hi.astype(f32)).astype(bf16)
    lane = lax.broadcasted_iota(i32, (32, 128), 1)
    firsts = [lane_take(goal, jnp.full((32, 128), f1, i32)).astype(i32) for f1 in range(4)]
    picks = [(lax.shift_right_logical(jnp.maximum(first, 0), 5) == lane).astype(f32) for first in firsts]
    found = jnp.dot(
        jnp.concatenate(picks, axis=0).astype(bf16), jnp.concatenate([k_hi, k_lo], axis=1), preferred_element_type=f32
    )
    for f1, first in enumerate(firsts):
        safe = jnp.maximum(first, 0)
        rows = found[32 * f1 : 32 * (f1 + 1), 0:128] + found[32 * f1 : 32 * (f1 + 1), 128:256]
        for n, q in enumerate(EDGE_Q):
            d1, d2 = [d for d in range(3) if vel[q][d]]
            if f1 == 2 * d1 + (1 if vel[q][d1] == 1 else 0):
                f2 = 2 * d2 + (1 if vel[q][d2] == 1 else 0)
                second = lane_take(rows, (f2 - 2) * 32 + lax.bitwise_and(safe, 31))
                goal = jnp.where(lane == 6 + n, jnp.where(first >= 0, second, -1.0), goal)
    return goal


def collide_kernel(near, got, pops, post, table, edge, goal, body, square):
    slots = got.shape[0] * 128 // WIDE
    found = find(near, got, square)
    lane = lax.broadcasted_iota(i32, (slots, 128), 1)
    ids = column(got, 24)
    picks = []
    for r in range(2):
        col = jnp.broadcast_to(ids[:, r : r + 1], (slots, 128))
        hit = (col == lane.astype(f32)).astype(f32)
        picks.append(jnp.transpose(hit)[0:32].astype(bf16))
    for n in range(3):
        total = jnp.zeros((32, 512), f32)
        for r in range(2):
            part = jnp.concatenate([column(got, 12 * r + 4 * n + a) for a in range(4)], axis=1)
            hi = part.astype(bf16)
            lo = (part - hi.astype(f32)).astype(bf16)
            total = total + jnp.dot(picks[r], hi, preferred_element_type=f32)
            total = total + jnp.dot(picks[r], lo, preferred_element_type=f32)
        body[n] = total
    lanes = lax.broadcasted_iota(i32, (8, 128), 1)
    low = lanes < 64
    keep = 1.0 - 1.0 / relax_time
    gain = 1.0 - 0.5 / relax_time

    def group(g, carry):
        rows = pl.ds(pl.multiple_of(g * 8, 8), 8)
        for a in range(4):
            cut = slice(128 * a, 128 * (a + 1))
            f = [pops[q, rows, cut] * wts[q] for q in range(19)]
            force = [body[d, rows, cut] for d in range(3)]
            rho = f[0]
            for q in range(1, 19):
                rho = rho + f[q]
            u = []
            for d in range(3):
                m = 0.5 * force[d]
                for q in range(1, 19):
                    if vel[q][d] == 1:
                        m = m + f[q]
                    elif vel[q][d] == -1:
                        m = m - f[q]
                u.append(m / rho)
            speed = u[0] * u[0] + u[1] * u[1] + u[2] * u[2]
            work = u[0] * force[0] + u[1] * force[1] + u[2] * force[2]
            rho_t = rho * (1.0 / relax_time)
            flat = rho_t * (1.0 - 1.5 * speed) - (3.0 * gain) * work
            post[0, rows, cut] = keep * f[0] + wts[0] * flat
            for q in range(1, 19, 2):
                along = push = None
                for d in range(3):
                    e = vel[q][d]
                    if e:
                        along = e * u[d] if along is None else along + e * u[d]
                        push = e * force[d] if push is None else push + e * force[d]
                even = wts[q] * (flat + along * (4.5 * rho_t * along + (9.0 * gain) * push))
                odd = wts[q] * (3.0 * rho_t * along + (3.0 * gain) * push)
                post[q, rows, cut] = keep * f[q] + (even + odd)
                post[q + 1, rows, cut] = keep * f[q + 1] + (even - odd)
        for n in range(5):
            table[n, rows, :] = jnp.where(low, post[NEG[0][n], rows, 0:128], post[POS[0][n], rows, 384:512])
            first, second = (lanes >> 3) & 7, lanes & 7
            for ax in (1, 2):
                picked = None
                for a in range(4):
                    inside = (first & 1) * 64
                    if ax == 1:
                        at_low, at_high = inside + second, inside + 56 + second
                    else:
                        at_low, at_high = inside + second * 8, inside + second * 8 + 7
                    cut = slice(128 * a, 128 * (a + 1))
                    val = jnp.where(
                        low, lane_take(post[NEG[ax][n], rows, cut], at_low), lane_take(post[POS[ax][n], rows, cut], at_high)
                    )
                    picked = val if picked is None else jnp.where(first >> 1 == a, val, picked)
                table[5 * ax + n, rows, :] = picked
        line = jnp.ones((8, 128), f32)
        w = lanes & 7
        for n, q in enumerate(EDGE_Q):
            ex, ey, ez = vel[q]
            at = [7 if e == 1 else 0 for e in vel[q]]
            mine = lanes >> 3 == n
            if ex:
                a = 3 if ex == 1 else 0
                base = 64 if ex == 1 else 0
                where_ = base + (at[1] * 8 + w if ey else w * 8 + at[2])
                val = lane_take(post[q, rows, 128 * a : 128 * (a + 1)], where_)
                line = jnp.where(mine, val, line)
            else:
                where_ = (w & 1) * 64 + at[1] * 8 + at[2]
                for a in range(4):
                    val = lane_take(post[q, rows, 128 * a : 128 * (a + 1)], where_)
                    line = jnp.where(mine & (w >> 1 == a), val, line)
        table[EDGE_TILE, rows, :] = line
        return carry

    lax.fori_loop(0, 4, group, 0, unroll=True)
    goal[...] = found
    lane = lax.broadcasted_iota(i32, (32, 128), 1)
    lines = jnp.where((lane >= IDS) & (lane < HAVE), pltpu.roll(found, IDS, 1), table[EDGE_TILE])
    table[EDGE_TILE] = lines
    edge[0] = lines


def collide(got, populations, neighbours):
    vmem = pl.BlockSpec(memory_space=pltpu.VMEM)
    return pl.pallas_call(
        collide_kernel,
        out_shape=(
            jax.ShapeDtypeStruct((19, 32, 512), f32),
            jax.ShapeDtypeStruct((NT, 32, 128), f32),
            jax.ShapeDtypeStruct((1, 32, 128), f32),
            jax.ShapeDtypeStruct((32, 128), f32),
        ),
        in_specs=[vmem, vmem, vmem],
        out_specs=(vmem,) * 4,
        scratch_shapes=[
            pltpu.VMEM((3, 32, 512), f32),
            pltpu.VMEM((128, 128), f32),
        ],
        compiler_params=pltpu.CompilerParams(vmem_limit_bytes=48 << 20),
        name="collide",
    )(jnp.transpose(neighbours), got, jnp.transpose(populations, (1, 0, 2)))


def route_kernel(sizes, left2, left, mine, right, right2, down, own, up, down2, up2, lines):
    n_gy = sizes[1]
    me_x, me_y = lax.axis_index("gx"), lax.axis_index("gy")
    for n, part in enumerate((left[EDGE_TILE], mine[EDGE_TILE], right[EDGE_TILE], left2[0], right2[0])):
        lines[32 * n : 32 * (n + 1), :] = part
    lines[160:256, :] = jnp.full((96, 128), -1.0, f32)
    ids = [jnp.transpose(lines[0:128, :]), jnp.transpose(lines[128:256, :])]
    slot = lax.broadcasted_iota(i32, (32, 128), 0).astype(f32)
    low = lax.broadcasted_iota(i32, (32, 128), 1) < 64
    named = {}
    for dy in range(-2, 3):
        owner = me_x * n_gy + lax.rem(me_y + (dy + n_gy), n_gy)
        named[dy] = slot + (owner * 32).astype(f32)

    def hot(half, row, dy):
        picked = jnp.broadcast_to(ids[half][IDS + row : IDS + row + 1, :], (32, 128)) == named[dy]
        return picked.astype(f32)

    none = jnp.zeros((32, 128), f32)
    for ax in range(3):
        planes = jnp.concatenate(
            [
                jnp.concatenate([left[t], mine[t], right[t], none], axis=0)
                for t in range(5 * ax, 5 * ax + 5)
            ],
            axis=1,
        )
        p_hi = planes.astype(bf16)
        p_lo = (planes - p_hi.astype(f32)).astype(bf16)
        picks = jnp.concatenate([hot(0, 2 * ax + s, dy) for s in range(2) for dy in (-1, 0, 1)], axis=0).astype(bf16)
        moved = jnp.dot(picks, p_hi, preferred_element_type=f32) + jnp.dot(picks, p_lo, preferred_element_type=f32)
        for k, goal in enumerate((down, own, up)):
            for n in range(5):
                cut = slice(128 * n, 128 * (n + 1))
                goal[5 * ax + n] = jnp.where(
                    low, moved[32 * k : 32 * (k + 1), cut], moved[96 + 32 * k : 96 + 32 * (k + 1), cut]
                )
    e_hi = lines[...].astype(bf16)
    e_lo = (lines[...] - e_hi.astype(f32)).astype(bf16)
    both = jnp.concatenate([e_hi, e_lo], axis=1)
    lane = lax.broadcasted_iota(i32, (160, 128), 1)
    total = jnp.zeros((160, 128), f32)
    for n in range(12):
        picks = jnp.concatenate(
            [jnp.concatenate([hot(h, 6 + n, dy) for dy in range(-2, 3)], axis=0) for h in range(2)], axis=1
        ).astype(bf16)
        moved = jnp.dot(picks, both, preferred_element_type=f32)
        wanted = (lane >> 3 == n) | (lane == HAVE + n)
        total = jnp.where(wanted, moved[:, 0:128] + moved[:, 128:256], total)
    for k, goal in enumerate((down2, down, own, up, up2)):
        goal[goal.shape[0] - 1] = total[32 * k : 32 * (k + 1)]


def route(left2, left, mine, right, right2):
    vmem = pl.BlockSpec(memory_space=pltpu.VMEM)
    sizes = (lax.axis_size("gx"), lax.axis_size("gy"))
    big = jax.ShapeDtypeStruct(mine.shape, f32)
    small = jax.ShapeDtypeStruct(left2.shape, f32)
    return pl.pallas_call(
        functools.partial(route_kernel, sizes),
        out_shape=(big, big, big, small, small),
        in_specs=[vmem] * 5,
        out_specs=(vmem,) * 5,
        scratch_shapes=[pltpu.VMEM((256, 128), f32)],
        compiler_params=pltpu.CompilerParams(vmem_limit_bytes=48 << 20),
        name="route",
    )(left2, left, mine, right, right2)


def crossings(q, a):
    lanes = lax.broadcasted_iota(i32, (8, 128), 1)
    coords = (2 * a + (lanes >> 6), (lanes >> 3) & 7, lanes & 7)
    e = vel[q]
    found = [None if e[d] == 0 else coords[d] == (0 if e[d] == 1 else 7) for d in range(3)]
    if e[0] == 1 and a != 0 or e[0] == -1 and a != 3:
        found[0] = None
    return coords, found, [d for d in range(3) if found[d] is not None]


def inside_kernel(post, most):
    lanes = lax.broadcasted_iota(i32, (8, 128), 1)
    for g in range(4):
        rows = slice(8 * g, 8 * g + 8)
        most[0, rows, :] = post[0, rows, :]
        for q in range(1, 19):
            ex, ey, ez = vel[q]
            shift = ex * 64 + ey * 8 + ez
            rolled = [pltpu.roll(post[q, rows, 128 * a : 128 * (a + 1)], shift % 128, 1) for a in range(4)]
            for a in range(4):
                if shift > 0:
                    val = jnp.where(lanes < shift, rolled[(a - 1) % 4], rolled[a])
                else:
                    val = jnp.where(lanes >= 128 + shift, rolled[(a + 1) % 4], rolled[a])
                coords, crossing, axes = crossings(q, a)
                if axes:
                    out_of = crossing[axes[0]]
                    for d in axes[1:]:
                        out_of = out_of | crossing[d]
                    val = jnp.where(out_of, post[opposite[q], rows, 128 * a : 128 * (a + 1)], val)
                most[q, rows, 128 * a : 128 * (a + 1)] = val


def inside(post):
    vmem = pl.BlockSpec(memory_space=pltpu.VMEM)
    return pl.pallas_call(
        inside_kernel,
        out_shape=jax.ShapeDtypeStruct(post.shape, f32),
        in_specs=[vmem],
        out_specs=vmem,
        compiler_params=pltpu.CompilerParams(vmem_limit_bytes=48 << 20),
        name="inside",
    )(post)


def opened(ax):
    lane = lax.broadcasted_iota(i32, (128, 512), 0)
    site = lax.broadcasted_iota(i32, (128, 512), 1)
    i, j, k = site >> 6, (site >> 3) & 7, site & 7
    along, across = (k, j) if ax == 1 else (j, k)
    wanted = jnp.where(lane < 64, 7, 0)
    return ((i * 8 + along == (lane & 63)) & (across == wanted)).astype(f32).astype(bf16)


def ghost_kernel(goal, most, own, below, above, below2, above2, result, out, ghost, sem):
    lanes = lax.broadcasted_iota(i32, (8, 128), 1)
    low = lax.broadcasted_iota(i32, (32, 128), 1) < 64
    for ax in (1, 2):
        other = 2 if ax == 1 else 1
        shifted = []
        for n in range(5):
            t = 5 * ax + n
            came = own[t] + below[t] + above[t]
            steps = [(vel[q][0] * 8 + vel[q][other]) % 128 for q in (NEG[ax][n], POS[ax][n])]
            both = [pltpu.roll(came, step, 1) if step else came for step in steps]
            shifted.append(jnp.where(low, both[0], both[1]))
        planes = jnp.concatenate(shifted, axis=0)
        p_hi = planes.astype(bf16)
        p_lo = (planes - p_hi.astype(f32)).astype(bf16)
        to = opened(ax)
        ghost[ax - 1] = jnp.dot(p_hi, to, preferred_element_type=f32) + jnp.dot(p_lo, to, preferred_element_type=f32)
    leaving = []
    for g in range(4):
        rows = slice(8 * g, 8 * g + 8)
        near = goal[rows, :]
        there = [lane_take(near, jnp.full((8, 128), f, i32)) >= 0.0 for f in range(6)]
        came = own[EDGE_TILE, rows, :] + below[EDGE_TILE, rows, :] + above[EDGE_TILE, rows, :]
        came = came + below2[0, rows, :] + above2[0, rows, :]
        have = lane_take(came, jnp.minimum(HAVE + (lanes >> 3), 127)) > 0.5
        edges = jnp.where(have, came, jnp.nan)
        out[0, rows, :] = most[0, rows, :]
        for q in range(1, 19):
            e = vel[q]
            ex, ey, ez = e
            for a in range(4):
                val = most[q, rows, 128 * a : 128 * (a + 1)]
                (ii, jj, kk), crossing, axes = crossings(q, a)
                for d in axes:
                    n = (POS[d] if e[d] == 1 else NEG[d]).index(q)
                    if d == 0:
                        source = own[n, rows, :] + below[n, rows, :] + above[n, rows, :]
                        brought = pltpu.roll(source, (64 + ey * 8 + ez) % 128, 1)
                    else:
                        brought = ghost[d - 1, 32 * n + 8 * g : 32 * n + 8 * g + 8, 128 * a : 128 * (a + 1)]
                    use = crossing[d] & there[2 * d + (0 if e[d] == 1 else 1)]
                    for other in axes:
                        if other != d:
                            use = use & ~crossing[other]
                    val = jnp.where(use, brought, val)
                if len(axes) == 2:
                    along = kk if ez == 0 else (jj if ey == 0 else ii)
                    brought = lane_take(edges, 8 * (q - 7) + along)
                    val = jnp.where(crossing[axes[0]] & crossing[axes[1]] & (brought == brought), brought, val)
                out[q, rows, 128 * a : 128 * (a + 1)] = val
        leaving.append(pltpu.make_async_copy(out.at[:, rows, :], result.at[:, rows, :], sem.at[g]))
        leaving[-1].start()
    for c in leaving:
        c.wait()


def fill(goal, post, *parts):
    vmem = pl.BlockSpec(memory_space=pltpu.VMEM)
    return pl.pallas_call(
        ghost_kernel,
        out_shape=jax.ShapeDtypeStruct((19, 32, 512), f32),
        in_specs=[vmem] * 7,
        out_specs=pl.BlockSpec(memory_space=pltpu.HBM),
        scratch_shapes=[pltpu.VMEM(post.shape, f32), pltpu.VMEM((2, 160, 512), f32), pltpu.SemaphoreType.DMA((4,))],
        compiler_params=pltpu.CompilerParams(vmem_limit_bytes=48 << 20),
        name="fill",
    )(goal, post, *parts)


def send(array, axis, step):
    size = lax.axis_size(axis)
    return lax.ppermute(array, axis, [(i, (i + step) % size) for i in range(size)])


def exchange(table, edge):
    left, right = send(table, "gx", 1), send(table, "gx", -1)
    left2, right2 = send(edge, "gx", 2), send(edge, "gx", -2)
    down, own, up, down2, up2 = route(left2, left, table, right, right2)
    return own, send(up, "gy", 1), send(down, "gy", -1), send(up2, "gy", 2), send(down2, "gy", -2)


def body(populations, neighbours, positions, stiffness, cell_owner, cell_block, triangles):
    devices = lax.axis_size("gx") * lax.axis_size("gy")
    slots = spread(cell_owner[:, 0], cell_block, positions, stiffness, triangles, neighbours, devices)
    got = lax.all_to_all(slots, BOTH, split_axis=0, concat_axis=0, tiled=True)
    post, table, edge, goal = collide(got.reshape(-1, 128), populations, neighbours)
    result = fill(goal, inside(post), *exchange(table, edge))
    return jnp.transpose(result, (1, 0, 2))


def solution(mesh):
    placed = (
        P(BOTH, None, None),
        P(BOTH, None),
        P(BOTH, None, None),
        P(BOTH),
        P(BOTH, None),
        P(BOTH),
        P(),
    )
    return jax.shard_map(
        body, mesh=mesh, in_specs=placed, out_specs=P(BOTH, None, None), check_vma=False
    )
```

```python
import functools

import jax
import jax.numpy as jnp
import numpy as np
from jax import lax
from jax.experimental import pallas as pl
from jax.experimental.pallas import tpu as pltpu
from jax.sharding import PartitionSpec as P

vel = [
    (0, 0, 0), (1, 0, 0), (-1, 0, 0), (0, 1, 0), (0, -1, 0), (0, 0, 1), (0, 0, -1),
    (1, 1, 0), (-1, -1, 0), (1, -1, 0), (-1, 1, 0),
    (1, 0, 1), (-1, 0, -1), (1, 0, -1), (-1, 0, 1),
    (0, 1, 1), (0, -1, -1), (0, 1, -1), (0, -1, 1),
]
wts = [1.0 / 3.0] + [1.0 / 18.0] * 6 + [1.0 / 36.0] * 12
opposite = [0, 2, 1, 4, 3, 6, 5, 8, 7, 10, 9, 12, 11, 14, 13, 16, 15, 18, 17]
relax_time = 0.6
NEG, POS = {}, {}
for ax in range(3):
    NEG[ax] = [q for q in range(19) if vel[q][ax] == -1]
    POS[ax] = [q for q in range(19) if vel[q][ax] == 1]
EDGE_Q = list(range(7, 19))
FACE_TILES = 15
EDGE_TILE = 15
NT = 16
IDS = 96
HAVE = 114
WIDE = 3328
BOTH = ("gx", "gy")
f32, bf16, i32 = jnp.float32, jnp.bfloat16, jnp.int32


def nt_dot(a, b):
    return lax.dot_general(a, b, (((1,), (1,)), ((), ())), preferred_element_type=f32)


def hat(x, grid):
    return jnp.maximum(0.0, 1.0 - jnp.abs(x - grid))


def spread_kernel(owner_in, block_in, stiff_in, raw_in, tri_in, near_in, out, owner, block, stiff, raw, tri, near, sem, st, pos, force, hats, count):
    cells, nv = pos.shape[1:]
    verts = raw.shape[1]
    pairs = ((tri_in, tri), (raw_in, raw), (near_in, near), (owner_in, owner), (block_in, block), (stiff_in, stiff))
    copies = [pltpu.make_async_copy(a, b, sem.at[n]) for n, (a, b) in enumerate(pairs)]
    for c in copies:
        c.start()
    copies[0].wait()
    for r in range(0, nv, 128):
        ids = lax.broadcasted_iota(i32, (128, tri.shape[1]), 0) + r
        hit = (ids == tri[0:1, :]) | (ids == tri[1:2, :]) | (ids == tri[2:3, :])
        st[r : r + 128, :] = hit.astype(f32).astype(jnp.float8_e4m3fn)
    links = nt_dot(st[...], st[...])
    for c in copies[1:]:
        c.wait()
    sub = lax.broadcasted_iota(i32, (8, 128), 0)
    lane = lax.broadcasted_iota(i32, (8, 128), 1)
    slots = out.shape[0]
    tail_row = jnp.full((8, 128), -1.0, f32)
    table_row = jnp.zeros((8, 128), f32)
    for f in range(4):
        one_face = jnp.concatenate([near[f + 2 : f + 3, :].astype(f32), jnp.zeros((1, 96), f32)], axis=1)
        one_face = jnp.broadcast_to(one_face, (8, 128))
        table_row = jnp.where(lane // 32 == f, pltpu.roll(one_face, 32 * f, 1) if f else one_face, table_row)

    def clear(t, carry):
        for m in range(8):
            out[t * 8 + m, :, 0:3072] = jnp.zeros((1, 3072), f32)
            out[t * 8 + m, :, 3072:3200] = tail_row[0:1]
            out[t * 8 + m, :, 3200:3328] = table_row[0:1]
            count[t * 8 + m] = 0
        return carry

    lax.fori_loop(0, slots // 8, clear, 0)
    for r in range(0, nv, 128):
        for d in range(3):
            have = min(verts - r, 128)
            piece = raw[d, r : r + have, :]
            if have < 128:
                piece = jnp.concatenate([piece, jnp.full((128 - have, cells), -100.0, f32)], axis=0)
            pos[d, :, r : r + 128] = jnp.transpose(piece)
    rows = lax.broadcasted_iota(i32, (nv, nv), 0)
    cols = lax.broadcasted_iota(i32, (nv, nv), 1)
    springs = jnp.where(rows == cols, -2.0 * links, links)
    s_hi = springs.astype(bf16)
    s_lo = (springs - s_hi.astype(f32)).astype(bf16)
    x = jnp.concatenate([pos[0], pos[1], pos[2]], axis=0)
    x_hi = x.astype(bf16)
    x_lo = (x - x_hi.astype(f32)).astype(bf16)
    most = jnp.dot(jnp.concatenate([x_hi, x_lo], axis=0), s_hi, preferred_element_type=f32)
    for d in range(3):
        lo, hi = d * cells, (d + 1) * cells
        force[d] = most[lo:hi] + most[3 * cells + lo : 3 * cells + hi]

    @pl.when(jnp.max(jnp.abs(springs)) > 256.0)
    def _():
        rest = jnp.dot(x_hi, s_lo, preferred_element_type=f32)
        for d in range(3):
            force[d] = force[d] + rest[d * cells : (d + 1) * cells]

    sub8 = lax.broadcasted_iota(i32, (8, nv), 0)
    g_even = (2 * (sub8 % 4)).astype(f32)
    g_odd = g_even + 1.0
    g_all = sub8.astype(f32)
    first4 = sub8 < 4

    def product(first, m):
        c = first + m
        near8 = pl.ds(pl.multiple_of(first + m // 8 * 8, 8), 8)
        x = jnp.broadcast_to(pos[0, near8, :][m % 8 : m % 8 + 1], (8, nv))
        y = jnp.broadcast_to(pos[1, near8, :][m % 8 : m % 8 + 1], (8, nv))
        z = jnp.broadcast_to(pos[2, near8, :][m % 8 : m % 8 + 1], (8, nv))
        f0 = jnp.broadcast_to(force[0, near8, :][m % 8 : m % 8 + 1], (8, nv))
        f1 = jnp.broadcast_to(force[1, near8, :][m % 8 : m % 8 + 1], (8, nv))
        f2 = jnp.broadcast_to(force[2, near8, :][m % 8 : m % 8 + 1], (8, nv))
        h_even = hat(x, g_even)
        h_odd = hat(x, g_odd)
        f01 = jnp.where(first4, f0, f1)
        left = jnp.concatenate(
            [h_even * f01, jnp.where(first4, h_even, h_odd) * f2, h_odd * f01], axis=0
        )
        l_lo = left - left.astype(bf16).astype(f32)
        left2 = jnp.concatenate([left, l_lo], axis=0).astype(bf16)
        hy = hat(y, g_all)
        hz = hat(z, g_all)
        plane = jnp.concatenate(
            [jnp.broadcast_to(hy[j : j + 1], (8, nv)) * hz for j in range(8)], axis=0
        )
        p_hi = plane.astype(bf16)
        p_lo = (plane - p_hi.astype(f32)).astype(bf16)
        prod = nt_dot(left2, jnp.concatenate([p_hi, p_lo], axis=0))
        hats[m] = prod[0:24] + prod[24:48]

    def place(c, m):
        both = hats[m]
        res = (both + pltpu.roll(both, 64, 1)) * stiff[c]
        main = jnp.where(lane < 64, res[0:8], res[16:24])
        mid = res[8:16]
        tail = jnp.where(lane < 64, mid, pltpu.roll(mid, 4, 0))
        t = owner[c]
        r = count[t]
        count[t] = r + 1
        for k in range(12):
            row = main[k : k + 1] if k < 8 else tail[k - 8 : k - 7]
            out[t, :, pl.ds(pl.multiple_of(r * 1536 + 128 * k, 128), 128)] = row
        old = out[t, :, 3072:3200]
        out[t, :, 3072:3200] = jnp.where(lane[0:1] == r, block[c].astype(f32), old)

    group = hats.shape[0]

    def finish(first):
        for m in range(group):
            place(first + m, m)

    for m in range(group):
        product(0, m)

    def step(n, carry):
        finish((n - 1) * group)
        for m in range(group):
            product(n * group, m)
        return carry

    lax.fori_loop(1, cells // group, step, 0)
    finish(cells - group)


def spread(owner, block, positions, stiffness, triangles, neighbours, devices):
    cells, _, verts = positions.shape
    nv = -(-verts // 256) * 256
    inputs = (owner, block, stiffness, jnp.transpose(positions, (1, 2, 0)), jnp.transpose(triangles), jnp.transpose(neighbours))
    hbm = pl.BlockSpec(memory_space=pltpu.HBM)
    vmem = pl.BlockSpec(memory_space=pltpu.VMEM)
    return pl.pallas_call(
        spread_kernel,
        out_shape=jax.ShapeDtypeStruct((devices, 1, WIDE), f32),
        in_specs=[hbm] * 6,
        out_specs=vmem,
        scratch_shapes=[
            pltpu.SMEM((cells,), i32),
            pltpu.SMEM((cells,), i32),
            pltpu.SMEM((cells,), f32),
            pltpu.VMEM((3, verts, cells), f32),
            pltpu.VMEM((3, triangles.shape[0]), i32),
            pltpu.VMEM((6, 32), i32),
            pltpu.SemaphoreType.DMA((6,)),
            pltpu.VMEM((nv, triangles.shape[0]), jnp.float8_e4m3fn),
            pltpu.VMEM((3, cells, nv), f32),
            pltpu.VMEM((3, cells, nv), f32),
            pltpu.VMEM((16, 24, 128), f32),
            pltpu.SMEM((devices,), i32),
        ],
        compiler_params=pltpu.CompilerParams(vmem_limit_bytes=48 << 20),
        name="spread",
    )(*[pltpu.with_memory_space_constraint(x, pltpu.HBM) for x in inputs])


def lane_take(x, index):
    return jnp.take_along_axis(x, index, axis=1, mode="promise_in_bounds")


def column(got, tile):
    tiles = WIDE // 128
    return got[pl.ds(tile, got.shape[0] // tiles, stride=tiles), :]


def find(near, got, square):
    square[...] = jnp.full((128, 128), -1.0, f32)
    square[0:6, 0:32] = near[...].astype(f32)
    goal = jnp.transpose(square[...])[0:32]
    known = column(got, 25)
    k_hi = known.astype(bf16)
    k_lo = (known - k_hi.astype(f32)).astype(bf16)
    lane = lax.broadcasted_iota(i32, (32, 128), 1)
    firsts = [lane_take(goal, jnp.full((32, 128), f1, i32)).astype(i32) for f1 in range(4)]
    picks = [(lax.shift_right_logical(jnp.maximum(first, 0), 5) == lane).astype(f32) for first in firsts]
    found = jnp.dot(
        jnp.concatenate(picks, axis=0).astype(bf16), jnp.concatenate([k_hi, k_lo], axis=1), preferred_element_type=f32
    )
    for f1, first in enumerate(firsts):
        safe = jnp.maximum(first, 0)
        rows = found[32 * f1 : 32 * (f1 + 1), 0:128] + found[32 * f1 : 32 * (f1 + 1), 128:256]
        for n, q in enumerate(EDGE_Q):
            d1, d2 = [d for d in range(3) if vel[q][d]]
            if f1 == 2 * d1 + (1 if vel[q][d1] == 1 else 0):
                f2 = 2 * d2 + (1 if vel[q][d2] == 1 else 0)
                second = lane_take(rows, (f2 - 2) * 32 + lax.bitwise_and(safe, 31))
                goal = jnp.where(lane == 6 + n, jnp.where(first >= 0, second, -1.0), goal)
    return goal


def collide_kernel(near, got, pops, post, table, edge, goal, body, square):
    slots = got.shape[0] * 128 // WIDE
    found = find(near, got, square)
    lane = lax.broadcasted_iota(i32, (slots, 128), 1)
    ids = column(got, 24)
    picks = []
    for r in range(2):
        col = jnp.broadcast_to(ids[:, r : r + 1], (slots, 128))
        hit = (col == lane.astype(f32)).astype(f32)
        picks.append(jnp.transpose(hit)[0:32].astype(bf16))
    for n in range(3):
        total = jnp.zeros((32, 512), f32)
        for r in range(2):
            part = jnp.concatenate([column(got, 12 * r + 4 * n + a) for a in range(4)], axis=1)
            hi = part.astype(bf16)
            lo = (part - hi.astype(f32)).astype(bf16)
            total = total + jnp.dot(picks[r], hi, preferred_element_type=f32)
            total = total + jnp.dot(picks[r], lo, preferred_element_type=f32)
        body[n] = total
    lanes = lax.broadcasted_iota(i32, (8, 128), 1)
    low = lanes < 64
    keep = 1.0 - 1.0 / relax_time
    gain = 1.0 - 0.5 / relax_time

    def group(g, carry):
        rows = pl.ds(pl.multiple_of(g * 8, 8), 8)
        for a in range(4):
            cut = slice(128 * a, 128 * (a + 1))
            f = [pops[q, rows, cut] * wts[q] for q in range(19)]
            force = [body[d, rows, cut] for d in range(3)]
            rho = f[0]
            for q in range(1, 19):
                rho = rho + f[q]
            u = []
            for d in range(3):
                m = 0.5 * force[d]
                for q in range(1, 19):
                    if vel[q][d] == 1:
                        m = m + f[q]
                    elif vel[q][d] == -1:
                        m = m - f[q]
                u.append(m / rho)
            speed = u[0] * u[0] + u[1] * u[1] + u[2] * u[2]
            work = u[0] * force[0] + u[1] * force[1] + u[2] * force[2]
            rho_t = rho * (1.0 / relax_time)
            flat = rho_t * (1.0 - 1.5 * speed) - (3.0 * gain) * work
            post[0, rows, cut] = keep * f[0] + wts[0] * flat
            for q in range(1, 19, 2):
                along = push = None
                for d in range(3):
                    e = vel[q][d]
                    if e:
                        along = e * u[d] if along is None else along + e * u[d]
                        push = e * force[d] if push is None else push + e * force[d]
                even = wts[q] * (flat + along * (4.5 * rho_t * along + (9.0 * gain) * push))
                odd = wts[q] * (3.0 * rho_t * along + (3.0 * gain) * push)
                post[q, rows, cut] = keep * f[q] + (even + odd)
                post[q + 1, rows, cut] = keep * f[q + 1] + (even - odd)
        for n in range(5):
            table[n, rows, :] = jnp.where(low, post[NEG[0][n], rows, 0:128], post[POS[0][n], rows, 384:512])
            first, second = (lanes >> 3) & 7, lanes & 7
            for ax in (1, 2):
                picked = None
                for a in range(4):
                    inside = (first & 1) * 64
                    if ax == 1:
                        at_low, at_high = inside + second, inside + 56 + second
                    else:
                        at_low, at_high = inside + second * 8, inside + second * 8 + 7
                    cut = slice(128 * a, 128 * (a + 1))
                    val = jnp.where(
                        low, lane_take(post[NEG[ax][n], rows, cut], at_low), lane_take(post[POS[ax][n], rows, cut], at_high)
                    )
                    picked = val if picked is None else jnp.where(first >> 1 == a, val, picked)
                table[5 * ax + n, rows, :] = picked
        line = jnp.ones((8, 128), f32)
        w = lanes & 7
        for n, q in enumerate(EDGE_Q):
            ex, ey, ez = vel[q]
            at = [7 if e == 1 else 0 for e in vel[q]]
            mine = lanes >> 3 == n
            if ex:
                a = 3 if ex == 1 else 0
                base = 64 if ex == 1 else 0
                where_ = base + (at[1] * 8 + w if ey else w * 8 + at[2])
                val = lane_take(post[q, rows, 128 * a : 128 * (a + 1)], where_)
                line = jnp.where(mine, val, line)
            else:
                where_ = (w & 1) * 64 + at[1] * 8 + at[2]
                for a in range(4):
                    val = lane_take(post[q, rows, 128 * a : 128 * (a + 1)], where_)
                    line = jnp.where(mine & (w >> 1 == a), val, line)
        table[EDGE_TILE, rows, :] = line
        return carry

    lax.fori_loop(0, 4, group, 0, unroll=True)
    goal[...] = found
    lane = lax.broadcasted_iota(i32, (32, 128), 1)
    lines = jnp.where((lane >= IDS) & (lane < HAVE), pltpu.roll(found, IDS, 1), table[EDGE_TILE])
    table[EDGE_TILE] = lines
    edge[0] = lines


def collide(got, populations, neighbours):
    vmem = pl.BlockSpec(memory_space=pltpu.VMEM)
    return pl.pallas_call(
        collide_kernel,
        out_shape=(
            jax.ShapeDtypeStruct((19, 32, 512), f32),
            jax.ShapeDtypeStruct((NT, 32, 128), f32),
            jax.ShapeDtypeStruct((1, 32, 128), f32),
            jax.ShapeDtypeStruct((32, 128), f32),
        ),
        in_specs=[vmem, vmem, vmem],
        out_specs=(vmem,) * 4,
        scratch_shapes=[
            pltpu.VMEM((3, 32, 512), f32),
            pltpu.VMEM((128, 128), f32),
        ],
        compiler_params=pltpu.CompilerParams(vmem_limit_bytes=48 << 20),
        name="collide",
    )(jnp.transpose(neighbours), got, jnp.transpose(populations, (1, 0, 2)))


def route_kernel(sizes, left2, left, mine, right, right2, down, own, up, down2, up2, lines):
    n_gy = sizes[1]
    me_x, me_y = lax.axis_index("gx"), lax.axis_index("gy")
    for n, part in enumerate((left[EDGE_TILE], mine[EDGE_TILE], right[EDGE_TILE], left2[0], right2[0])):
        lines[32 * n : 32 * (n + 1), :] = part
    lines[160:256, :] = jnp.full((96, 128), -1.0, f32)
    ids = [jnp.transpose(lines[0:128, :]), jnp.transpose(lines[128:256, :])]
    slot = lax.broadcasted_iota(i32, (32, 128), 0).astype(f32)
    low = lax.broadcasted_iota(i32, (32, 128), 1) < 64
    named = {}
    for dy in range(-2, 3):
        owner = me_x * n_gy + lax.rem(me_y + (dy + n_gy), n_gy)
        named[dy] = slot + (owner * 32).astype(f32)

    def hot(half, row, dy):
        picked = jnp.broadcast_to(ids[half][IDS + row : IDS + row + 1, :], (32, 128)) == named[dy]
        return picked.astype(f32)

    none = jnp.zeros((32, 128), f32)
    for ax in range(3):
        planes = jnp.concatenate(
            [
                jnp.concatenate([left[t], mine[t], right[t], none], axis=0)
                for t in range(5 * ax, 5 * ax + 5)
            ],
            axis=1,
        )
        p_hi = planes.astype(bf16)
        p_lo = (planes - p_hi.astype(f32)).astype(bf16)
        picks = jnp.concatenate([hot(0, 2 * ax + s, dy) for s in range(2) for dy in (-1, 0, 1)], axis=0).astype(bf16)
        moved = jnp.dot(picks, p_hi, preferred_element_type=f32) + jnp.dot(picks, p_lo, preferred_element_type=f32)
        for k, goal in enumerate((down, own, up)):
            for n in range(5):
                cut = slice(128 * n, 128 * (n + 1))
                goal[5 * ax + n] = jnp.where(
                    low, moved[32 * k : 32 * (k + 1), cut], moved[96 + 32 * k : 96 + 32 * (k + 1), cut]
                )
    e_hi = lines[...].astype(bf16)
    e_lo = (lines[...] - e_hi.astype(f32)).astype(bf16)
    both = jnp.concatenate([e_hi, e_lo], axis=1)
    lane = lax.broadcasted_iota(i32, (160, 128), 1)
    total = jnp.zeros((160, 128), f32)
    for n in range(12):
        picks = jnp.concatenate(
            [jnp.concatenate([hot(h, 6 + n, dy) for dy in range(-2, 3)], axis=0) for h in range(2)], axis=1
        ).astype(bf16)
        moved = jnp.dot(picks, both, preferred_element_type=f32)
        wanted = (lane >> 3 == n) | (lane == HAVE + n)
        total = jnp.where(wanted, moved[:, 0:128] + moved[:, 128:256], total)
    for k, goal in enumerate((down2, down, own, up, up2)):
        goal[goal.shape[0] - 1] = total[32 * k : 32 * (k + 1)]


def route(left2, left, mine, right, right2):
    vmem = pl.BlockSpec(memory_space=pltpu.VMEM)
    sizes = (lax.axis_size("gx"), lax.axis_size("gy"))
    big = jax.ShapeDtypeStruct(mine.shape, f32)
    small = jax.ShapeDtypeStruct(left2.shape, f32)
    return pl.pallas_call(
        functools.partial(route_kernel, sizes),
        out_shape=(big, big, big, small, small),
        in_specs=[vmem] * 5,
        out_specs=(vmem,) * 5,
        scratch_shapes=[pltpu.VMEM((256, 128), f32)],
        compiler_params=pltpu.CompilerParams(vmem_limit_bytes=48 << 20),
        name="route",
    )(left2, left, mine, right, right2)


def crossings(q, a):
    lanes = lax.broadcasted_iota(i32, (8, 128), 1)
    coords = (2 * a + (lanes >> 6), (lanes >> 3) & 7, lanes & 7)
    e = vel[q]
    found = [None if e[d] == 0 else coords[d] == (0 if e[d] == 1 else 7) for d in range(3)]
    if e[0] == 1 and a != 0 or e[0] == -1 and a != 3:
        found[0] = None
    return coords, found, [d for d in range(3) if found[d] is not None]


def inside_kernel(post, most):
    lanes = lax.broadcasted_iota(i32, (8, 128), 1)
    for g in range(4):
        rows = slice(8 * g, 8 * g + 8)
        most[0, rows, :] = post[0, rows, :]
        for q in range(1, 19):
            ex, ey, ez = vel[q]
            shift = ex * 64 + ey * 8 + ez
            rolled = [pltpu.roll(post[q, rows, 128 * a : 128 * (a + 1)], shift % 128, 1) for a in range(4)]
            for a in range(4):
                if shift > 0:
                    val = jnp.where(lanes < shift, rolled[(a - 1) % 4], rolled[a])
                else:
                    val = jnp.where(lanes >= 128 + shift, rolled[(a + 1) % 4], rolled[a])
                coords, crossing, axes = crossings(q, a)
                if axes:
                    out_of = crossing[axes[0]]
                    for d in axes[1:]:
                        out_of = out_of | crossing[d]
                    val = jnp.where(out_of, post[opposite[q], rows, 128 * a : 128 * (a + 1)], val)
                most[q, rows, 128 * a : 128 * (a + 1)] = val


def inside(post):
    vmem = pl.BlockSpec(memory_space=pltpu.VMEM)
    return pl.pallas_call(
        inside_kernel,
        out_shape=jax.ShapeDtypeStruct(post.shape, f32),
        in_specs=[vmem],
        out_specs=vmem,
        compiler_params=pltpu.CompilerParams(vmem_limit_bytes=48 << 20),
        name="inside",
    )(post)


def opened(ax):
    lane = lax.broadcasted_iota(i32, (128, 512), 0)
    site = lax.broadcasted_iota(i32, (128, 512), 1)
    i, j, k = site >> 6, (site >> 3) & 7, site & 7
    along, across = (k, j) if ax == 1 else (j, k)
    wanted = jnp.where(lane < 64, 7, 0)
    return ((i * 8 + along == (lane & 63)) & (across == wanted)).astype(f32).astype(bf16)


def ghost_kernel(goal, most, own, below, above, below2, above2, result, out, ghost, sem):
    lanes = lax.broadcasted_iota(i32, (8, 128), 1)
    low = lax.broadcasted_iota(i32, (32, 128), 1) < 64
    for ax in (1, 2):
        other = 2 if ax == 1 else 1
        shifted = []
        for n in range(5):
            t = 5 * ax + n
            came = own[t] + below[t] + above[t]
            steps = [(vel[q][0] * 8 + vel[q][other]) % 128 for q in (NEG[ax][n], POS[ax][n])]
            both = [pltpu.roll(came, step, 1) if step else came for step in steps]
            shifted.append(jnp.where(low, both[0], both[1]))
        planes = jnp.concatenate(shifted, axis=0)
        p_hi = planes.astype(bf16)
        p_lo = (planes - p_hi.astype(f32)).astype(bf16)
        to = opened(ax)
        ghost[ax - 1] = jnp.dot(p_hi, to, preferred_element_type=f32) + jnp.dot(p_lo, to, preferred_element_type=f32)
    leaving = []
    for g in range(4):
        rows = slice(8 * g, 8 * g + 8)
        near = goal[rows, :]
        there = [lane_take(near, jnp.full((8, 128), f, i32)) >= 0.0 for f in range(6)]
        came = own[EDGE_TILE, rows, :] + below[EDGE_TILE, rows, :] + above[EDGE_TILE, rows, :]
        came = came + below2[0, rows, :] + above2[0, rows, :]
        have = lane_take(came, jnp.minimum(HAVE + (lanes >> 3), 127)) > 0.5
        edges = jnp.where(have, came, jnp.nan)
        out[0, rows, :] = most[0, rows, :]
        for q in range(1, 19):
            e = vel[q]
            ex, ey, ez = e
            for a in range(4):
                val = most[q, rows, 128 * a : 128 * (a + 1)]
                (ii, jj, kk), crossing, axes = crossings(q, a)
                for d in axes:
                    n = (POS[d] if e[d] == 1 else NEG[d]).index(q)
                    if d == 0:
                        source = own[n, rows, :] + below[n, rows, :] + above[n, rows, :]
                        brought = pltpu.roll(source, (64 + ey * 8 + ez) % 128, 1)
                    else:
                        brought = ghost[d - 1, 32 * n + 8 * g : 32 * n + 8 * g + 8, 128 * a : 128 * (a + 1)]
                    use = crossing[d] & there[2 * d + (0 if e[d] == 1 else 1)]
                    for other in axes:
                        if other != d:
                            use = use & ~crossing[other]
                    val = jnp.where(use, brought, val)
                if len(axes) == 2:
                    along = kk if ez == 0 else (jj if ey == 0 else ii)
                    brought = lane_take(edges, 8 * (q - 7) + along)
                    val = jnp.where(crossing[axes[0]] & crossing[axes[1]] & (brought == brought), brought, val)
                out[q, rows, 128 * a : 128 * (a + 1)] = val
        leaving.append(pltpu.make_async_copy(out.at[:, rows, :], result.at[:, rows, :], sem.at[g]))
        leaving[-1].start()
    for c in leaving:
        c.wait()


def fill(goal, post, *parts):
    vmem = pl.BlockSpec(memory_space=pltpu.VMEM)
    return pl.pallas_call(
        ghost_kernel,
        out_shape=jax.ShapeDtypeStruct((19, 32, 512), f32),
        in_specs=[vmem] * 7,
        out_specs=pl.BlockSpec(memory_space=pltpu.HBM),
        scratch_shapes=[pltpu.VMEM(post.shape, f32), pltpu.VMEM((2, 160, 512), f32), pltpu.SemaphoreType.DMA((4,))],
        compiler_params=pltpu.CompilerParams(vmem_limit_bytes=48 << 20),
        name="fill",
    )(goal, post, *parts)


def send(array, axis, step):
    size = lax.axis_size(axis)
    return lax.ppermute(array, axis, [(i, (i + step) % size) for i in range(size)])


def exchange(table, edge):
    left, right = send(table, "gx", 1), send(table, "gx", -1)
    left2, right2 = send(edge, "gx", 2), send(edge, "gx", -2)
    down, own, up, down2, up2 = route(left2, left, table, right, right2)
    return own, send(up, "gy", 1), send(down, "gy", -1), send(up2, "gy", 2), send(down2, "gy", -2)


def body(populations, neighbours, positions, stiffness, cell_owner, cell_block, triangles):
    devices = lax.axis_size("gx") * lax.axis_size("gy")
    slots = spread(cell_owner[:, 0], cell_block, positions, stiffness, triangles, neighbours, devices)
    got = lax.all_to_all(slots, BOTH, split_axis=0, concat_axis=0, tiled=True)
    post, table, edge, goal = collide(got.reshape(-1, 128), populations, neighbours)
    result = fill(goal, inside(post), *exchange(table, edge))
    return jnp.transpose(result, (1, 0, 2))


def solution(mesh):
    placed = (
        P(BOTH, None, None),
        P(BOTH, None),
        P(BOTH, None, None),
        P(BOTH),
        P(BOTH, None),
        P(BOTH),
        P(),
    )
    return jax.shard_map(
        body, mesh=mesh, in_specs=placed, out_specs=P(BOTH, None, None), check_vma=False
    )
```
